32 devices in a mesh: tile: 2 (over y), strip: 4 (over x, core), focus: 4 (over z).
Axes of the slice: x: 2, y: 2, z: 4, core: 2. Of those that a mesh axis runs over, the one named last changes fastest.
Arguments:
- phi: float32 [512, 2048], P(('tile', 'strip')), parts along dimension 0, may hold values from -6 to 6
- target: int32 [512, 2048], P(('tile', 'strip')), parts along dimension 0, may hold values 0 or 1
- defocus_ids: int32 [8], P(('tile', 'focus')), parts along dimension 0, may hold values from 0 to 30
- kernels: float32 [2, 4, 48, 512], replicated, may hold values from -16 to 16
- psi: float32 [48, 512], replicated, may hold values from -3.140625 to 3.140625
- row_freqs: int32 [48], replicated, may hold values from -96 to 95, as said below
- col_freqs: int32 [512], replicated, may hold values from -1024 to 1023, as said below
Outputs:
- phi_next: float32 [512, 2048], P(('tile', 'strip')), parts along dimension 0
The draws below stay inside these ranges and needn't reach their ends.
There are 2 independent parts, one for each index of `tile`. The reference program is written for one: setup_inputs(seed, part) draws one part's arguments, and reference() takes and returns one part's arrays. A program takes and returns all parts, laid end to end along the dimension named above; an argument that names none is the same for every part. Nothing has to cross between parts.
Inputs may be any that keep to these rules, and one draw needn't show every extreme that they name: `row_freqs`: distinct whole frequencies; the lowest and highest of the range are always among them. `col_freqs`: distinct whole frequencies; the lowest and highest of the range are always among them.
All inputs are finite; a program needn't handle non-finite values. No bound on the sum of `target` on one device may be relied on, other than what follows from the above.
Results may differ from the reference program's by a relative error of at most 0.02.
Values may be sent and summed in bfloat16 or wider, within the bound.
No kernel may reach another device: no remote copies, remote signals or barrier semaphores. Data moves between devices by JAX's collectives and lax.ppermute only.
A program may use at most 64 MiB of HBM per device.

```python
import jax
import jax.numpy as jnp
from jax import lax

ROWS = 64
MARGIN = 64
COLS = 2048
FR = 48
FC = 512
KERN = 4
LEVELS = 31
SWEEPS = 2
WIN = 192
STRIPS = 4
PLANES = 4


def pick_freqs(key, period, number):
    inner = jax.random.permutation(key, period - 2)[:number - 2] + 1
    picked = jnp.concatenate([jnp.array([0, period - 1], jnp.int32), inner.astype(jnp.int32)])
    return (picked - period // 2).astype(jnp.int32)


def draw_row_freqs(key, part):
    return pick_freqs(jax.random.fold_in(key, 11), WIN, FR)


def draw_col_freqs(key, part):
    return pick_freqs(jax.random.fold_in(key, 23), COLS, FC)


def touch_ends(values, own_key, smallest, high):
    longest = values.shape.index(max(values.shape))
    spots = []
    for shift in (0, 1):
        where = [jax.random.randint(jax.random.fold_in(own_key, axis), (), 0, length) for axis, length in enumerate(values.shape)]
        where[longest] = (where[longest] + shift) % values.shape[longest]
        spots.append(tuple(where))
    return values.at[spots[0]].set(smallest).at[spots[1]].set(high)


def shard_levels(stream_key, shape, split, least, largest):
    loudness, own = 1.0, jax.random.fold_in(stream_key, 6)
    for dim, blocks in split:
        steps = jnp.exp(jax.random.uniform(jax.random.fold_in(own, dim), (blocks,), jnp.float32, least / len(split), largest / len(split)))
        loudness = loudness * jnp.repeat(steps, shape[dim] // blocks).reshape([-1 if axis == dim else 1 for axis in range(len(shape))])
    return loudness


def normal_values(own_key, extent, deviation, bound, pieces=(), kind=jnp.bfloat16):
    level = shard_levels(own_key, extent, pieces, -0.22, 0.18) if pieces else 1.0
    values = jax.random.normal(own_key, extent, jnp.float32) * deviation * level
    return jnp.minimum(jnp.maximum(values, -bound), bound).astype(kind)


def setup_inputs(seed: int = 0, part: int = 0) -> dict:
    splits = jax.random.split(jax.random.key(seed), 8)
    part_keys = jax.random.split(jax.random.fold_in(splits[7], part), 8)
    return {
        "phi": normal_values(part_keys[0], (STRIPS * ROWS, COLS), 1.0, 6.0, ((0, 4),), jnp.float32),
        "target": touch_ends((jax.random.randint(part_keys[1], (STRIPS * ROWS, COLS), 0, 2) < 1).astype(jnp.int32), jax.random.fold_in(part_keys[1], 1), 0, 1),
        "defocus_ids": touch_ends(jax.random.randint(part_keys[2], (PLANES,), 0, LEVELS), jax.random.fold_in(part_keys[2], 1), 0, LEVELS - 1).astype(jnp.int32),
        "kernels": normal_values(splits[3], (2, KERN, FR, FC), 3.0, 16.0, (), jnp.float32),
        "psi": jnp.clip(jax.random.uniform(splits[4], (FR, FC), jnp.float32, -3.140625, 3.140625), -3.140625, 3.140625),
        "row_freqs": draw_row_freqs(jax.random.fold_in(splits[7], 71), part),
        "col_freqs": draw_col_freqs(jax.random.fold_in(splits[7], 71), part),
    }


slope_resist = 4.0
level_resist = 0.5
step_size = 1.0
flow_rate = 0.2

def tables(freq_list, period, length):
    positions = jnp.arange(length, dtype=jnp.int32)
    phase_int = jnp.mod(freq_list[:, None] * positions[None, :], period)
    angles = phase_int.astype(jnp.float32) * (2.0 * jnp.pi / period)
    return (jnp.cos(angles).astype(jnp.bfloat16), jnp.sin(angles).astype(jnp.bfloat16))

def product(lhs_mat, rhs_mat):
    return jnp.dot(lhs_mat, rhs_mat, preferred_element_type=jnp.float32)

def product_t(lhs_mat, rhs_mat):
    return lax.dot_general(lhs_mat, rhs_mat, (((1,), (1,)), ((), ())), preferred_element_type=jnp.float32)

def exact_t(lhs_mat, rhs_mat):
    return lax.dot_general(lhs_mat.astype(jnp.float32), rhs_mat, (((0,), (0,)), ((), ())), precision=lax.Precision.HIGHEST, preferred_element_type=jnp.float32)

def batch(form, lhs_mat, rhs_mat):
    return jnp.einsum(form, lhs_mat.astype(jnp.float32), rhs_mat.astype(jnp.float32), precision=lax.Precision.HIGHEST)

def spectral_rows(cos_part, sin_part, y_re, y_im):
    z_re = exact_t(cos_part, y_re) - exact_t(sin_part, y_im)
    z_im = exact_t(cos_part, y_im) + exact_t(sin_part, y_re)
    return (z_re.astype(jnp.bfloat16), z_im.astype(jnp.bfloat16))

def curvature_step(padded):
    center = padded[1:-1, 1:-1]
    upper_row = padded[2:, 1:-1]
    lower_row = padded[:-2, 1:-1]
    right_col = padded[1:-1, 2:]
    left_col = padded[1:-1, :-2]
    diagonal = padded[2:, 2:] - padded[2:, :-2] - padded[:-2, 2:] + padded[:-2, :-2]
    grad_x = 0.5 * (upper_row - lower_row)
    grad_y = 0.5 * (right_col - left_col)
    second_x = upper_row - 2.0 * center + lower_row
    second_y = right_col - 2.0 * center + left_col
    cross_term = 0.25 * diagonal
    flow_term = (second_x * grad_y * grad_y - 2.0 * grad_x * grad_y * cross_term + second_y * grad_x * grad_x) / (1.0 + grad_x * grad_x + grad_y * grad_y)
    return center + flow_rate * flow_term

def reference(phi, target, defocus_ids, kernels, psi, row_freqs, col_freqs):
    scale_norm = 1.0 / jnp.sqrt(jnp.float32(WIN * COLS))
    row_cos, row_sin = tables(row_freqs, WIN, WIN)
    col_cos, col_sin = tables(col_freqs, COLS, COLS)
    inner_cos = row_cos[:, MARGIN:MARGIN + ROWS]
    inner_sin = row_sin[:, MARGIN:MARGIN + ROWS]
    middle = (LEVELS - 1) / 2.0
    defocus_all = (defocus_ids.astype(jnp.float32) - middle) / middle
    mask_pad = jnp.pad(jnp.tanh(phi).astype(jnp.bfloat16), ((MARGIN, MARGIN), (0, 0)))
    target_f = target.astype(jnp.float32)

    def strip_terms(index):
        start = index * ROWS
        window = lax.dynamic_slice_in_dim(mask_pad, start, WIN, 0)
        goal = lax.dynamic_slice_in_dim(target_f, start, ROWS, 0)
        p_re = product_t(window, col_cos).astype(jnp.bfloat16)
        p_im = (-product_t(window, col_sin)).astype(jnp.bfloat16)
        s_re = scale_norm * (product(row_cos, p_re) + product(row_sin, p_im))
        s_im = scale_norm * (product(row_cos, p_im) - product(row_sin, p_re))

        def plane_terms(defocus):
            phase_turn = defocus * psi
            cos_turn = jnp.cos(phase_turn)
            sin_turn = jnp.sin(phase_turn)
            k_re = kernels[0] * cos_turn - kernels[1] * sin_turn
            k_im = kernels[0] * sin_turn + kernels[1] * cos_turn
            g_re = (k_re * s_re - k_im * s_im).astype(jnp.bfloat16)
            g_im = (k_re * s_im + k_im * s_re).astype(jnp.bfloat16)
            q_re = (batch('fr,kfc->krc', inner_cos, g_re) - batch('fr,kfc->krc', inner_sin, g_im)).astype(jnp.bfloat16)
            q_im = (batch('fr,kfc->krc', inner_cos, g_im) + batch('fr,kfc->krc', inner_sin, g_re)).astype(jnp.bfloat16)
            e_re = scale_norm * (batch('krc,cy->kry', q_re, col_cos) - batch('krc,cy->kry', q_im, col_sin))
            e_im = scale_norm * (batch('krc,cy->kry', q_re, col_sin) + batch('krc,cy->kry', q_im, col_cos))
            intensity = lax.optimization_barrier(jnp.mean(e_re * e_re + e_im * e_im, axis=0))
            resist = jax.nn.sigmoid(slope_resist * (intensity - level_resist))
            weight = 4.0 * slope_resist / KERN * (resist - goal) * resist * (1.0 - resist)
            v_re = (weight * e_re).astype(jnp.bfloat16)
            v_im = (weight * e_im).astype(jnp.bfloat16)
            u_re = (batch('kry,cy->krc', v_re, col_cos) + batch('kry,cy->krc', v_im, col_sin)).astype(jnp.bfloat16)
            u_im = (batch('kry,cy->krc', v_im, col_cos) - batch('kry,cy->krc', v_re, col_sin)).astype(jnp.bfloat16)
            w_re = scale_norm * (batch('fr,krc->kfc', inner_cos, u_re) + batch('fr,krc->kfc', inner_sin, u_im))
            w_im = scale_norm * (batch('fr,krc->kfc', inner_cos, u_im) - batch('fr,krc->kfc', inner_sin, u_re))
            y_re = lax.optimization_barrier(jnp.sum(k_re * w_re + k_im * w_im, axis=0))
            y_im = lax.optimization_barrier(jnp.sum(k_re * w_im - k_im * w_re, axis=0))
            return (y_re, y_im)
        plane_re, plane_im = lax.map(plane_terms, defocus_all)
        z_re, z_im = spectral_rows(row_cos, row_sin, lax.optimization_barrier(jnp.sum(plane_re, axis=0)), lax.optimization_barrier(jnp.sum(plane_im, axis=0)))
        return scale_norm * (product(z_re, col_cos) - product(z_im, col_sin))
    windows = lax.map(strip_terms, jnp.arange(STRIPS, dtype=jnp.int32))
    from_prev = jnp.pad(windows[:-1, MARGIN + ROWS:], ((1, 0), (0, 0), (0, 0)))
    from_next = jnp.pad(windows[1:, :MARGIN], ((0, 1), (0, 0), (0, 0)))
    folded = windows[:, MARGIN:MARGIN + ROWS]
    folded = folded.at[:, :MARGIN].add(from_prev).at[:, ROWS - MARGIN:].add(from_next)
    folded = folded.reshape(STRIPS * ROWS, COLS)
    mask_slope = 1.0 - jnp.tanh(phi) * jnp.tanh(phi)
    level_set = phi - step_size * mask_slope * folded
    for counter in range(SWEEPS):
        level_set = curvature_step(jnp.pad(level_set, 1))
    return level_set
```

```python
import jax
import jax.numpy as jnp
from jax import lax
from jax.sharding import PartitionSpec as P

MARGIN = 64
LEVELS = 31
SWEEPS = 2
HALO = SWEEPS


slope_resist = 4.0
level_resist = 0.5
step_size = 1.0
flow_rate = 0.2


def ring_shift(block, axis, step):
    count = lax.axis_size(axis)
    return lax.ppermute(block, axis, [(i, (i + step) % count) for i in range(count)])


def focus_sum(part):
    count = lax.axis_size("focus")
    total = part
    step = 1
    while step < count:
        held = lax.optimization_barrier(total.astype(jnp.bfloat16))
        other = lax.ppermute(held, "focus", [(i, i ^ step) for i in range(count)])
        total = held.astype(jnp.float32) + other.astype(jnp.float32)
        step *= 2
    return total


SIN_TERMS = (1.0, -1.0 / 6, 1.0 / 120, -1.0 / 5040, 1.0 / 362880, -1.0 / 39916800)
COS_TERMS = (1.0, -0.5, 1.0 / 24, -1.0 / 720, 1.0 / 40320, -1.0 / 3628800, 1.0 / 479001600)


def cos_sin(angle):
    half = 0.5 * angle
    square = half * half
    s = jnp.full_like(half, SIN_TERMS[-1])
    for term in SIN_TERMS[-2::-1]:
        s = s * square + term
    s = s * half
    c = jnp.full_like(half, COS_TERMS[-1])
    for term in COS_TERMS[-2::-1]:
        c = c * square + term
    return 1.0 - 2.0 * s * s, 2.0 * s * c


def tables(freq_list, positions, period):
    phase_int = jnp.mod(freq_list[:, None] * positions[None, :], period)
    phase_int = jnp.where(2 * phase_int >= period, phase_int - period, phase_int)
    angles = phase_int.astype(jnp.float32) * (2.0 * jnp.pi / period)
    cos_part, sin_part = cos_sin(angles)
    return cos_part.astype(jnp.bfloat16), sin_part.astype(jnp.bfloat16)


def product(lhs_mat, rhs_mat):
    return jnp.dot(lhs_mat, rhs_mat, preferred_element_type=jnp.float32)


def product_t(lhs_mat, rhs_mat):
    return lax.dot_general(
        lhs_mat, rhs_mat, (((1,), (1,)), ((), ())), preferred_element_type=jnp.float32
    )


def curvature_step(extended):
    padded = jnp.pad(extended, ((0, 0), (1, 1)))
    center = padded[1:-1, 1:-1]
    upper_row = padded[2:, 1:-1]
    lower_row = padded[:-2, 1:-1]
    right_col = padded[1:-1, 2:]
    left_col = padded[1:-1, :-2]
    diagonal = padded[2:, 2:] - padded[2:, :-2] - padded[:-2, 2:] + padded[:-2, :-2]
    grad_x = 0.5 * (upper_row - lower_row)
    grad_y = 0.5 * (right_col - left_col)
    second_x = upper_row - 2.0 * center + lower_row
    second_y = right_col - 2.0 * center + left_col
    cross_term = 0.25 * diagonal
    flow_term = (
        second_x * grad_y * grad_y - 2.0 * grad_x * grad_y * cross_term + second_y * grad_x * grad_x
    ) / (1.0 + grad_x * grad_x + grad_y * grad_y)
    return center + flow_rate * flow_term


def on_device(phi, target, defocus_ids, kernels, psi, row_freqs, col_freqs):
    strip_rows, col_count = phi.shape
    spectrum = psi.shape[1]
    kernel_count = kernels.shape[1]
    window_rows = strip_rows + 2 * MARGIN
    scale_norm = 1.0 / jnp.sqrt(jnp.float32(window_rows * col_count))
    strips = lax.axis_size("strip")
    place = lax.axis_index("strip")
    columns = jnp.arange(col_count, dtype=jnp.int32)
    col_cos, col_sin = tables(col_freqs, columns, col_count)
    row_cos, row_sin = tables(row_freqs, jnp.arange(window_rows, dtype=jnp.int32), window_rows)
    forward = jnp.concatenate([col_cos, -col_sin], axis=0)
    adjoint = jnp.concatenate([col_sin, col_cos], axis=0)
    inner_cos = row_cos[:, MARGIN : MARGIN + strip_rows]
    inner_sin = row_sin[:, MARGIN : MARGIN + strip_rows]
    mask = jnp.tanh(phi)
    mask_bf = mask.astype(jnp.bfloat16)
    edges = jnp.concatenate([phi[:HALO], phi[strip_rows - HALO :]], axis=0)
    edges_high = edges.astype(jnp.bfloat16)
    edges_low = (edges - edges_high.astype(jnp.float32)).astype(jnp.bfloat16)
    packet = jnp.concatenate([mask_bf, edges_high, edges_low], axis=0)
    above = ring_shift(packet, "strip", 1)
    below = ring_shift(packet, "strip", -1)
    above = jnp.where(place > 0, above, jnp.zeros_like(above))
    below = jnp.where(place < strips - 1, below, jnp.zeros_like(below))
    window = jnp.concatenate(
        [above[strip_rows - MARGIN : strip_rows], mask_bf, below[:MARGIN]], axis=0
    )
    above_edges = above[strip_rows:].astype(jnp.float32)
    below_edges = below[strip_rows:].astype(jnp.float32)
    above_phi = above_edges[HALO : 2 * HALO] + above_edges[3 * HALO :]
    below_phi = below_edges[:HALO] + below_edges[2 * HALO : 3 * HALO]
    tall_phi = jnp.concatenate([above_phi, phi, below_phi], axis=0)
    spec_pair = product_t(window, forward).astype(jnp.bfloat16)
    cos_half = product(row_cos, spec_pair)
    sin_half = product(row_sin, spec_pair)
    s_re = scale_norm * (cos_half[:, :spectrum] + sin_half[:, spectrum:])
    s_im = scale_norm * (cos_half[:, spectrum:] - sin_half[:, :spectrum])
    middle = (LEVELS - 1) / 2.0
    defocus = (defocus_ids[0].astype(jnp.float32) - middle) / middle
    phase_turn = defocus * psi
    cos_turn, sin_turn = cos_sin(phase_turn)
    k_re = kernels[0] * cos_turn - kernels[1] * sin_turn
    k_im = kernels[0] * sin_turn + kernels[1] * cos_turn
    g_pair = jnp.concatenate([k_re * s_re - k_im * s_im, k_re * s_im + k_im * s_re], axis=2).astype(
        jnp.bfloat16
    )
    head_part = jnp.einsum("fr,kfc->krc", inner_cos, g_pair, preferred_element_type=jnp.float32)
    tail_part = jnp.einsum("fr,kfc->krc", inner_sin, g_pair, preferred_element_type=jnp.float32)
    q_re = head_part[..., :spectrum] - tail_part[..., spectrum:]
    q_im = head_part[..., spectrum:] + tail_part[..., :spectrum]
    q_pair = (
        jnp.concatenate([q_re, q_im], axis=2)
        .astype(jnp.bfloat16)
        .reshape(kernel_count * strip_rows, 2 * spectrum)
    )
    e_re = (scale_norm * product(q_pair, forward)).reshape(kernel_count, strip_rows, col_count)
    e_im = (scale_norm * product(q_pair, adjoint)).reshape(kernel_count, strip_rows, col_count)
    intensity = jnp.mean(e_re * e_re + e_im * e_im, axis=0)
    resist = jax.nn.sigmoid(slope_resist * (intensity - level_resist))
    weight = (
        4.0
        * slope_resist
        / kernel_count
        * (resist - target.astype(jnp.float32))
        * resist
        * (1.0 - resist)
    )
    v_re = (weight * e_re).astype(jnp.bfloat16).reshape(kernel_count * strip_rows, col_count)
    v_im = (weight * e_im).astype(jnp.bfloat16).reshape(kernel_count * strip_rows, col_count)
    u_pair = (
        (product_t(v_re, forward) + product_t(v_im, adjoint))
        .astype(jnp.bfloat16)
        .reshape(kernel_count, strip_rows, 2 * spectrum)
    )
    head_back = jnp.einsum("fr,krc->kfc", inner_cos, u_pair, preferred_element_type=jnp.float32)
    tail_back = jnp.einsum("fr,krc->kfc", inner_sin, u_pair, preferred_element_type=jnp.float32)
    w_re = scale_norm * (head_back[..., :spectrum] + tail_back[..., spectrum:])
    w_im = scale_norm * (head_back[..., spectrum:] - tail_back[..., :spectrum])
    y_re = jnp.sum(k_re * w_re + k_im * w_im, axis=0)
    y_im = jnp.sum(k_re * w_im - k_im * w_re, axis=0)
    own = focus_sum(jnp.concatenate([y_re, y_im], axis=0)).astype(jnp.bfloat16)
    reach = (MARGIN + HALO + strip_rows - 1) // strip_rows
    rows = jnp.arange(-HALO, strip_rows + HALO, dtype=jnp.int32)
    groups = {}
    for offset in range(-reach, reach + 1):
        groups.setdefault(offset % strips, []).append(offset)
    z_pair = 0.0
    for shift, offsets in groups.items():
        spectra = own if shift == 0 else ring_shift(own, "strip", -shift)
        kept = 0.0
        for offset in offsets:
            spot = rows - offset * strip_rows + MARGIN
            valid = (spot >= 0) & (spot < window_rows)
            valid = valid & (place + offset >= 0) & (place + offset < strips)
            part_cos, part_sin = tables(row_freqs, spot, window_rows)
            weight_row = valid.astype(jnp.float32)[None, :]
            part = jnp.concatenate(
                [
                    jnp.concatenate([part_cos, part_sin], axis=1),
                    jnp.concatenate([-part_sin, part_cos], axis=1),
                ],
                axis=0,
            )
            kept = kept + part * jnp.concatenate([weight_row, weight_row], axis=1)
        z_pair = z_pair + lax.dot_general(
            kept.astype(jnp.bfloat16),
            spectra,
            (((0,), (0,)), ((), ())),
            preferred_element_type=jnp.float32,
        )
    tall = rows.shape[0]
    z_pair = jnp.concatenate([z_pair[:tall], z_pair[tall:]], axis=1).astype(jnp.bfloat16)
    gradient = scale_norm * product(z_pair, forward)
    tall_mask = jnp.tanh(tall_phi)
    level_set = tall_phi - step_size * (1.0 - tall_mask * tall_mask) * gradient
    inside = (rows + place * strip_rows >= 0) & (rows + place * strip_rows < strips * strip_rows)
    for counter in range(SWEEPS):
        trim = slice(counter, tall - counter)
        level_set = jnp.where(inside[trim, None], level_set, 0.0)
        level_set = curvature_step(level_set)
    return level_set


def solution(mesh):
    return jax.shard_map(
        on_device,
        mesh=mesh,
        in_specs=(
            P(("tile", "strip"), None),
            P(("tile", "strip"), None),
            P(("tile", "focus")),
            P(),
            P(),
            P(),
            P(),
        ),
        out_specs=P(("tile", "strip"), None),
        check_vma=False,
    )
```

```python
import functools

import jax
import jax.numpy as jnp
from jax import lax
from jax.experimental import pallas as pl
from jax.experimental.pallas import tpu as pltpu
from jax.sharding import PartitionSpec as P

MARGIN = 64
LEVELS = 31
SWEEPS = 2
HALO = SWEEPS
LANES = 128
PAD = 8
CHUNK = 256

slope_resist = 4.0
level_resist = 0.5
step_size = 1.0
flow_rate = 0.2

SIN_TERMS = (1.0, -1.0 / 6, 1.0 / 120, -1.0 / 5040, 1.0 / 362880, -1.0 / 39916800)
COS_TERMS = (1.0, -0.5, 1.0 / 24, -1.0 / 720, 1.0 / 40320, -1.0 / 3628800, 1.0 / 479001600)


def cos_sin(angle):
    half = 0.5 * angle
    square = half * half
    s = jnp.full_like(half, SIN_TERMS[-1])
    for term in SIN_TERMS[-2::-1]:
        s = s * square + term
    s = s * half
    c = jnp.full_like(half, COS_TERMS[-1])
    for term in COS_TERMS[-2::-1]:
        c = c * square + term
    return 1.0 - 2.0 * s * s, 2.0 * s * c


def turn(product, period):
    rest = product - jnp.round(product * (1.0 / period)) * period
    return cos_sin(rest * (2.0 * jnp.pi / period))


def mirrored(block):
    spots = (LANES - 1) - lax.broadcasted_iota(jnp.int32, block.shape, 1)
    return jnp.take_along_axis(block, spots, axis=1, mode="promise_in_bounds")


def dot(lhs_mat, rhs_mat):
    return jnp.dot(lhs_mat, rhs_mat, preferred_element_type=jnp.float32)


def dot_t(lhs_mat, rhs_mat):
    return lax.dot_general(
        lhs_mat, rhs_mat, (((1,), (1,)), ((), ())), preferred_element_type=jnp.float32
    )


def packet_kernel(phi_ref, out_ref):
    rows, cols = phi_ref.shape
    half = cols // 2
    for b in range(half // LANES):
        left = jnp.tanh(phi_ref[:, b * LANES : (b + 1) * LANES])
        right = mirrored(jnp.tanh(phi_ref[:, cols - (b + 1) * LANES : cols - b * LANES]))
        out_ref[:rows, b * LANES : (b + 1) * LANES] = (left + right).astype(jnp.bfloat16)
        out_ref[:rows, half + b * LANES : half + (b + 1) * LANES] = (left - right).astype(
            jnp.bfloat16
        )
    first = phi_ref[:HALO]
    last = phi_ref[rows - HALO :]
    first_high = first.astype(jnp.bfloat16).astype(jnp.float32)
    last_high = last.astype(jnp.bfloat16).astype(jnp.float32)
    filler = jnp.zeros((2 * PAD - 4 * HALO, cols), jnp.float32)
    edges = jnp.concatenate(
        [first_high, first - first_high, last_high, last - last_high, filler], axis=0
    )
    out_ref[rows:] = edges.astype(jnp.bfloat16)


def offset_groups(rows, strips):
    reach = (MARGIN + HALO + rows - 1) // rows
    groups = {}
    for offset in range(-reach, reach + 1):
        groups.setdefault(offset % strips, []).append(offset)
    return groups


def tables_kernel(
    rows,
    strips,
    groups,
    defocus_ref,
    row_freqs_ref,
    col_freqs_ref,
    kernels_ref,
    psi_ref,
    cos_ref,
    sin_ref,
    window_ref,
    inner_ref,
    inner_t_ref,
    tall_ref,
    k_re_ref,
    k_im_ref,
    freq_lanes,
):
    place = lax.axis_index("strip")
    fr = psi_ref.shape[0]
    fc, half = cos_ref.shape
    cols = 2 * half
    window = rows + 2 * MARGIN

    freqs = jnp.broadcast_to(col_freqs_ref[...].astype(jnp.float32), (8, fc)).T[:, :1]
    lane = lax.broadcasted_iota(jnp.int32, (fc, LANES), 1).astype(jnp.float32)
    c, s = turn(freqs * (2.0 * lane + 1.0), 2.0 * cols)
    step_c, step_s = turn(freqs * float(LANES), float(cols))
    step_c = jnp.broadcast_to(step_c, (fc, LANES))
    step_s = jnp.broadcast_to(step_s, (fc, LANES))
    for b in range(half // LANES):
        if b:
            c, s = c * step_c - s * step_s, s * step_c + c * step_s
        cos_ref[:, b * LANES : (b + 1) * LANES] = c.astype(jnp.bfloat16)
        sin_ref[:, b * LANES : (b + 1) * LANES] = s.astype(jnp.bfloat16)

    freq_lanes[...] = jnp.zeros_like(freq_lanes)
    freq_lanes[0:1, 0:fr] = row_freqs_ref[...].astype(jnp.float32)
    freq_lanes[0:1, fr : 2 * fr] = row_freqs_ref[...].astype(jnp.float32)
    across = freq_lanes[0:1, :]
    down = jnp.broadcast_to(across, (8, LANES)).T[: 2 * fr, :1]

    def rotation(length, first, down_first):
        shape = (2 * fr, 2 * length) if down_first else (2 * length, LANES)
        freq_dim, spot_dim = (0, 1) if down_first else (1, 0)
        spot = lax.broadcasted_iota(jnp.int32, shape, spot_dim)
        second = spot >= length
        spot = jnp.where(second, spot - length, spot) + first
        imag = lax.broadcasted_iota(jnp.int32, shape, freq_dim) >= fr
        c, s = turn((down if down_first else across) * spot.astype(jnp.float32), float(window))
        plain = second == imag
        return jnp.where(plain, c, jnp.where(second, s, -s)), spot

    table, spot = rotation(window, 0, True)
    keep = ((spot >= MARGIN) | (place > 0)) & ((spot < MARGIN + rows) | (place < strips - 1))
    window_ref[...] = jnp.where(keep, table, 0.0).astype(jnp.bfloat16)
    inner_ref[...] = rotation(rows, MARGIN, True)[0].astype(jnp.bfloat16)
    inner_t_ref[...] = rotation(rows, MARGIN, False)[0][:, : 2 * fr].astype(jnp.bfloat16)
    for index, offsets in enumerate(groups.values()):
        total = 0.0
        for offset in offsets:
            table, spot = rotation(rows + 2 * PAD, MARGIN - PAD - offset * rows, False)
            keep = (spot >= 0) & (spot < window)
            keep = keep & (place + offset >= 0) & (place + offset < strips)
            total = total + jnp.where(keep, table, 0.0)
        tall_ref[index] = total[:, : 2 * fr].astype(jnp.bfloat16)

    middle = (LEVELS - 1) / 2.0
    defocus = (defocus_ref[0].astype(jnp.float32) - middle) * (1.0 / middle)
    turn_c, turn_s = cos_sin(psi_ref[...] * defocus)
    for k in range(kernels_ref.shape[1]):
        k_re_ref[k] = kernels_ref[0, k] * turn_c - kernels_ref[1, k] * turn_s
        k_im_ref[k] = kernels_ref[0, k] * turn_s + kernels_ref[1, k] * turn_c


def main_kernel(
    own_ref,
    above_ref,
    below_ref,
    target_ref,
    cos_ref,
    sin_ref,
    window_ref,
    inner_ref,
    inner_t_ref,
    k_re_ref,
    k_im_ref,
    out_ref,
    q_ref,
    u_ref,
):
    rows, cols = target_ref.shape
    half = cols // 2
    count, fr, fc = k_re_ref.shape
    scale = 1.0 / float((rows + 2 * MARGIN) * cols) ** 0.5
    bf = jnp.bfloat16

    mask = jnp.concatenate(
        [above_ref[rows - MARGIN : rows], own_ref[:rows], below_ref[:MARGIN]], axis=0
    )
    p_re = dot_t(mask[:, :half], cos_ref[...])
    p_im = -dot_t(mask[:, half:], sin_ref[...])
    p = jnp.concatenate([p_re, p_im], axis=0).astype(bf)
    spec = scale * dot(window_ref[...], p)
    s_re, s_im = spec[:fr], spec[fr:]
    for k in range(count):
        k_re, k_im = k_re_ref[k], k_im_ref[k]
        g = jnp.concatenate([k_re * s_re - k_im * s_im, k_re * s_im + k_im * s_re], axis=0)
        q_ref[k * 2 * rows : (k + 1) * 2 * rows] = dot(inner_t_ref[...], g.astype(bf)).astype(bf)

    u_ref[...] = jnp.zeros_like(u_ref)
    gain = 4.0 * slope_resist / count * scale
    width = min(CHUNK, half)
    for start in range(0, half, width):
        cos_part = cos_ref[:, start : start + width]
        sin_part = sin_ref[:, start : start + width]
        af = dot(q_ref[...], cos_part)
        db = dot(q_ref[...], sin_part)
        even = 0.0
        cross = 0.0
        for k in range(count):
            a = af[2 * k * rows : (2 * k + 1) * rows]
            f = af[(2 * k + 1) * rows : (2 * k + 2) * rows]
            d = db[2 * k * rows : (2 * k + 1) * rows]
            b = db[(2 * k + 1) * rows : (2 * k + 2) * rows]
            even = even + ((a * a + f * f) + (d * d + b * b))
            cross = cross + (a * b - d * f)
        norm = scale * scale / count

        def weight(intensity, goal):
            resist = jax.nn.sigmoid(slope_resist * (norm * intensity - level_resist))
            return gain * (resist - goal) * resist * (1.0 - resist)

        goal_left = target_ref[:, start : start + width].astype(jnp.float32)
        goal_right = jnp.concatenate(
            [
                mirrored(
                    target_ref[:, cols - x - LANES : cols - x].astype(jnp.float32)
                )
                for x in range(start, start + width, LANES)
            ],
            axis=1,
        )
        w_left = weight(even - 2.0 * cross, goal_left)
        w_right = weight(even + 2.0 * cross, goal_right)
        p_w = w_left + w_right
        q_w = w_right - w_left
        x_cos = []
        x_sin = []
        for k in range(count):
            a = af[2 * k * rows : (2 * k + 1) * rows]
            f = af[(2 * k + 1) * rows : (2 * k + 2) * rows]
            d = db[2 * k * rows : (2 * k + 1) * rows]
            b = db[(2 * k + 1) * rows : (2 * k + 2) * rows]
            x_cos += [(p_w * a + q_w * b).astype(bf), (p_w * f - q_w * d).astype(bf)]
            x_sin += [(p_w * d - q_w * f).astype(bf), (q_w * a + p_w * b).astype(bf)]
        u_ref[...] += dot_t(jnp.concatenate(x_cos, axis=0), cos_part) + dot_t(
            jnp.concatenate(x_sin, axis=0), sin_part
        )

    y_re = 0.0
    y_im = 0.0
    for k in range(count):
        u = u_ref[k * 2 * rows : (k + 1) * 2 * rows].astype(bf)
        w = scale * dot(inner_ref[...], u)
        w_re, w_im = w[:fr], w[fr:]
        k_re, k_im = k_re_ref[k], k_im_ref[k]
        y_re = y_re + (k_re * w_re + k_im * w_im)
        y_im = y_im + (k_re * w_im - k_im * w_re)
    out_ref[:fr] = y_re.astype(bf)
    out_ref[fr:] = y_im.astype(bf)


def final_kernel(
    strips,
    count,
    phi_ref,
    above_ref,
    below_ref,
    cos_ref,
    sin_ref,
    tall_ref,
    *rest,
):
    spectra, (out_ref, level_ref, next_ref) = rest[:count], rest[count:]
    place = lax.axis_index("strip")
    rows, cols = phi_ref.shape
    half = cols // 2
    tall = rows + 2 * PAD
    bf = jnp.bfloat16
    scale = 1.0 / float((rows + 2 * MARGIN) * cols) ** 0.5

    z = 0.0
    for index in range(count):
        z = z + dot(tall_ref[index], spectra[index][...])
    z = z.astype(bf)
    even = dot(z[:tall], cos_ref[...])
    odd = dot(z[tall:], sin_ref[...])

    above = above_ref[rows:].astype(jnp.float32)
    below = below_ref[rows:].astype(jnp.float32)
    level_ref[:PAD] = jnp.zeros((PAD, cols), jnp.float32)
    level_ref[tall - PAD :] = jnp.zeros((PAD, cols), jnp.float32)
    level_ref[PAD - HALO : PAD] = above[2 * HALO : 3 * HALO] + above[3 * HALO : 4 * HALO]
    level_ref[PAD : PAD + rows] = phi_ref[...]
    level_ref[PAD + rows : PAD + rows + HALO] = below[:HALO] + below[HALO : 2 * HALO]
    down = lax.broadcasted_iota(jnp.int32, (tall, LANES), 0)
    inside = ((down >= PAD) | (place > 0)) & ((down < PAD + rows) | (place < strips - 1))

    def advance(start, grad):
        phi = level_ref[:, start : start + LANES]
        mask = jnp.tanh(phi)
        stepped = phi - step_size * (1.0 - mask * mask) * (scale * grad)
        level_ref[:, start : start + LANES] = jnp.where(inside, stepped, 0.0)

    for b in range(half // LANES):
        part = slice(b * LANES, (b + 1) * LANES)
        advance(b * LANES, even[:, part] - odd[:, part])
        advance(cols - (b + 1) * LANES, mirrored(even[:, part] + odd[:, part]))

    def sweep(source, first, number):
        center = source[first : first + number]
        upper = source[first + 1 : first + 1 + number]
        lower = source[first - 1 : first - 1 + number]
        lane = lax.broadcasted_iota(jnp.int32, (number, cols), 1)

        def beside(values):
            right = jnp.where(lane < cols - 1, pltpu.roll(values, cols - 1, 1), 0.0)
            left = jnp.where(lane > 0, pltpu.roll(values, 1, 1), 0.0)
            return right, left

        right, left = beside(center)
        slope = upper - lower
        slope_right, slope_left = beside(slope)
        grad_x = 0.5 * slope
        grad_y = 0.5 * (right - left)
        second_x = upper - 2.0 * center + lower
        second_y = right - 2.0 * center + left
        crossed = 0.25 * (slope_right - slope_left)
        flow = (
            second_x * grad_y * grad_y
            - 2.0 * grad_x * grad_y * crossed
            + second_y * grad_x * grad_x
        ) / (1.0 + grad_x * grad_x + grad_y * grad_y)
        return center + flow_rate * flow

    top_inside = place > 0
    low_inside = place < strips - 1
    for block in range(PAD - 1, PAD + rows + 1, 8):
        number = min(8, PAD + rows + 1 - block)
        swept = sweep(level_ref, block, number)
        spot = lax.broadcasted_iota(jnp.int32, (number, cols), 0) + block
        keep = ((spot >= PAD) | top_inside) & ((spot < PAD + rows) | low_inside)
        next_ref[block : block + number] = jnp.where(keep, swept, 0.0)
    for block in range(0, rows, 8):
        out_ref[block : block + 8] = sweep(next_ref, PAD + block, 8)


def vmem(count):
    return [pl.BlockSpec(memory_space=pltpu.VMEM)] * count


def call(kernel, out_shape, args, scratch=(), scalars=0, limit=24, flops=1000000):
    outs = out_shape if isinstance(out_shape, list) else [out_shape]
    single = not isinstance(out_shape, list)
    return pl.pallas_call(
        kernel,
        out_shape=out_shape,
        in_specs=[pl.BlockSpec(memory_space=pltpu.SMEM)] * scalars + vmem(len(args) - scalars),
        out_specs=vmem(1)[0] if single else vmem(len(outs)),
        scratch_shapes=list(scratch),
        compiler_params=pltpu.CompilerParams(vmem_limit_bytes=limit << 20),
        cost_estimate=pl.CostEstimate(flops=flops, bytes_accessed=4 << 20, transcendentals=0),
    )(*args)


def ring_shift(block, axis, step):
    count = lax.axis_size(axis)
    return lax.ppermute(block, axis, [(i, (i + step) % count) for i in range(count)])


def focus_sum(part):
    count = lax.axis_size("focus")
    step = 1
    while step < count:
        other = lax.ppermute(part, "focus", [(i, i ^ step) for i in range(count)])
        part = lax.optimization_barrier(
            (part.astype(jnp.float32) + other.astype(jnp.float32)).astype(jnp.bfloat16)
        )
        step *= 2
    return part


def on_device(phi, target, defocus_ids, kernels, psi, row_freqs, col_freqs):
    rows, cols = phi.shape
    half = cols // 2
    fr, fc = psi.shape
    count = kernels.shape[1]
    strips = lax.axis_size("strip")
    groups = offset_groups(rows, strips)
    tall = rows + 2 * PAD
    window = rows + 2 * MARGIN
    bf = jnp.bfloat16
    f32 = jnp.float32
    shape = jax.ShapeDtypeStruct

    packet = call(packet_kernel, shape((rows + 2 * PAD, cols), bf), (phi,))
    above = ring_shift(packet, "strip", 1)
    below = ring_shift(packet, "strip", -1)
    cos_t, sin_t, window_t, inner, inner_t, tall_t, k_re, k_im = call(
        functools.partial(tables_kernel, rows, strips, groups),
        [
            shape((fc, half), bf),
            shape((fc, half), bf),
            shape((2 * fr, 2 * window), bf),
            shape((2 * fr, 2 * rows), bf),
            shape((2 * rows, 2 * fr), bf),
            shape((len(groups), 2 * tall, 2 * fr), bf),
            shape((count, fr, fc), f32),
            shape((count, fr, fc), f32),
        ],
        (defocus_ids, row_freqs.reshape(1, fr), col_freqs.reshape(1, fc), kernels, psi),
        scratch=[pltpu.VMEM((8, LANES), f32)],
        scalars=1,
        flops=4000000000,
    )
    spectrum = call(
        main_kernel,
        shape((2 * fr, fc), bf),
        (packet, above, below, target, cos_t, sin_t, window_t, inner, inner_t, k_re, k_im),
        scratch=[
            pltpu.VMEM((count * 2 * rows, fc), bf),
            pltpu.VMEM((count * 2 * rows, fc), f32),
        ],
        limit=40,
        flops=4000000000,
    )
    own = focus_sum(spectrum)
    spectra = [own if turn_by == 0 else ring_shift(own, "strip", -turn_by) for turn_by in groups]
    return call(
        functools.partial(final_kernel, strips, len(spectra)),
        shape((rows, cols), f32),
        (phi, above, below, cos_t, sin_t, tall_t, *spectra),
        scratch=[pltpu.VMEM((tall, cols), f32), pltpu.VMEM((tall, cols), f32)],
        limit=24,
    )


def solution(mesh):
    return jax.shard_map(
        on_device,
        mesh=mesh,
        in_specs=(
            P(("tile", "strip"), None),
            P(("tile", "strip"), None),
            P(("tile", "focus")),
            P(),
            P(),
            P(),
            P(),
        ),
        out_specs=P(("tile", "strip"), None),
        check_vma=False,
    )
```

```python
import functools

import jax
import jax.numpy as jnp
from jax import lax
from jax.experimental import pallas as pl
from jax.experimental.pallas import tpu as pltpu
from jax.sharding import PartitionSpec as P

MARGIN = 64
LEVELS = 31
SWEEPS = 2
HALO = SWEEPS
LANES = 128
PAD = 8
CHUNK = 256

slope_resist = 4.0
level_resist = 0.5
step_size = 1.0
flow_rate = 0.2

SIN_TERMS = (1.0, -1.0 / 6, 1.0 / 120, -1.0 / 5040, 1.0 / 362880, -1.0 / 39916800)
COS_TERMS = (1.0, -0.5, 1.0 / 24, -1.0 / 720, 1.0 / 40320, -1.0 / 3628800, 1.0 / 479001600)


def cos_sin(angle):
    half = 0.5 * angle
    square = half * half
    s = jnp.full_like(half, SIN_TERMS[-1])
    for term in SIN_TERMS[-2::-1]:
        s = s * square + term
    s = s * half
    c = jnp.full_like(half, COS_TERMS[-1])
    for term in COS_TERMS[-2::-1]:
        c = c * square + term
    return 1.0 - 2.0 * s * s, 2.0 * s * c


def turn(product, period):
    rest = product - jnp.round(product * (1.0 / period)) * period
    return cos_sin(rest * (2.0 * jnp.pi / period))


def mirrored(block):
    spots = (LANES - 1) - lax.broadcasted_iota(jnp.int32, block.shape, 1)
    return jnp.take_along_axis(block, spots, axis=1, mode="promise_in_bounds")


def dot(lhs_mat, rhs_mat):
    return jnp.dot(lhs_mat, rhs_mat, preferred_element_type=jnp.float32)


def dot_t(lhs_mat, rhs_mat):
    return lax.dot_general(
        lhs_mat, rhs_mat, (((1,), (1,)), ((), ())), preferred_element_type=jnp.float32
    )


def offset_groups(rows, strips):
    reach = (MARGIN + HALO + rows - 1) // rows
    groups = {}
    for offset in range(-reach, reach + 1):
        if abs(offset) > 1:
            groups.setdefault(offset % strips, []).append(offset)
    return groups


def partners(strips):
    place = lax.axis_index("strip")
    first = jnp.where(place % 2 == 0, 1, -1)
    second = -first

    def inside(offset):
        return (place + offset >= 0) & (place + offset < strips)

    return place, first, second, inside(first), inside(second)


def rotation(freqs, shape, length, freq_dim, fr, start, period):
    spot = lax.broadcasted_iota(jnp.int32, shape, 1 - freq_dim)
    second = spot >= length
    spot = jnp.where(second, spot - length, spot) + start
    imag = lax.broadcasted_iota(jnp.int32, shape, freq_dim) >= fr
    c, s = turn(freqs * spot.astype(jnp.float32), float(period))
    return jnp.where(second == imag, c, jnp.where(second, s, -s)), spot


def row_freq_lanes(row_freqs_ref, freq_lanes):
    fr = row_freqs_ref.shape[1]
    freqs = row_freqs_ref[...].astype(jnp.float32)
    freq_lanes[...] = jnp.zeros_like(freq_lanes)
    freq_lanes[0:1, 0:fr] = freqs
    freq_lanes[0:1, fr : 2 * fr] = freqs
    across = freq_lanes[0:1, :]
    down = jnp.broadcast_to(across, (8, LANES)).T[: 2 * fr, :1]
    return across, down


def first_kernel(
    strips,
    phi_hbm,
    row_freqs_ref,
    col_freqs_ref,
    table_ref,
    own_ref,
    send_a_ref,
    send_b_ref,
    phi_ref,
    mask_ref,
    p_ref,
    freq_lanes,
    sem,
):
    rows, cols = phi_ref.shape
    half = cols // 2
    fr, fc = row_freqs_ref.shape[1], table_ref.shape[0]
    window = rows + 2 * MARGIN
    bf = jnp.bfloat16
    load = pltpu.make_async_copy(phi_hbm, phi_ref, sem)
    load.start()
    place, first, second, first_in, second_in = partners(strips)

    down = row_freq_lanes(row_freqs_ref, freq_lanes)[1]

    def rows_in(offset, keep):
        table, spot = rotation(
            down, (2 * fr, 2 * rows), rows, 0, fr, MARGIN - offset * rows, window
        )
        keep = keep & (spot >= 0) & (spot < window)
        return jnp.where(keep, table, 0.0).astype(bf)

    in_own = rows_in(0, True)
    in_a = rows_in(first, first_in)
    in_b = rows_in(second, second_in)

    freqs = jnp.broadcast_to(col_freqs_ref[...].astype(jnp.float32), (8, fc)).T[:, :1]

    def make_columns(start, number):
        f = freqs[start : start + number]
        spot = lax.broadcasted_iota(jnp.int32, (number, LANES), 1).astype(jnp.float32)
        c, s = turn(f * (2.0 * spot + 1.0), 2.0 * cols)
        step_c, step_s = turn(f * float(LANES), float(cols))
        step_c = jnp.broadcast_to(step_c, (number, LANES))
        step_s = jnp.broadcast_to(step_s, (number, LANES))
        for b in range(half // LANES):
            if b:
                c, s = c * step_c - s * step_s, s * step_c + c * step_s
            here = slice(start, start + number)
            table_ref[here, b * LANES : (b + 1) * LANES] = c.astype(bf)
            table_ref[here, half + b * LANES : half + (b + 1) * LANES] = s.astype(bf)

    def transform(start, number):
        here = slice(start, start + number)
        p_ref[:rows, here] = dot_t(mask_ref[:, :half], table_ref[here, :half]).astype(bf)
        p_ref[rows:, here] = (-dot_t(mask_ref[:, half:], table_ref[here, half:])).astype(bf)

    group = fc // 2
    piece = 64
    for start in range(0, group, piece):
        make_columns(start, piece)
    load.wait()
    for b in range(half // LANES):
        left = jnp.tanh(phi_ref[:, b * LANES : (b + 1) * LANES])
        right = mirrored(jnp.tanh(phi_ref[:, cols - (b + 1) * LANES : cols - b * LANES]))
        mask_ref[:, b * LANES : (b + 1) * LANES] = (left + right).astype(bf)
        mask_ref[:, half + b * LANES : half + (b + 1) * LANES] = (left - right).astype(bf)
    transform(0, group)
    for start in range(group, fc, piece):
        make_columns(start, piece)
    transform(group, fc - group)

    p = p_ref[...]
    send_b_ref[: 2 * fr] = dot(in_b, p).astype(bf)
    send_a_ref[: 2 * fr] = dot(in_a, p).astype(bf)
    own_ref[...] = dot(in_own, p)
    tops = [phi_ref[i : i + 1, q : q + fc] for i in range(HALO) for q in range(0, cols, fc)]
    lows = [
        phi_ref[rows - HALO + i : rows - HALO + i + 1, q : q + fc]
        for i in range(HALO)
        for q in range(0, cols, fc)
    ]
    tops = jnp.concatenate(tops, axis=0)
    lows = jnp.concatenate(lows, axis=0)
    send_a_ref[2 * fr :] = jnp.where(first > 0, lows, tops).astype(bf)
    send_b_ref[2 * fr :] = jnp.where(second > 0, lows, tops).astype(bf)


def second_kernel(
    strips,
    groups,
    defocus_ref,
    row_freqs_ref,
    kernels_ref,
    psi_ref,
    phi_ref,
    target_ref,
    inner_ref,
    inner_t_ref,
    tall_ref,
    far_ref,
    k_re_ref,
    k_im_ref,
    goal_ref,
    slope_ref,
    freq_lanes,
):
    rows, cols = phi_ref.shape
    half = cols // 2
    fr = psi_ref.shape[0]
    window = rows + 2 * MARGIN
    bf = jnp.bfloat16
    place, first, second, first_in, second_in = partners(strips)
    across, down = row_freq_lanes(row_freqs_ref, freq_lanes)

    inner_ref[...] = rotation(down, (2 * fr, 2 * rows), rows, 0, fr, MARGIN, window)[0].astype(bf)
    table = rotation(across, (2 * rows, LANES), rows, 1, fr, MARGIN, window)[0]
    inner_t_ref[...] = table[:, : 2 * fr].astype(bf)

    def rows_from(offset, keep, first_row, number):
        table, spot = rotation(
            across, (2 * number, LANES), number, 1, fr, first_row - offset * rows + MARGIN, window
        )
        keep = keep & (spot >= 0) & (spot < window)
        return jnp.where(keep, table, 0.0)

    tall = rows + 2 * PAD
    for index, (offset, keep) in enumerate(((0, True), (first, first_in), (second, second_in))):
        tall_ref[index] = rows_from(offset, keep, -PAD, tall)[:, : 2 * fr].astype(bf)
    for index, offsets in enumerate(groups.values()):
        total = jnp.zeros((4 * PAD, LANES), jnp.float32)
        for offset in offsets:
            keep = (place - offset >= 0) & (place - offset < strips)
            part = rows_from(offset, keep, -PAD if offset < 0 else rows, PAD)
            nothing = jnp.zeros((PAD, LANES), jnp.float32)
            if offset < 0:
                total = total + jnp.concatenate([part[:PAD], nothing, part[PAD:], nothing], axis=0)
            else:
                total = total + jnp.concatenate([nothing, part[:PAD], nothing, part[PAD:]], axis=0)
        far_ref[index] = total[:, : 2 * fr].astype(bf)

    middle = (LEVELS - 1) / 2.0
    defocus = (defocus_ref[0].astype(jnp.float32) - middle) * (1.0 / middle)
    turn_c, turn_s = cos_sin(psi_ref[...] * defocus)
    for k in range(kernels_ref.shape[1]):
        k_re_ref[k] = kernels_ref[0, k] * turn_c - kernels_ref[1, k] * turn_s
        k_im_ref[k] = kernels_ref[0, k] * turn_s + kernels_ref[1, k] * turn_c

    scale = 1.0 / float(window * cols) ** 0.5
    goal_ref[:, :half] = target_ref[:, :half].astype(jnp.float32)
    for b in range(half // LANES):
        goal_ref[:, half + b * LANES : half + (b + 1) * LANES] = mirrored(
            target_ref[:, cols - (b + 1) * LANES : cols - b * LANES].astype(jnp.float32)
        )
    mask = jnp.tanh(phi_ref[...])
    slope_ref[...] = (step_size * scale) * (1.0 - mask * mask)


def main_kernel(
    own_ref,
    from_a_ref,
    from_b_ref,
    goal_ref,
    table_ref,
    inner_ref,
    inner_t_ref,
    k_re_ref,
    k_im_ref,
    out_ref,
    q_ref,
    x_ref,
):
    rows, cols = goal_ref.shape
    half = cols // 2
    count, fr, fc = k_re_ref.shape
    scale = 1.0 / float((rows + 2 * MARGIN) * cols) ** 0.5
    bf = jnp.bfloat16
    f32 = jnp.float32

    spec = scale * (
        own_ref[...] + from_a_ref[: 2 * fr].astype(f32) + from_b_ref[: 2 * fr].astype(f32)
    )
    s_re, s_im = spec[:fr], spec[fr:]
    for k in range(count):
        k_re, k_im = k_re_ref[k], k_im_ref[k]
        g = jnp.concatenate([k_re * s_re - k_im * s_im, k_re * s_im + k_im * s_re], axis=0)
        q_ref[k * 2 * rows : (k + 1) * 2 * rows] = dot(inner_t_ref[...], g.astype(bf)).astype(bf)

    gain = 4.0 * slope_resist / count * scale
    norm = scale * scale / count

    def weight(intensity, goal):
        resist = jax.nn.sigmoid(slope_resist * (norm * intensity - level_resist))
        return gain * (resist - goal) * resist * (1.0 - resist)

    width = min(CHUNK, half)
    for start in range(0, half, width):
        left_half = slice(start, start + width)
        right_half = slice(half + start, half + start + width)
        af = dot(q_ref[...], table_ref[:, left_half])
        db = dot(q_ref[...], table_ref[:, right_half])

        def parts(k):
            re = slice(2 * k * rows, (2 * k + 1) * rows)
            im = slice((2 * k + 1) * rows, (2 * k + 2) * rows)
            return af[re], db[im], af[im], db[re], re, im

        even = 0.0
        cross = 0.0
        for k in range(count):
            a, b, f, d, _, _ = parts(k)
            even = even + ((a * a + f * f) + (d * d + b * b))
            cross = cross + (a * b - d * f)
        cross = 2.0 * cross
        w_left = weight(even - cross, goal_ref[:, left_half])
        w_right = weight(even + cross, goal_ref[:, right_half])
        p_w = w_left + w_right
        q_w = w_right - w_left
        for k in range(count):
            a, b, f, d, re, im = parts(k)
            x_ref[re, left_half] = (p_w * a + q_w * b).astype(bf)
            x_ref[im, left_half] = (p_w * f - q_w * d).astype(bf)
            x_ref[re, right_half] = (p_w * d - q_w * f).astype(bf)
            x_ref[im, right_half] = (q_w * a + p_w * b).astype(bf)

    y_re = 0.0
    y_im = 0.0
    for k in range(count):
        u = dot_t(x_ref[k * 2 * rows : (k + 1) * 2 * rows], table_ref[...]).astype(bf)
        w = scale * dot(inner_ref[...], u)
        w_re, w_im = w[:fr], w[fr:]
        k_re, k_im = k_re_ref[k], k_im_ref[k]
        y_re = y_re + (k_re * w_re + k_im * w_im)
        y_im = y_im + (k_re * w_im - k_im * w_re)
    out_ref[:fr] = y_re.astype(bf)
    out_ref[fr:] = y_im.astype(bf)


def sum_kernel(part_ref, other_ref, far_ref, total_ref, *payload_refs):
    total = part_ref[...].astype(jnp.float32) + other_ref[...].astype(jnp.float32)
    total = total.astype(jnp.bfloat16)
    total_ref[...] = total
    for index, payload_ref in enumerate(payload_refs):
        payload_ref[...] = dot(far_ref[index], total).astype(jnp.bfloat16)


def final_kernel(
    strips,
    phi_ref,
    slope_ref,
    from_a_ref,
    from_b_ref,
    table_ref,
    tall_ref,
    y_own_ref,
    y_a_ref,
    y_b_ref,
    *rest,
):
    payload_refs = rest[:-6]
    out_hbm, level_ref, next_ref, halo_ref, out_ref, sems = rest[-6:]
    place, first, second, _, _ = partners(strips)
    rows, cols = phi_ref.shape
    half = cols // 2
    blocks = cols // LANES
    tall = rows + 2 * PAD
    fc = y_own_ref.shape[1]
    lead = y_own_ref.shape[0]
    bf = jnp.bfloat16
    f32 = jnp.float32
    scale = 1.0 / float((rows + 2 * MARGIN) * cols) ** 0.5

    z = dot(tall_ref[0], y_own_ref[...])
    z = z + dot(tall_ref[1], y_a_ref[...]) + dot(tall_ref[2], y_b_ref[...])
    for payload_ref in payload_refs:
        far = payload_ref[...].astype(f32)
        nothing = jnp.zeros((rows, fc), f32)
        z = z + jnp.concatenate(
            [
                far[:PAD],
                nothing,
                far[PAD : 2 * PAD],
                far[2 * PAD : 3 * PAD],
                nothing,
                far[3 * PAD :],
            ],
            axis=0,
        )
    z = z.astype(bf)
    even = dot(z[:tall], table_ref[:, :half])
    odd = dot(z[tall:], table_ref[:, half:])

    halo_ref[...] = jnp.zeros_like(halo_ref)
    edges_a = from_a_ref[lead:].astype(f32)
    edges_b = from_b_ref[lead:].astype(f32)
    above = jnp.where(first < 0, edges_a, edges_b)
    below = jnp.where(first < 0, edges_b, edges_a)
    per_row = cols // fc
    for i in range(HALO):
        for q in range(per_row):
            here = slice(q * fc, (q + 1) * fc)
            spot = i * per_row + q
            halo_ref[PAD - HALO + i : PAD - HALO + i + 1, here] = above[spot : spot + 1]
            halo_ref[PAD + i : PAD + i + 1, here] = below[spot : spot + 1]
    top_in = place > 0
    low_in = place < strips - 1

    def advance(b, grad):
        here = slice(b * LANES, (b + 1) * LANES)
        level_ref[b, PAD : PAD + rows] = phi_ref[:, here] - slope_ref[:, here] * grad[
            PAD : PAD + rows
        ]
        for inside, edge, to in ((top_in, 0, 0), (low_in, PAD, PAD + rows)):
            phi = halo_ref[edge : edge + PAD, here]
            mask = jnp.tanh(phi)
            slope = (step_size * scale) * (1.0 - mask * mask)
            level_ref[b, to : to + PAD] = jnp.where(
                inside, phi - slope * grad[to : to + PAD], 0.0
            )

    for b in range(half // LANES):
        part = slice(b * LANES, (b + 1) * LANES)
        advance(b, even[:, part] - odd[:, part])
        advance(blocks - 1 - b, mirrored(even[:, part] + odd[:, part]))

    lane = lax.broadcasted_iota(jnp.int32, (8, LANES), 1)

    def sweep(source, first_row, store):
        center, rise, turned = [], [], []
        nothing = jnp.zeros((8, LANES), f32)
        for b in range(blocks):
            c = source[b, first_row : first_row + 8]
            u = source[b, first_row + 1 : first_row + 9]
            d = source[b, first_row - 1 : first_row + 7]
            x = u - d
            center.append(c)
            rise.append((x, (u + d) - 2.0 * c))
            turned.append(
                (
                    pltpu.roll(c, LANES - 1, 1),
                    pltpu.roll(c, 1, 1),
                    pltpu.roll(x, LANES - 1, 1),
                    pltpu.roll(x, 1, 1),
                )
            )
        for b in range(blocks):
            after = turned[b + 1] if b + 1 < blocks else (nothing,) * 4
            before = turned[b - 1] if b else (nothing,) * 4
            right = jnp.where(lane == LANES - 1, after[0], turned[b][0])
            left = jnp.where(lane == 0, before[1], turned[b][1])
            x_right = jnp.where(lane == LANES - 1, after[2], turned[b][2])
            x_left = jnp.where(lane == 0, before[3], turned[b][3])
            c = center[b]
            x, second_x = rise[b]
            y = right - left
            second_y = (right + left) - 2.0 * c
            x_x = x * x
            y_y = y * y
            numer = second_x * y_y + second_y * x_x - (0.5 * x) * y * (x_right - x_left)
            store(b, c + flow_rate * (numer / (4.0 + x_x + y_y)))

    starts = list(range(PAD - 1, PAD + rows - 7, 8))
    if starts[-1] + 8 < PAD + rows + 1:
        starts.append(PAD + rows - 7)
    for at in starts:
        spot = lax.broadcasted_iota(jnp.int32, (8, LANES), 0) + at
        keep = ((spot >= PAD) | top_in) & ((spot < PAD + rows) | low_in)
        edge = at < PAD or at + 8 > PAD + rows

        def store_next(b, value):
            next_ref[b, at : at + 8] = jnp.where(keep, value, 0.0) if edge else value

        sweep(level_ref, at, store_next)

    copies = []
    for index in range(rows // 8):

        def store_out(b, value):
            out_ref[8 * index : 8 * index + 8, b * LANES : (b + 1) * LANES] = value

        sweep(next_ref, PAD + 8 * index, store_out)
        here = pl.ds(8 * index, 8)
        copies.append(pltpu.make_async_copy(out_ref.at[here], out_hbm.at[here], sems.at[index]))
        copies[-1].start()
    for copy in copies:
        copy.wait()


def spec(kind):
    return pl.BlockSpec(memory_space={"v": pltpu.VMEM, "s": pltpu.SMEM, "h": pltpu.HBM}[kind])


def call(kernel, outs, args, kinds=None, out_kinds=None, scratch=(), limit=24, flops=1000000):
    kinds = kinds or "v" * len(args)
    out_kinds = out_kinds or "v" * len(outs)
    return pl.pallas_call(
        kernel,
        out_shape=outs,
        in_specs=[spec(kind) for kind in kinds],
        out_specs=[spec(kind) for kind in out_kinds],
        scratch_shapes=list(scratch),
        compiler_params=pltpu.CompilerParams(vmem_limit_bytes=limit << 20),
        cost_estimate=pl.CostEstimate(flops=flops, bytes_accessed=4 << 20, transcendentals=0),
    )(*args)


def pair_up(block, first):
    count = lax.axis_size("strip")
    low = range(0 if first else 1, count, 2)
    pairs = [(i, (i + 1) % count) for i in low]
    return lax.ppermute(block, "strip", pairs + [(b, a) for a, b in pairs])


def on_device(phi, target, defocus_ids, kernels, psi, row_freqs, col_freqs):
    rows, cols = phi.shape
    half = cols // 2
    fr, fc = psi.shape
    count = kernels.shape[1]
    strips = lax.axis_size("strip")
    planes = lax.axis_size("focus")
    groups = offset_groups(rows, strips)
    tall = rows + 2 * PAD
    bf = jnp.bfloat16
    f32 = jnp.float32
    shape = jax.ShapeDtypeStruct
    lanes = pltpu.VMEM((8, LANES), f32)
    packet = shape((2 * fr + HALO * (cols // fc), fc), bf)
    row_freqs = row_freqs.reshape(1, fr)

    table, s_own, send_a, send_b = call(
        functools.partial(first_kernel, strips),
        [shape((fc, cols), bf), shape((2 * fr, fc), f32), packet, packet],
        (phi, row_freqs, col_freqs.reshape(1, fc)),
        kinds="hvv",
        scratch=[
            pltpu.VMEM((rows, cols), f32),
            pltpu.VMEM((rows, cols), bf),
            pltpu.VMEM((2 * rows, fc), bf),
            lanes,
            pltpu.SemaphoreType.DMA(()),
        ],
    )
    from_b = pair_up(send_b, False)
    from_a = pair_up(send_a, True)
    inner, inner_t, tall_t, far_t, k_re, k_im, goal, slope = call(
        functools.partial(second_kernel, strips, groups),
        [
            shape((2 * fr, 2 * rows), bf),
            shape((2 * rows, 2 * fr), bf),
            shape((3, 2 * tall, 2 * fr), bf),
            shape((max(1, len(groups)), 4 * PAD, 2 * fr), bf),
            shape((count, fr, fc), f32),
            shape((count, fr, fc), f32),
            shape((rows, cols), f32),
            shape((rows, cols), f32),
        ],
        (defocus_ids, row_freqs, kernels, psi, phi, target),
        kinds="svvvvv",
        scratch=[lanes],
        flops=4000000000,
    )
    (part,) = call(
        main_kernel,
        [shape((2 * fr, fc), bf)],
        (s_own, from_a, from_b, goal, table, inner, inner_t, k_re, k_im),
        scratch=[
            pltpu.VMEM((count * 2 * rows, fc), bf),
            pltpu.VMEM((count * 2 * rows, cols), bf),
        ],
        flops=4000000000,
    )
    step = 1
    other = jnp.zeros_like(part)
    while step < planes:
        if step > 1:
            part = lax.optimization_barrier(
                (part.astype(f32) + other.astype(f32)).astype(bf)
            )
        other = lax.ppermute(part, "focus", [(i, i ^ step) for i in range(planes)])
        step *= 2
    total, *payloads = call(
        sum_kernel,
        [shape((2 * fr, fc), bf)] + [shape((4 * PAD, fc), bf)] * len(groups),
        (part, other, far_t),
    )
    far = [
        lax.ppermute(payload, "strip", [(i, (i - turn_by) % strips) for i in range(strips)])
        for turn_by, payload in zip(groups, payloads)
    ]
    y_b = pair_up(total, False)
    y_a = pair_up(total, True)
    return call(
        functools.partial(final_kernel, strips),
        [shape((rows, cols), f32)],
        (phi, slope, from_a, from_b, table, tall_t, total, y_a, y_b, *far),
        out_kinds="h",
        scratch=[
            pltpu.VMEM((cols // LANES, tall, LANES), f32),
            pltpu.VMEM((cols // LANES, tall, LANES), f32),
            pltpu.VMEM((2 * PAD, cols), f32),
            pltpu.VMEM((rows, cols), f32),
            pltpu.SemaphoreType.DMA((rows // 8,)),
        ],
    )[0]


def solution(mesh):
    return jax.shard_map(
        on_device,
        mesh=mesh,
        in_specs=(
            P(("tile", "strip"), None),
            P(("tile", "strip"), None),
            P(("tile", "focus")),
            P(),
            P(),
            P(),
            P(),
        ),
        out_specs=P(("tile", "strip"), None),
        check_vma=False,
    )
```

```python
import functools

import jax
import jax.numpy as jnp
from jax import lax
from jax.experimental import pallas as pl
from jax.experimental.pallas import tpu as pltpu
from jax.sharding import PartitionSpec as P

MARGIN = 64
LEVELS = 31
SWEEPS = 2
HALO = SWEEPS
LANES = 128
PAD = 8
CHUNK = 256

slope_resist = 4.0
level_resist = 0.5
step_size = 1.0
flow_rate = 0.2

SIN_TERMS = (1.0, -1.0 / 6, 1.0 / 120, -1.0 / 5040, 1.0 / 362880, -1.0 / 39916800)
COS_TERMS = (1.0, -0.5, 1.0 / 24, -1.0 / 720, 1.0 / 40320, -1.0 / 3628800, 1.0 / 479001600)


def cos_sin(angle):
    half = 0.5 * angle
    square = half * half
    s = jnp.full_like(half, SIN_TERMS[-1])
    for term in SIN_TERMS[-2::-1]:
        s = s * square + term
    s = s * half
    c = jnp.full_like(half, COS_TERMS[-1])
    for term in COS_TERMS[-2::-1]:
        c = c * square + term
    return 1.0 - 2.0 * s * s, 2.0 * s * c


def turn(product, period):
    rest = product - jnp.round(product * (1.0 / period)) * period
    return cos_sin(rest * (2.0 * jnp.pi / period))


def mirrored(block):
    spots = (LANES - 1) - lax.broadcasted_iota(jnp.int32, block.shape, 1)
    return jnp.take_along_axis(block, spots, axis=1, mode="promise_in_bounds")


def dot(lhs_mat, rhs_mat):
    return jnp.dot(lhs_mat, rhs_mat, preferred_element_type=jnp.float32)


def dot_t(lhs_mat, rhs_mat):
    return lax.dot_general(
        lhs_mat, rhs_mat, (((1,), (1,)), ((), ())), preferred_element_type=jnp.float32
    )


def offset_groups(rows, strips):
    reach = (MARGIN + HALO + rows - 1) // rows
    groups = {}
    for offset in range(-reach, reach + 1):
        if abs(offset) > 1:
            groups.setdefault(offset % strips, []).append(offset)
    return groups


def partners(strips):
    place = lax.axis_index("strip")
    first = jnp.where(place % 2 == 0, 1, -1)
    second = -first

    def inside(offset):
        return (place + offset >= 0) & (place + offset < strips)

    return place, first, second, inside(first), inside(second)


def quarter(second, imag, c, s):
    return jnp.where(second == imag, c, jnp.where(second, s, -s))


def rotation(freqs, shape, length, freq_dim, fr, start, period):
    spot = lax.broadcasted_iota(jnp.int32, shape, 1 - freq_dim)
    second = spot >= length
    spot = jnp.where(second, spot - length, spot) + start
    imag = lax.broadcasted_iota(jnp.int32, shape, freq_dim) >= fr
    c, s = turn(freqs * spot.astype(jnp.float32), float(period))
    return quarter(second, imag, c, s), spot


def interleaved(freqs, shape, freq_dim, fr, start, period):
    index = lax.broadcasted_iota(jnp.int32, shape, 1 - freq_dim)
    spot = ((index >> 4) << 3) + (index & 7) + start
    second = (index & 8) > 0
    imag = lax.broadcasted_iota(jnp.int32, shape, freq_dim) >= fr
    c, s = turn(freqs * spot.astype(jnp.float32), float(period))
    return quarter(second, imag, c, s)


def row_freq_lanes(row_freqs_ref, freq_ref):
    fr = row_freqs_ref.shape[1]
    freqs = jnp.broadcast_to(row_freqs_ref[...].astype(jnp.float32), (8, fr))
    freq_ref[...] = jnp.zeros_like(freq_ref)
    freq_ref[:, 0:fr] = freqs
    freq_ref[:, fr : 2 * fr] = freqs


def first_kernel(
    strips,
    phi_hbm,
    row_freqs_hbm,
    col_freqs_hbm,
    table_ref,
    own_ref,
    send_a_ref,
    send_b_ref,
    phi_ref,
    freq_ref,
    mask_ref,
    p_ref,
    row_freqs_ref,
    col_freqs_ref,
    sems,
):
    rows, cols = phi_ref.shape
    half = cols // 2
    fr, fc = row_freqs_ref.shape[1], table_ref.shape[0]
    window = rows + 2 * MARGIN
    bf = jnp.bfloat16
    load_cols = pltpu.make_async_copy(col_freqs_hbm, col_freqs_ref, sems.at[0])
    load_rows = pltpu.make_async_copy(row_freqs_hbm, row_freqs_ref, sems.at[1])
    load_phi = pltpu.make_async_copy(phi_hbm, phi_ref, sems.at[2])
    load_cols.start()
    load_rows.start()
    load_phi.start()
    place, first, second, first_in, second_in = partners(strips)

    load_cols.wait()
    freqs = jnp.broadcast_to(col_freqs_ref[...].astype(jnp.float32), (8, fc)).T[:, :1]

    def make_columns(start, number):
        f = freqs[start : start + number]
        spot = lax.broadcasted_iota(jnp.int32, (number, LANES), 1).astype(jnp.float32)
        c, s = turn(f * (2.0 * spot + 1.0), 2.0 * cols)
        step_c, step_s = turn(f * float(LANES), float(cols))
        step_c = jnp.broadcast_to(step_c, (number, LANES))
        step_s = jnp.broadcast_to(step_s, (number, LANES))
        twice = 2.0 * step_c
        c_old, s_old = c, s
        here = slice(start, start + number)
        for b in range(half // LANES):
            if b == 1:
                c, s = c * step_c - s * step_s, s * step_c + c * step_s
            elif b:
                c, s, c_old, s_old = twice * c - c_old, twice * s - s_old, c, s
            table_ref[here, b * LANES : (b + 1) * LANES] = c.astype(bf)
            table_ref[here, half + b * LANES : half + (b + 1) * LANES] = s.astype(bf)

    def transform(start, number):
        here = slice(start, start + number)
        p_ref[:rows, here] = dot_t(mask_ref[:, :half], table_ref[here, :half]).astype(bf)
        p_ref[rows:, here] = (-dot_t(mask_ref[:, half:], table_ref[here, half:])).astype(bf)

    group = fc // 2
    piece = 64
    for start in range(0, group, piece):
        make_columns(start, piece)
    load_rows.wait()
    load_phi.wait()
    for b in range(half // LANES):
        left = jnp.tanh(phi_ref[:, b * LANES : (b + 1) * LANES])
        right = mirrored(jnp.tanh(phi_ref[:, cols - (b + 1) * LANES : cols - b * LANES]))
        mask_ref[:, b * LANES : (b + 1) * LANES] = (left + right).astype(bf)
        mask_ref[:, half + b * LANES : half + (b + 1) * LANES] = (left - right).astype(bf)
    transform(0, group)
    for start in range(group, fc, piece):
        make_columns(start, piece)
    transform(group, fc - group)

    row_freq_lanes(row_freqs_ref, freq_ref)
    down = freq_ref[...].T[:fr, :1]
    spot = lax.broadcasted_iota(jnp.int32, (fr, 2 * rows), 1)
    later = spot >= rows
    spot = jnp.where(later, spot - rows, spot)
    c, s = turn(down * (spot + MARGIN).astype(jnp.float32), float(window))
    turn_c, turn_s = turn(down * float(rows), float(window))
    turn_c = jnp.broadcast_to(turn_c, c.shape)
    turn_s = jnp.broadcast_to(turn_s, c.shape)

    def rows_in(c, s, offset, keep):
        at = spot + MARGIN - offset * rows
        keep = keep & (at >= 0) & (at < window)
        c = jnp.where(keep, c, 0.0)
        s = jnp.where(keep, s, 0.0)
        return jnp.concatenate([jnp.where(later, s, c), jnp.where(later, c, -s)], axis=0).astype(bf)

    in_own = rows_in(c, s, 0, True)
    sign = -first.astype(jnp.float32)
    in_a = rows_in(c * turn_c - s * (sign * turn_s), s * turn_c + c * (sign * turn_s), first, first_in)
    in_b = rows_in(
        c * turn_c + s * (sign * turn_s), s * turn_c - c * (sign * turn_s), second, second_in
    )

    p = p_ref[...]
    send_b_ref[: 2 * fr] = dot(in_b, p).astype(bf)
    send_a_ref[: 2 * fr] = dot(in_a, p).astype(bf)
    own_ref[...] = dot(in_own, p)
    tops = [phi_ref[i : i + 1, q : q + fc] for i in range(HALO) for q in range(0, cols, fc)]
    lows = [
        phi_ref[rows - HALO + i : rows - HALO + i + 1, q : q + fc]
        for i in range(HALO)
        for q in range(0, cols, fc)
    ]
    tops = jnp.concatenate(tops, axis=0)
    lows = jnp.concatenate(lows, axis=0)
    send_a_ref[2 * fr :] = jnp.where(first > 0, lows, tops).astype(bf)
    send_b_ref[2 * fr :] = jnp.where(second > 0, lows, tops).astype(bf)


def second_kernel(
    strips,
    groups,
    defocus_ref,
    freq_ref,
    phi_ref,
    kernels_hbm,
    psi_hbm,
    target_hbm,
    inner_ref,
    inner_t_ref,
    tall_ref,
    far_ref,
    k_re_ref,
    k_im_ref,
    goal_ref,
    slope_ref,
    kernels_ref,
    psi_ref,
    target_ref,
    sems,
):
    rows, cols = phi_ref.shape
    half = cols // 2
    fr = psi_ref.shape[0]
    load_psi = pltpu.make_async_copy(psi_hbm, psi_ref, sems.at[0])
    load_kernels = pltpu.make_async_copy(kernels_hbm, kernels_ref, sems.at[1])
    load_target = pltpu.make_async_copy(target_hbm, target_ref, sems.at[2])
    load_psi.start()
    load_kernels.start()
    load_target.start()
    window = rows + 2 * MARGIN
    bf = jnp.bfloat16
    place, first, second, first_in, second_in = partners(strips)
    across = freq_ref[0:1, :]
    down = freq_ref[...].T[: 2 * fr, :1]

    inner_ref[...] = interleaved(down, (2 * fr, 2 * rows), 0, fr, MARGIN, window).astype(bf)
    table = interleaved(across, (2 * rows, LANES), 1, fr, MARGIN, window)
    inner_t_ref[...] = table[:, : 2 * fr].astype(bf)

    def rows_from(offset, keep, first_row, number):
        table, spot = rotation(
            across, (2 * number, LANES), number, 1, fr, first_row - offset * rows + MARGIN, window
        )
        keep = keep & (spot >= 0) & (spot < window)
        return jnp.where(keep, table, 0.0)

    tall = rows + 2 * PAD
    for index, (offset, keep) in enumerate(((0, True), (first, first_in), (second, second_in))):
        tall_ref[index] = rows_from(offset, keep, -PAD, tall)[:, : 2 * fr].astype(bf)
    for index, offsets in enumerate(groups.values()):
        total = jnp.zeros((4 * PAD, LANES), jnp.float32)
        for offset in offsets:
            keep = (place - offset >= 0) & (place - offset < strips)
            part = rows_from(offset, keep, -PAD if offset < 0 else rows, PAD)
            nothing = jnp.zeros((PAD, LANES), jnp.float32)
            if offset < 0:
                total = total + jnp.concatenate([part[:PAD], nothing, part[PAD:], nothing], axis=0)
            else:
                total = total + jnp.concatenate([nothing, part[:PAD], nothing, part[PAD:]], axis=0)
        far_ref[index] = total[:, : 2 * fr].astype(bf)

    scale = 1.0 / float(window * cols) ** 0.5
    mask = jnp.tanh(phi_ref[...])
    slope_ref[...] = (step_size * scale) * (1.0 - mask * mask)

    load_psi.wait()
    load_kernels.wait()
    middle = (LEVELS - 1) / 2.0
    defocus = (defocus_ref[0].astype(jnp.float32) - middle) * (1.0 / middle)
    turn_c, turn_s = cos_sin(psi_ref[...] * defocus)
    for k in range(kernels_ref.shape[1]):
        k_re_ref[k] = kernels_ref[0, k] * turn_c - kernels_ref[1, k] * turn_s
        k_im_ref[k] = kernels_ref[0, k] * turn_s + kernels_ref[1, k] * turn_c

    load_target.wait()
    goal_ref[:, :half] = target_ref[:, :half].astype(jnp.float32)
    for b in range(half // LANES):
        goal_ref[:, half + b * LANES : half + (b + 1) * LANES] = mirrored(
            target_ref[:, cols - (b + 1) * LANES : cols - b * LANES].astype(jnp.float32)
        )


def main_kernel(
    own_ref,
    from_a_ref,
    from_b_ref,
    goal_ref,
    table_ref,
    inner_ref,
    inner_t_ref,
    k_re_ref,
    k_im_ref,
    out_ref,
    q_ref,
    x_ref,
):
    rows, cols = goal_ref.shape
    half = cols // 2
    count, fr, fc = k_re_ref.shape
    scale = 1.0 / float((rows + 2 * MARGIN) * cols) ** 0.5
    bf = jnp.bfloat16
    f32 = jnp.float32

    spec = scale * (
        own_ref[...] + from_a_ref[: 2 * fr].astype(f32) + from_b_ref[: 2 * fr].astype(f32)
    )
    s_re, s_im = spec[:fr], spec[fr:]
    unit = 16 * count
    for k in range(count):
        k_re, k_im = k_re_ref[k], k_im_ref[k]
        g = jnp.concatenate([k_re * s_re - k_im * s_im, k_re * s_im + k_im * s_re], axis=0)
        q = dot(inner_t_ref[...], g.astype(bf)).astype(bf)
        for r in range(rows // 8):
            q_ref[r * unit + 16 * k : r * unit + 16 * k + 16] = q[16 * r : 16 * r + 16]

    gain = 4.0 * slope_resist / count * scale
    norm = scale * scale / count

    def weight(intensity, goal):
        resist = jax.nn.sigmoid(slope_resist * (norm * intensity - level_resist))
        return gain * (resist - goal) * resist * (1.0 - resist)

    width = min(CHUNK, half)
    for start in range(0, half, width):
        left_half = slice(start, start + width)
        right_half = slice(half + start, half + start + width)
        af = dot(q_ref[...], table_ref[:, left_half])
        db = dot(q_ref[...], table_ref[:, right_half])
        for r in range(rows // 8):

            def parts(k):
                at = r * unit + 16 * k
                return af[at : at + 8], db[at + 8 : at + 16], af[at + 8 : at + 16], db[at : at + 8]

            even = 0.0
            cross = 0.0
            for k in range(count):
                a, b, f, d = parts(k)
                even = even + ((a * a + f * f) + (d * d + b * b))
                cross = cross + (a * b - d * f)
            cross = 2.0 * cross
            here = slice(8 * r, 8 * r + 8)
            w_left = weight(even - cross, goal_ref[here, left_half])
            w_right = weight(even + cross, goal_ref[here, right_half])
            p_w = w_left + w_right
            q_w = w_right - w_left
            for k in range(count):
                a, b, f, d = parts(k)
                at = slice(r * unit + 16 * k, r * unit + 16 * k + 16)
                x_ref[at, left_half] = jnp.concatenate(
                    [p_w * a + q_w * b, p_w * f - q_w * d], axis=0
                ).astype(bf)
                x_ref[at, right_half] = jnp.concatenate(
                    [p_w * d - q_w * f, q_w * a + p_w * b], axis=0
                ).astype(bf)

    q_ref[...] = dot_t(x_ref[...], table_ref[...]).astype(bf)
    y_re = 0.0
    y_im = 0.0
    for k in range(count):
        u = jnp.concatenate(
            [q_ref[r * unit + 16 * k : r * unit + 16 * k + 16] for r in range(rows // 8)], axis=0
        )
        w = scale * dot(inner_ref[...], u)
        w_re, w_im = w[:fr], w[fr:]
        k_re, k_im = k_re_ref[k], k_im_ref[k]
        y_re = y_re + (k_re * w_re + k_im * w_im)
        y_im = y_im + (k_re * w_im - k_im * w_re)
    out_ref[:fr] = y_re.astype(bf)
    out_ref[fr:] = y_im.astype(bf)


def sum_kernel(part_ref, other_ref, far_ref, total_ref, *payload_refs):
    total = part_ref[...].astype(jnp.float32) + other_ref[...].astype(jnp.float32)
    total = total.astype(jnp.bfloat16)
    total_ref[...] = total
    for index, payload_ref in enumerate(payload_refs):
        payload_ref[...] = dot(far_ref[index], total).astype(jnp.bfloat16)


def final_kernel(
    strips,
    phi_ref,
    slope_ref,
    from_a_ref,
    from_b_ref,
    table_ref,
    tall_ref,
    y_own_ref,
    y_a_ref,
    y_b_ref,
    *rest,
):
    payload_refs = rest[:-6]
    out_hbm, level_ref, next_ref, halo_ref, out_ref, sems = rest[-6:]
    place, first, second, _, _ = partners(strips)
    rows, cols = phi_ref.shape
    half = cols // 2
    blocks = cols // LANES
    tall = rows + 2 * PAD
    fc = y_own_ref.shape[1]
    lead = y_own_ref.shape[0]
    bf = jnp.bfloat16
    f32 = jnp.float32
    scale = 1.0 / float((rows + 2 * MARGIN) * cols) ** 0.5

    z = dot(tall_ref[0], y_own_ref[...])
    z = z + dot(tall_ref[1], y_a_ref[...]) + dot(tall_ref[2], y_b_ref[...])
    for payload_ref in payload_refs:
        far = payload_ref[...].astype(f32)
        nothing = jnp.zeros((rows, fc), f32)
        z = z + jnp.concatenate(
            [
                far[:PAD],
                nothing,
                far[PAD : 2 * PAD],
                far[2 * PAD : 3 * PAD],
                nothing,
                far[3 * PAD :],
            ],
            axis=0,
        )
    z = z.astype(bf)
    even = dot(z[:tall], table_ref[:, :half])
    odd = dot(z[tall:], table_ref[:, half:])

    halo_ref[...] = jnp.zeros_like(halo_ref)
    edges_a = from_a_ref[lead:].astype(f32)
    edges_b = from_b_ref[lead:].astype(f32)
    above = jnp.where(first < 0, edges_a, edges_b)
    below = jnp.where(first < 0, edges_b, edges_a)
    per_row = cols // fc
    for i in range(HALO):
        for q in range(per_row):
            here = slice(q * fc, (q + 1) * fc)
            spot = i * per_row + q
            halo_ref[PAD - HALO + i : PAD - HALO + i + 1, here] = above[spot : spot + 1]
            halo_ref[PAD + i : PAD + i + 1, here] = below[spot : spot + 1]
    top_in = place > 0
    low_in = place < strips - 1

    def advance(b, grad):
        here = slice(b * LANES, (b + 1) * LANES)
        level_ref[b, PAD : PAD + rows] = phi_ref[:, here] - slope_ref[:, here] * grad[
            PAD : PAD + rows
        ]
        for inside, edge, to in ((top_in, 0, 0), (low_in, PAD, PAD + rows)):
            phi = halo_ref[edge : edge + PAD, here]
            mask = jnp.tanh(phi)
            slope = (step_size * scale) * (1.0 - mask * mask)
            level_ref[b, to : to + PAD] = jnp.where(
                inside, phi - slope * grad[to : to + PAD], 0.0
            )

    for b in range(half // LANES):
        part = slice(b * LANES, (b + 1) * LANES)
        advance(b, even[:, part] - odd[:, part])
        advance(blocks - 1 - b, mirrored(even[:, part] + odd[:, part]))

    lane = lax.broadcasted_iota(jnp.int32, (8, LANES), 1)

    def sweep(source, first_row, store):
        center, rise, turned = [], [], []
        nothing = jnp.zeros((8, LANES), f32)
        for b in range(blocks):
            c = source[b, first_row : first_row + 8]
            u = source[b, first_row + 1 : first_row + 9]
            d = source[b, first_row - 1 : first_row + 7]
            x = u - d
            center.append(c)
            rise.append((x, (u + d) - 2.0 * c))
            turned.append(
                (
                    pltpu.roll(c, LANES - 1, 1),
                    pltpu.roll(c, 1, 1),
                    pltpu.roll(x, LANES - 1, 1),
                    pltpu.roll(x, 1, 1),
                )
            )
        for b in range(blocks):
            after = turned[b + 1] if b + 1 < blocks else (nothing,) * 4
            before = turned[b - 1] if b else (nothing,) * 4
            right = jnp.where(lane == LANES - 1, after[0], turned[b][0])
            left = jnp.where(lane == 0, before[1], turned[b][1])
            x_right = jnp.where(lane == LANES - 1, after[2], turned[b][2])
            x_left = jnp.where(lane == 0, before[3], turned[b][3])
            c = center[b]
            x, second_x = rise[b]
            y = right - left
            second_y = (right + left) - 2.0 * c
            x_x = x * x
            y_y = y * y
            numer = second_x * y_y + second_y * x_x - (0.5 * x) * y * (x_right - x_left)
            store(b, c + flow_rate * (numer / (4.0 + x_x + y_y)))

    starts = list(range(PAD - 1, PAD + rows - 7, 8))
    if starts[-1] + 8 < PAD + rows + 1:
        starts.append(PAD + rows - 7)
    for at in starts:
        spot = lax.broadcasted_iota(jnp.int32, (8, LANES), 0) + at
        keep = ((spot >= PAD) | top_in) & ((spot < PAD + rows) | low_in)
        edge = at < PAD or at + 8 > PAD + rows

        def store_next(b, value):
            next_ref[b, at : at + 8] = jnp.where(keep, value, 0.0) if edge else value

        sweep(level_ref, at, store_next)

    copies = []
    for index in range(rows // 8):

        def store_out(b, value):
            out_ref[8 * index : 8 * index + 8, b * LANES : (b + 1) * LANES] = value

        sweep(next_ref, PAD + 8 * index, store_out)
        here = pl.ds(8 * index, 8)
        copies.append(pltpu.make_async_copy(out_ref.at[here], out_hbm.at[here], sems.at[index]))
        copies[-1].start()
    for copy in copies:
        copy.wait()


def spec(kind):
    return pl.BlockSpec(memory_space={"v": pltpu.VMEM, "s": pltpu.SMEM, "h": pltpu.HBM}[kind])


def call(kernel, outs, args, kinds=None, out_kinds=None, scratch=(), limit=24, flops=1000000):
    kinds = kinds or "v" * len(args)
    out_kinds = out_kinds or "v" * len(outs)
    return pl.pallas_call(
        kernel,
        out_shape=outs,
        in_specs=[spec(kind) for kind in kinds],
        out_specs=[spec(kind) for kind in out_kinds],
        scratch_shapes=list(scratch),
        compiler_params=pltpu.CompilerParams(vmem_limit_bytes=limit << 20),
        cost_estimate=pl.CostEstimate(flops=flops, bytes_accessed=4 << 20, transcendentals=0),
    )(*args)


def pair_up(block, first):
    count = lax.axis_size("strip")
    low = range(0 if first else 1, count, 2)
    pairs = [(i, (i + 1) % count) for i in low]
    return lax.ppermute(block, "strip", pairs + [(b, a) for a, b in pairs])


def on_device(phi, target, defocus_ids, kernels, psi, row_freqs, col_freqs):
    rows, cols = phi.shape
    half = cols // 2
    fr, fc = psi.shape
    count = kernels.shape[1]
    strips = lax.axis_size("strip")
    planes = lax.axis_size("focus")
    groups = offset_groups(rows, strips)
    tall = rows + 2 * PAD
    bf = jnp.bfloat16
    f32 = jnp.float32
    shape = jax.ShapeDtypeStruct
    packet = shape((2 * fr + HALO * (cols // fc), fc), bf)
    row_freqs = row_freqs.reshape(1, fr)

    table, s_own, send_a, send_b, phi, freqs = call(
        functools.partial(first_kernel, strips),
        [
            shape((fc, cols), bf),
            shape((2 * fr, fc), f32),
            packet,
            packet,
            shape((rows, cols), f32),
            shape((8, LANES), f32),
        ],
        (phi, row_freqs, col_freqs.reshape(1, fc)),
        kinds="hhh",
        scratch=[
            pltpu.VMEM((rows, cols), bf),
            pltpu.VMEM((2 * rows, fc), bf),
            pltpu.VMEM((1, fr), jnp.int32),
            pltpu.VMEM((1, fc), jnp.int32),
            pltpu.SemaphoreType.DMA((3,)),
        ],
    )
    from_b = pair_up(send_b, False)
    from_a = pair_up(send_a, True)
    inner, inner_t, tall_t, far_t, k_re, k_im, goal, slope = call(
        functools.partial(second_kernel, strips, groups),
        [
            shape((2 * fr, 2 * rows), bf),
            shape((2 * rows, 2 * fr), bf),
            shape((3, 2 * tall, 2 * fr), bf),
            shape((max(1, len(groups)), 4 * PAD, 2 * fr), bf),
            shape((count, fr, fc), f32),
            shape((count, fr, fc), f32),
            shape((rows, cols), f32),
            shape((rows, cols), f32),
        ],
        (defocus_ids, freqs, phi, kernels, psi, target),
        kinds="svvhhh",
        scratch=[
            pltpu.VMEM(kernels.shape, f32),
            pltpu.VMEM(psi.shape, f32),
            pltpu.VMEM(target.shape, jnp.int32),
            pltpu.SemaphoreType.DMA((3,)),
        ],
        flops=4000000000,
    )
    (part,) = call(
        main_kernel,
        [shape((2 * fr, fc), bf)],
        (s_own, from_a, from_b, goal, table, inner, inner_t, k_re, k_im),
        scratch=[
            pltpu.VMEM((count * 2 * rows, fc), bf),
            pltpu.VMEM((count * 2 * rows, cols), bf),
        ],
        flops=4000000000,
    )
    step = 1
    other = jnp.zeros_like(part)
    while step < planes:
        if step > 1:
            part = lax.optimization_barrier(
                (part.astype(f32) + other.astype(f32)).astype(bf)
            )
        other = lax.ppermute(part, "focus", [(i, i ^ step) for i in range(planes)])
        step *= 2
    total, *payloads = call(
        sum_kernel,
        [shape((2 * fr, fc), bf)] + [shape((4 * PAD, fc), bf)] * len(groups),
        (part, other, far_t),
    )
    far = [
        lax.ppermute(payload, "strip", [(i, (i - turn_by) % strips) for i in range(strips)])
        for turn_by, payload in zip(groups, payloads)
    ]
    y_b = pair_up(total, False)
    y_a = pair_up(total, True)
    return call(
        functools.partial(final_kernel, strips),
        [shape((rows, cols), f32)],
        (phi, slope, from_a, from_b, table, tall_t, total, y_a, y_b, *far),
        out_kinds="h",
        scratch=[
            pltpu.VMEM((cols // LANES, tall, LANES), f32),
            pltpu.VMEM((cols // LANES, tall, LANES), f32),
            pltpu.VMEM((2 * PAD, cols), f32),
            pltpu.VMEM((rows, cols), f32),
            pltpu.SemaphoreType.DMA((rows // 8,)),
        ],
    )[0]


def solution(mesh):
    return jax.shard_map(
        on_device,
        mesh=mesh,
        in_specs=(
            P(("tile", "strip"), None),
            P(("tile", "strip"), None),
            P(("tile", "focus")),
            P(),
            P(),
            P(),
            P(),
        ),
        out_specs=P(("tile", "strip"), None),
        check_vma=False,
    )
```

```python
import functools

import jax
import jax.numpy as jnp
from jax import lax
from jax.experimental import pallas as pl
from jax.experimental.pallas import tpu as pltpu
from jax.sharding import PartitionSpec as P

MARGIN = 64
LEVELS = 31
SWEEPS = 2
HALO = SWEEPS
LANES = 128
PAD = 8
CHUNK = 256

slope_resist = 4.0
level_resist = 0.5
step_size = 1.0
flow_rate = 0.2

SIN_TERMS = (1.0, -1.0 / 6, 1.0 / 120, -1.0 / 5040, 1.0 / 362880, -1.0 / 39916800)
COS_TERMS = (1.0, -0.5, 1.0 / 24, -1.0 / 720, 1.0 / 40320, -1.0 / 3628800, 1.0 / 479001600)


def cos_sin(angle):
    half = 0.5 * angle
    square = half * half
    s = jnp.full_like(half, SIN_TERMS[-1])
    for term in SIN_TERMS[-2::-1]:
        s = s * square + term
    s = s * half
    c = jnp.full_like(half, COS_TERMS[-1])
    for term in COS_TERMS[-2::-1]:
        c = c * square + term
    return 1.0 - 2.0 * s * s, 2.0 * s * c


def turn(product, period):
    rest = product - jnp.round(product * (1.0 / period)) * period
    return cos_sin(rest * (2.0 * jnp.pi / period))


def mirrored(block):
    spots = (LANES - 1) - lax.broadcasted_iota(jnp.int32, block.shape, 1)
    return jnp.take_along_axis(block, spots, axis=1, mode="promise_in_bounds")


def dot(lhs_mat, rhs_mat):
    return jnp.dot(lhs_mat, rhs_mat, preferred_element_type=jnp.float32)


def dot_t(lhs_mat, rhs_mat):
    return lax.dot_general(
        lhs_mat, rhs_mat, (((1,), (1,)), ((), ())), preferred_element_type=jnp.float32
    )


def offset_groups(rows, strips):
    reach = (MARGIN + HALO + rows - 1) // rows
    groups = {}
    for offset in range(-reach, reach + 1):
        if abs(offset) > 1:
            groups.setdefault(offset % strips, []).append(offset)
    return groups


def partners(strips):
    place = lax.axis_index("strip")
    first = jnp.where(place % 2 == 0, 1, -1)
    second = -first

    def inside(offset):
        return (place + offset >= 0) & (place + offset < strips)

    return place, first, second, inside(first), inside(second)


def quarter(second, imag, c, s):
    return jnp.where(second == imag, c, jnp.where(second, s, -s))


def rotation(freqs, shape, length, freq_dim, fr, start, period):
    spot = lax.broadcasted_iota(jnp.int32, shape, 1 - freq_dim)
    second = spot >= length
    spot = jnp.where(second, spot - length, spot) + start
    imag = lax.broadcasted_iota(jnp.int32, shape, freq_dim) >= fr
    c, s = turn(freqs * spot.astype(jnp.float32), float(period))
    return quarter(second, imag, c, s), spot


def interleaved(freqs, shape, freq_dim, fr, start, period):
    index = lax.broadcasted_iota(jnp.int32, shape, 1 - freq_dim)
    spot = ((index >> 4) << 3) + (index & 7) + start
    second = (index & 8) > 0
    imag = lax.broadcasted_iota(jnp.int32, shape, freq_dim) >= fr
    c, s = turn(freqs * spot.astype(jnp.float32), float(period))
    return quarter(second, imag, c, s)


def row_freq_lanes(row_freqs_ref, freq_ref):
    fr = row_freqs_ref.shape[1]
    freqs = jnp.broadcast_to(row_freqs_ref[...].astype(jnp.float32), (8, fr))
    freq_ref[...] = jnp.zeros_like(freq_ref)
    freq_ref[:, 0:fr] = freqs
    freq_ref[:, fr : 2 * fr] = freqs


def first_kernel(
    strips,
    phi_hbm,
    row_freqs_hbm,
    col_freqs_hbm,
    table_ref,
    own_ref,
    send_a_ref,
    send_b_ref,
    phi_ref,
    freq_ref,
    mask_ref,
    p_ref,
    row_freqs_ref,
    col_freqs_ref,
    sems,
):
    rows, cols = phi_ref.shape
    half = cols // 2
    fr, fc = row_freqs_ref.shape[1], table_ref.shape[0]
    window = rows + 2 * MARGIN
    bf = jnp.bfloat16
    load_cols = pltpu.make_async_copy(col_freqs_hbm, col_freqs_ref, sems.at[0])
    load_rows = pltpu.make_async_copy(row_freqs_hbm, row_freqs_ref, sems.at[1])
    load_phi = pltpu.make_async_copy(phi_hbm, phi_ref, sems.at[2])
    load_cols.start()
    load_rows.start()
    load_phi.start()
    place, first, second, first_in, second_in = partners(strips)

    load_cols.wait()
    freqs = jnp.broadcast_to(col_freqs_ref[...].astype(jnp.float32), (8, fc)).T[:, :1]

    def make_columns(start, number):
        f = freqs[start : start + number]
        spot = lax.broadcasted_iota(jnp.int32, (number, LANES), 1).astype(jnp.float32)
        c, s = turn(f * (2.0 * spot + 1.0), 2.0 * cols)
        step_c, step_s = turn(f * float(LANES), float(cols))
        step_c = jnp.broadcast_to(step_c, (number, LANES))
        step_s = jnp.broadcast_to(step_s, (number, LANES))
        twice = 2.0 * step_c
        c_old, s_old = c, s
        here = slice(start, start + number)
        for b in range(half // LANES):
            if b == 1:
                c, s = c * step_c - s * step_s, s * step_c + c * step_s
            elif b:
                c, s, c_old, s_old = twice * c - c_old, twice * s - s_old, c, s
            table_ref[here, b * LANES : (b + 1) * LANES] = c.astype(bf)
            table_ref[here, half + b * LANES : half + (b + 1) * LANES] = s.astype(bf)

    def transform(start, number):
        here = slice(start, start + number)
        p_ref[:rows, here] = dot_t(mask_ref[:, :half], table_ref[here, :half]).astype(bf)
        p_ref[rows:, here] = (-dot_t(mask_ref[:, half:], table_ref[here, half:])).astype(bf)

    group = fc // 2
    piece = 64
    for start in range(0, group, piece):
        make_columns(start, piece)
    load_rows.wait()
    load_phi.wait()
    for b in range(half // LANES):
        left = jnp.tanh(phi_ref[:, b * LANES : (b + 1) * LANES])
        right = mirrored(jnp.tanh(phi_ref[:, cols - (b + 1) * LANES : cols - b * LANES]))
        mask_ref[:, b * LANES : (b + 1) * LANES] = (left + right).astype(bf)
        mask_ref[:, half + b * LANES : half + (b + 1) * LANES] = (left - right).astype(bf)
    transform(0, group)
    for start in range(group, fc, piece):
        make_columns(start, piece)
    transform(group, fc - group)

    row_freq_lanes(row_freqs_ref, freq_ref)
    down = freq_ref[...].T[:fr, :1]
    spot = lax.broadcasted_iota(jnp.int32, (fr, 2 * rows), 1)
    later = spot >= rows
    spot = jnp.where(later, spot - rows, spot)
    c, s = turn(down * (spot + MARGIN).astype(jnp.float32), float(window))
    turn_c, turn_s = turn(down * float(rows), float(window))
    turn_c = jnp.broadcast_to(turn_c, c.shape)
    turn_s = jnp.broadcast_to(turn_s, c.shape)

    def rows_in(c, s, offset, keep):
        at = spot + MARGIN - offset * rows
        keep = keep & (at >= 0) & (at < window)
        c = jnp.where(keep, c, 0.0)
        s = jnp.where(keep, s, 0.0)
        return jnp.concatenate([jnp.where(later, s, c), jnp.where(later, c, -s)], axis=0).astype(bf)

    in_own = rows_in(c, s, 0, True)
    sign = -first.astype(jnp.float32)
    in_a = rows_in(c * turn_c - s * (sign * turn_s), s * turn_c + c * (sign * turn_s), first, first_in)
    in_b = rows_in(
        c * turn_c + s * (sign * turn_s), s * turn_c - c * (sign * turn_s), second, second_in
    )

    p = p_ref[...]
    send_b_ref[: 2 * fr] = dot(in_b, p).astype(bf)
    send_a_ref[: 2 * fr] = dot(in_a, p).astype(bf)
    own_ref[...] = dot(in_own, p)
    tops = [phi_ref[i : i + 1, q : q + fc] for i in range(HALO) for q in range(0, cols, fc)]
    lows = [
        phi_ref[rows - HALO + i : rows - HALO + i + 1, q : q + fc]
        for i in range(HALO)
        for q in range(0, cols, fc)
    ]
    tops = jnp.concatenate(tops, axis=0)
    lows = jnp.concatenate(lows, axis=0)
    send_a_ref[2 * fr :] = jnp.where(first > 0, lows, tops).astype(bf)
    send_b_ref[2 * fr :] = jnp.where(second > 0, lows, tops).astype(bf)


def second_kernel(
    strips,
    groups,
    defocus_ref,
    freq_ref,
    phi_ref,
    kernels_hbm,
    psi_hbm,
    target_hbm,
    inner_ref,
    inner_t_ref,
    tall_ref,
    far_ref,
    k_re_ref,
    k_im_ref,
    goal_ref,
    slope_ref,
    kernels_ref,
    psi_ref,
    target_ref,
    sems,
):
    rows, cols = phi_ref.shape
    half = cols // 2
    fr = psi_ref.shape[0]
    load_psi = pltpu.make_async_copy(psi_hbm, psi_ref, sems.at[0])
    load_kernels = pltpu.make_async_copy(kernels_hbm, kernels_ref, sems.at[1])
    load_target = pltpu.make_async_copy(target_hbm, target_ref, sems.at[2])
    load_psi.start()
    load_kernels.start()
    load_target.start()
    window = rows + 2 * MARGIN
    bf = jnp.bfloat16
    place, first, second, first_in, second_in = partners(strips)
    across = freq_ref[0:1, :]
    down = freq_ref[...].T[: 2 * fr, :1]

    inner_ref[...] = interleaved(down, (2 * fr, 2 * rows), 0, fr, MARGIN, window).astype(bf)
    table = interleaved(across, (2 * rows, LANES), 1, fr, MARGIN, window)
    inner_t_ref[...] = table[:, : 2 * fr].astype(bf)

    def rows_from(offset, keep, first_row, number):
        table, spot = rotation(
            across, (2 * number, LANES), number, 1, fr, first_row - offset * rows + MARGIN, window
        )
        keep = keep & (spot >= 0) & (spot < window)
        return jnp.where(keep, table, 0.0)

    tall = rows + 2 * PAD
    for index, (offset, keep) in enumerate(((0, True), (first, first_in), (second, second_in))):
        tall_ref[index] = rows_from(offset, keep, -PAD, tall)[:, : 2 * fr].astype(bf)
    for index, offsets in enumerate(groups.values()):
        total = jnp.zeros((4 * PAD, LANES), jnp.float32)
        for offset in offsets:
            keep = (place - offset >= 0) & (place - offset < strips)
            part = rows_from(offset, keep, -PAD if offset < 0 else rows, PAD)
            nothing = jnp.zeros((PAD, LANES), jnp.float32)
            if offset < 0:
                total = total + jnp.concatenate([part[:PAD], nothing, part[PAD:], nothing], axis=0)
            else:
                total = total + jnp.concatenate([nothing, part[:PAD], nothing, part[PAD:]], axis=0)
        far_ref[index] = total[:, : 2 * fr].astype(bf)

    scale = 1.0 / float(window * cols) ** 0.5
    mask = jnp.tanh(phi_ref[...])
    slope_ref[...] = (step_size * scale) * (1.0 - mask * mask)

    load_psi.wait()
    load_kernels.wait()
    middle = (LEVELS - 1) / 2.0
    defocus = (defocus_ref[0].astype(jnp.float32) - middle) * (1.0 / middle)
    turn_c, turn_s = cos_sin(psi_ref[...] * defocus)
    for k in range(kernels_ref.shape[1]):
        k_re_ref[k] = kernels_ref[0, k] * turn_c - kernels_ref[1, k] * turn_s
        k_im_ref[k] = kernels_ref[0, k] * turn_s + kernels_ref[1, k] * turn_c

    load_target.wait()
    goal_ref[:, :half] = target_ref[:, :half].astype(jnp.float32)
    for b in range(half // LANES):
        goal_ref[:, half + b * LANES : half + (b + 1) * LANES] = mirrored(
            target_ref[:, cols - (b + 1) * LANES : cols - b * LANES].astype(jnp.float32)
        )


def main_kernel(
    own_ref,
    from_a_ref,
    from_b_ref,
    goal_ref,
    table_ref,
    inner_ref,
    inner_t_ref,
    k_re_ref,
    k_im_ref,
    out_ref,
    q_ref,
    x_ref,
):
    rows, cols = goal_ref.shape
    half = cols // 2
    count, fr, fc = k_re_ref.shape
    scale = 1.0 / float((rows + 2 * MARGIN) * cols) ** 0.5
    bf = jnp.bfloat16
    f32 = jnp.float32

    spec = scale * (
        own_ref[...] + from_a_ref[: 2 * fr].astype(f32) + from_b_ref[: 2 * fr].astype(f32)
    )
    s_re, s_im = spec[:fr], spec[fr:]
    unit = 16 * count
    for k in range(count):
        k_re, k_im = k_re_ref[k], k_im_ref[k]
        g = jnp.concatenate([k_re * s_re - k_im * s_im, k_re * s_im + k_im * s_re], axis=0)
        q = dot(inner_t_ref[...], g.astype(bf)).astype(bf)
        for r in range(rows // 8):
            q_ref[r * unit + 16 * k : r * unit + 16 * k + 16] = q[16 * r : 16 * r + 16]

    gain = 4.0 * slope_resist / count * scale
    norm = scale * scale / count

    def weight(intensity, goal):
        resist = jax.nn.sigmoid(slope_resist * (norm * intensity - level_resist))
        return gain * (resist - goal) * resist * (1.0 - resist)

    width = min(CHUNK, half)
    for start in range(0, half, width):
        left_half = slice(start, start + width)
        right_half = slice(half + start, half + start + width)
        af = dot(q_ref[...], table_ref[:, left_half])
        db = dot(q_ref[...], table_ref[:, right_half])
        for r in range(rows // 8):

            def parts(k):
                at = r * unit + 16 * k
                return af[at : at + 8], db[at + 8 : at + 16], af[at + 8 : at + 16], db[at : at + 8]

            even = 0.0
            cross = 0.0
            for k in range(count):
                a, b, f, d = parts(k)
                even = even + ((a * a + f * f) + (d * d + b * b))
                cross = cross + (a * b - d * f)
            cross = 2.0 * cross
            here = slice(8 * r, 8 * r + 8)
            w_left = weight(even - cross, goal_ref[here, left_half])
            w_right = weight(even + cross, goal_ref[here, right_half])
            p_w = w_left + w_right
            q_w = w_right - w_left
            for k in range(count):
                a, b, f, d = parts(k)
                at = slice(r * unit + 16 * k, r * unit + 16 * k + 16)
                x_ref[at, left_half] = jnp.concatenate(
                    [p_w * a + q_w * b, p_w * f - q_w * d], axis=0
                ).astype(bf)
                x_ref[at, right_half] = jnp.concatenate(
                    [p_w * d - q_w * f, q_w * a + p_w * b], axis=0
                ).astype(bf)

    q_ref[...] = dot_t(x_ref[...], table_ref[...]).astype(bf)
    y_re = 0.0
    y_im = 0.0
    for k in range(count):
        u = jnp.concatenate(
            [q_ref[r * unit + 16 * k : r * unit + 16 * k + 16] for r in range(rows // 8)], axis=0
        )
        w = scale * dot(inner_ref[...], u)
        w_re, w_im = w[:fr], w[fr:]
        k_re, k_im = k_re_ref[k], k_im_ref[k]
        y_re = y_re + (k_re * w_re + k_im * w_im)
        y_im = y_im + (k_re * w_im - k_im * w_re)
    out_ref[:fr] = y_re.astype(bf)
    out_ref[fr:] = y_im.astype(bf)


def sum_kernel(part_ref, other_ref, far_ref, total_ref, *payload_refs):
    total = part_ref[...].astype(jnp.float32) + other_ref[...].astype(jnp.float32)
    total = total.astype(jnp.bfloat16)
    total_ref[...] = total
    for index, payload_ref in enumerate(payload_refs):
        payload_ref[...] = dot(far_ref[index], total).astype(jnp.bfloat16)


def final_kernel(
    strips,
    phi_ref,
    slope_ref,
    from_a_ref,
    from_b_ref,
    table_ref,
    tall_ref,
    y_own_ref,
    y_a_ref,
    y_b_ref,
    *rest,
):
    payload_refs = rest[:-6]
    out_hbm, level_ref, next_ref, halo_ref, out_ref, sems = rest[-6:]
    place, first, second, _, _ = partners(strips)
    rows, cols = phi_ref.shape
    half = cols // 2
    blocks = cols // LANES
    tall = rows + 2 * PAD
    fc = y_own_ref.shape[1]
    lead = y_own_ref.shape[0]
    bf = jnp.bfloat16
    f32 = jnp.float32
    scale = 1.0 / float((rows + 2 * MARGIN) * cols) ** 0.5

    z = dot(tall_ref[0], y_own_ref[...])
    z = z + dot(tall_ref[1], y_a_ref[...]) + dot(tall_ref[2], y_b_ref[...])
    for payload_ref in payload_refs:
        far = payload_ref[...].astype(f32)
        nothing = jnp.zeros((rows, fc), f32)
        z = z + jnp.concatenate(
            [
                far[:PAD],
                nothing,
                far[PAD : 2 * PAD],
                far[2 * PAD : 3 * PAD],
                nothing,
                far[3 * PAD :],
            ],
            axis=0,
        )
    z = z.astype(bf)
    even = dot(z[:tall], table_ref[:, :half])
    odd = dot(z[tall:], table_ref[:, half:])

    halo_ref[...] = jnp.zeros_like(halo_ref)
    edges_a = from_a_ref[lead:].astype(f32)
    edges_b = from_b_ref[lead:].astype(f32)
    above = jnp.where(first < 0, edges_a, edges_b)
    below = jnp.where(first < 0, edges_b, edges_a)
    per_row = cols // fc
    for i in range(HALO):
        for q in range(per_row):
            here = slice(q * fc, (q + 1) * fc)
            spot = i * per_row + q
            halo_ref[PAD - HALO + i : PAD - HALO + i + 1, here] = above[spot : spot + 1]
            halo_ref[PAD + i : PAD + i + 1, here] = below[spot : spot + 1]
    top_in = place > 0
    low_in = place < strips - 1

    def advance(b, grad):
        here = slice(b * LANES, (b + 1) * LANES)
        level_ref[b, PAD : PAD + rows] = phi_ref[:, here] - slope_ref[:, here] * grad[
            PAD : PAD + rows
        ]
        for inside, edge, to in ((top_in, 0, 0), (low_in, PAD, PAD + rows)):
            phi = halo_ref[edge : edge + PAD, here]
            mask = jnp.tanh(phi)
            slope = (step_size * scale) * (1.0 - mask * mask)
            level_ref[b, to : to + PAD] = jnp.where(
                inside, phi - slope * grad[to : to + PAD], 0.0
            )

    for b in range(half // LANES):
        part = slice(b * LANES, (b + 1) * LANES)
        advance(b, even[:, part] - odd[:, part])
        advance(blocks - 1 - b, mirrored(even[:, part] + odd[:, part]))

    lane = lax.broadcasted_iota(jnp.int32, (8, LANES), 1)

    def sweep(source, first_row, store):
        center, rise, turned = [], [], []
        nothing = jnp.zeros((8, LANES), f32)
        for b in range(blocks):
            c = source[b, first_row : first_row + 8]
            u = source[b, first_row + 1 : first_row + 9]
            d = source[b, first_row - 1 : first_row + 7]
            x = u - d
            center.append(c)
            rise.append((x, (u + d) - 2.0 * c))
            turned.append(
                (
                    pltpu.roll(c, LANES - 1, 1),
                    pltpu.roll(c, 1, 1),
                    pltpu.roll(x, LANES - 1, 1),
                    pltpu.roll(x, 1, 1),
                )
            )
        for b in range(blocks):
            after = turned[b + 1] if b + 1 < blocks else (nothing,) * 4
            before = turned[b - 1] if b else (nothing,) * 4
            right = jnp.where(lane == LANES - 1, after[0], turned[b][0])
            left = jnp.where(lane == 0, before[1], turned[b][1])
            x_right = jnp.where(lane == LANES - 1, after[2], turned[b][2])
            x_left = jnp.where(lane == 0, before[3], turned[b][3])
            c = center[b]
            x, second_x = rise[b]
            y = right - left
            second_y = (right + left) - 2.0 * c
            x_x = x * x
            y_y = y * y
            numer = second_x * y_y + second_y * x_x - (0.5 * x) * y * (x_right - x_left)
            store(b, c + flow_rate * (numer / (4.0 + x_x + y_y)))

    starts = list(range(PAD - 1, PAD + rows - 7, 8))
    if starts[-1] + 8 < PAD + rows + 1:
        starts.append(PAD + rows - 7)
    for at in starts:
        spot = lax.broadcasted_iota(jnp.int32, (8, LANES), 0) + at
        keep = ((spot >= PAD) | top_in) & ((spot < PAD + rows) | low_in)
        edge = at < PAD or at + 8 > PAD + rows

        def store_next(b, value):
            next_ref[b, at : at + 8] = jnp.where(keep, value, 0.0) if edge else value

        sweep(level_ref, at, store_next)

    copies = []
    for index in range(rows // 8):

        def store_out(b, value):
            out_ref[8 * index : 8 * index + 8, b * LANES : (b + 1) * LANES] = value

        sweep(next_ref, PAD + 8 * index, store_out)
        here = pl.ds(8 * index, 8)
        copies.append(pltpu.make_async_copy(out_ref.at[here], out_hbm.at[here], sems.at[index]))
        copies[-1].start()
    for copy in copies:
        copy.wait()


def spec(kind):
    return pl.BlockSpec(memory_space={"v": pltpu.VMEM, "s": pltpu.SMEM, "h": pltpu.HBM}[kind])


def call(kernel, outs, args, kinds=None, out_kinds=None, scratch=(), limit=24, flops=1000000):
    kinds = kinds or "v" * len(args)
    out_kinds = out_kinds or "v" * len(outs)
    args = [
        pltpu.with_memory_space_constraint(arg, pltpu.HBM) if kind == "h" else arg
        for kind, arg in zip(kinds, args)
    ]
    return pl.pallas_call(
        kernel,
        out_shape=outs,
        in_specs=[spec(kind) for kind in kinds],
        out_specs=[spec(kind) for kind in out_kinds],
        scratch_shapes=list(scratch),
        compiler_params=pltpu.CompilerParams(vmem_limit_bytes=limit << 20),
        cost_estimate=pl.CostEstimate(flops=flops, bytes_accessed=4 << 20, transcendentals=0),
    )(*args)


def pair_up(block, first):
    count = lax.axis_size("strip")
    low = range(0 if first else 1, count, 2)
    pairs = [(i, (i + 1) % count) for i in low]
    return lax.ppermute(block, "strip", pairs + [(b, a) for a, b in pairs])


def on_device(phi, target, defocus_ids, kernels, psi, row_freqs, col_freqs):
    rows, cols = phi.shape
    half = cols // 2
    fr, fc = psi.shape
    count = kernels.shape[1]
    strips = lax.axis_size("strip")
    planes = lax.axis_size("focus")
    groups = offset_groups(rows, strips)
    tall = rows + 2 * PAD
    bf = jnp.bfloat16
    f32 = jnp.float32
    shape = jax.ShapeDtypeStruct
    packet = shape((2 * fr + HALO * (cols // fc), fc), bf)
    row_freqs = row_freqs.reshape(1, fr)

    table, s_own, send_a, send_b, phi, freqs = call(
        functools.partial(first_kernel, strips),
        [
            shape((fc, cols), bf),
            shape((2 * fr, fc), f32),
            packet,
            packet,
            shape((rows, cols), f32),
            shape((8, LANES), f32),
        ],
        (phi, row_freqs, col_freqs.reshape(1, fc)),
        kinds="hhh",
        scratch=[
            pltpu.VMEM((rows, cols), bf),
            pltpu.VMEM((2 * rows, fc), bf),
            pltpu.VMEM((1, fr), jnp.int32),
            pltpu.VMEM((1, fc), jnp.int32),
            pltpu.SemaphoreType.DMA((3,)),
        ],
    )
    from_b = pair_up(send_b, False)
    from_a = pair_up(send_a, True)
    inner, inner_t, tall_t, far_t, k_re, k_im, goal, slope = call(
        functools.partial(second_kernel, strips, groups),
        [
            shape((2 * fr, 2 * rows), bf),
            shape((2 * rows, 2 * fr), bf),
            shape((3, 2 * tall, 2 * fr), bf),
            shape((max(1, len(groups)), 4 * PAD, 2 * fr), bf),
            shape((count, fr, fc), f32),
            shape((count, fr, fc), f32),
            shape((rows, cols), f32),
            shape((rows, cols), f32),
        ],
        (defocus_ids, freqs, phi, kernels, psi, target),
        kinds="svvhhh",
        scratch=[
            pltpu.VMEM(kernels.shape, f32),
            pltpu.VMEM(psi.shape, f32),
            pltpu.VMEM(target.shape, jnp.int32),
            pltpu.SemaphoreType.DMA((3,)),
        ],
        flops=4000000000,
    )
    (part,) = call(
        main_kernel,
        [shape((2 * fr, fc), bf)],
        (s_own, from_a, from_b, goal, table, inner, inner_t, k_re, k_im),
        scratch=[
            pltpu.VMEM((count * 2 * rows, fc), bf),
            pltpu.VMEM((count * 2 * rows, cols), bf),
        ],
        flops=4000000000,
    )
    step = 1
    other = jnp.zeros_like(part)
    while step < planes:
        if step > 1:
            part = lax.optimization_barrier(
                (part.astype(f32) + other.astype(f32)).astype(bf)
            )
        other = lax.ppermute(part, "focus", [(i, i ^ step) for i in range(planes)])
        step *= 2
    total, *payloads = call(
        sum_kernel,
        [shape((2 * fr, fc), bf)] + [shape((4 * PAD, fc), bf)] * len(groups),
        (part, other, far_t),
    )
    far = [
        lax.ppermute(payload, "strip", [(i, (i - turn_by) % strips) for i in range(strips)])
        for turn_by, payload in zip(groups, payloads)
    ]
    y_b = pair_up(total, False)
    y_a = pair_up(total, True)
    return call(
        functools.partial(final_kernel, strips),
        [shape((rows, cols), f32)],
        (phi, slope, from_a, from_b, table, tall_t, total, y_a, y_b, *far),
        out_kinds="h",
        scratch=[
            pltpu.VMEM((cols // LANES, tall, LANES), f32),
            pltpu.VMEM((cols // LANES, tall, LANES), f32),
            pltpu.VMEM((2 * PAD, cols), f32),
            pltpu.VMEM((rows, cols), f32),
            pltpu.SemaphoreType.DMA((rows // 8,)),
        ],
    )[0]


def solution(mesh):
    return jax.shard_map(
        on_device,
        mesh=mesh,
        in_specs=(
            P(("tile", "strip"), None),
            P(("tile", "strip"), None),
            P(("tile", "focus")),
            P(),
            P(),
            P(),
            P(),
        ),
        out_specs=P(("tile", "strip"), None),
        check_vma=False,
    )
```

```python
import functools

import jax
import jax.numpy as jnp
from jax import lax
from jax.experimental import pallas as pl
from jax.experimental.pallas import tpu as pltpu
from jax.sharding import PartitionSpec as P

MARGIN = 64
LEVELS = 31
SWEEPS = 2
HALO = SWEEPS
LANES = 128
PAD = 8
CHUNK = 256

slope_resist = 4.0
level_resist = 0.5
step_size = 1.0
flow_rate = 0.2

SIN_TERMS = (1.0, -1.0 / 6, 1.0 / 120, -1.0 / 5040, 1.0 / 362880, -1.0 / 39916800)
COS_TERMS = (1.0, -0.5, 1.0 / 24, -1.0 / 720, 1.0 / 40320, -1.0 / 3628800, 1.0 / 479001600)


def cos_sin(angle):
    half = 0.5 * angle
    square = half * half
    s = jnp.full_like(half, SIN_TERMS[-1])
    for term in SIN_TERMS[-2::-1]:
        s = s * square + term
    s = s * half
    c = jnp.full_like(half, COS_TERMS[-1])
    for term in COS_TERMS[-2::-1]:
        c = c * square + term
    return 1.0 - 2.0 * s * s, 2.0 * s * c


def turn(product, period):
    rest = product - jnp.round(product * (1.0 / period)) * period
    return cos_sin(rest * (2.0 * jnp.pi / period))


def mirrored(block):
    spots = (LANES - 1) - lax.broadcasted_iota(jnp.int32, block.shape, 1)
    return jnp.take_along_axis(block, spots, axis=1, mode="promise_in_bounds")


def dot(lhs_mat, rhs_mat):
    return jnp.dot(lhs_mat, rhs_mat, preferred_element_type=jnp.float32)


def dot_t(lhs_mat, rhs_mat):
    return lax.dot_general(
        lhs_mat, rhs_mat, (((1,), (1,)), ((), ())), preferred_element_type=jnp.float32
    )


def offset_groups(rows, strips):
    reach = (MARGIN + HALO + rows - 1) // rows
    groups = {}
    for offset in range(-reach, reach + 1):
        if abs(offset) > 1:
            groups.setdefault(offset % strips, []).append(offset)
    return groups


def partners(strips):
    place = lax.axis_index("strip")
    first = jnp.where(place % 2 == 0, 1, -1)
    second = -first

    def inside(offset):
        return (place + offset >= 0) & (place + offset < strips)

    return place, first, second, inside(first), inside(second)


def quarter(second, imag, c, s):
    return jnp.where(second == imag, c, jnp.where(second, s, -s))


def rotation(freqs, shape, length, freq_dim, fr, start, period):
    spot = lax.broadcasted_iota(jnp.int32, shape, 1 - freq_dim)
    second = spot >= length
    spot = jnp.where(second, spot - length, spot) + start
    imag = lax.broadcasted_iota(jnp.int32, shape, freq_dim) >= fr
    c, s = turn(freqs * spot.astype(jnp.float32), float(period))
    return quarter(second, imag, c, s), spot


def interleaved(freqs, shape, freq_dim, fr, start, period):
    index = lax.broadcasted_iota(jnp.int32, shape, 1 - freq_dim)
    spot = ((index >> 4) << 3) + (index & 7) + start
    second = (index & 8) > 0
    imag = lax.broadcasted_iota(jnp.int32, shape, freq_dim) >= fr
    c, s = turn(freqs * spot.astype(jnp.float32), float(period))
    return quarter(second, imag, c, s)


def row_freq_lanes(row_freqs_ref, freq_ref):
    fr = row_freqs_ref.shape[1]
    freqs = jnp.broadcast_to(row_freqs_ref[...].astype(jnp.float32), (8, fr))
    freq_ref[...] = jnp.zeros_like(freq_ref)
    freq_ref[:, 0:fr] = freqs
    freq_ref[:, fr : 2 * fr] = freqs


def first_kernel(
    strips,
    phi_hbm,
    row_freqs_hbm,
    col_freqs_hbm,
    table_ref,
    own_ref,
    send_a_ref,
    send_b_ref,
    phi_ref,
    freq_ref,
    mask_ref,
    p_ref,
    row_freqs_ref,
    col_freqs_ref,
    sems,
):
    rows, cols = phi_ref.shape
    half = cols // 2
    fr, fc = row_freqs_ref.shape[1], table_ref.shape[0]
    window = rows + 2 * MARGIN
    bf = jnp.bfloat16
    load_cols = pltpu.make_async_copy(col_freqs_hbm, col_freqs_ref, sems.at[0])
    load_rows = pltpu.make_async_copy(row_freqs_hbm, row_freqs_ref, sems.at[1])
    load_phi = pltpu.make_async_copy(phi_hbm, phi_ref, sems.at[2])
    load_cols.start()
    load_rows.start()
    load_phi.start()
    _, first, second, first_in, second_in = partners(strips)

    load_cols.wait()
    freq_row = jnp.broadcast_to(col_freqs_ref[...].astype(jnp.float32), (8, fc))
    step_row_c, step_row_s = turn(freq_row * float(LANES), float(cols))
    freqs, steps_c, steps_s = freq_row.T[:, :1], step_row_c.T[:, :1], step_row_s.T[:, :1]

    def make_columns(start, number):
        f = freqs[start : start + number]
        spot = lax.broadcasted_iota(jnp.int32, (number, LANES), 1).astype(jnp.float32)
        c, s = turn(f * (2.0 * spot + 1.0), 2.0 * cols)
        step_c = jnp.broadcast_to(steps_c[start : start + number], (number, LANES))
        step_s = jnp.broadcast_to(steps_s[start : start + number], (number, LANES))
        twice = 2.0 * step_c
        c_old, s_old = c, s
        here = slice(start, start + number)
        for b in range(half // LANES):
            if b == 1:
                c, s = c * step_c - s * step_s, s * step_c + c * step_s
            elif b:
                c, s, c_old, s_old = twice * c - c_old, twice * s - s_old, c, s
            table_ref[here, b * LANES : (b + 1) * LANES] = c.astype(bf)
            table_ref[here, half + b * LANES : half + (b + 1) * LANES] = s.astype(bf)

    def transform(start, number):
        here = slice(start, start + number)
        p_ref[:rows, here] = dot_t(mask_ref[:, :half], table_ref[here, :half]).astype(bf)
        p_ref[rows:, here] = (-dot_t(mask_ref[:, half:], table_ref[here, half:])).astype(bf)

    group = fc // 2
    piece = 64
    for start in range(0, group, piece):
        make_columns(start, piece)
    load_rows.wait()
    load_phi.wait()
    for b in range(half // LANES):
        left = jnp.tanh(phi_ref[:, b * LANES : (b + 1) * LANES])
        right = mirrored(jnp.tanh(phi_ref[:, cols - (b + 1) * LANES : cols - b * LANES]))
        mask_ref[:, b * LANES : (b + 1) * LANES] = (left + right).astype(bf)
        mask_ref[:, half + b * LANES : half + (b + 1) * LANES] = (left - right).astype(bf)
    transform(0, group)
    for start in range(group, fc, piece):
        make_columns(start, piece)
    transform(group, fc - group)

    row_freq_lanes(row_freqs_ref, freq_ref)
    down = freq_ref[...].T[:fr, :1]
    spot = lax.broadcasted_iota(jnp.int32, (fr, 2 * rows), 1)
    later = spot >= rows
    spot = jnp.where(later, spot - rows, spot)
    c, s = turn(down * (spot + MARGIN).astype(jnp.float32), float(window))
    turn_c, turn_s = turn(down * float(rows), float(window))
    turn_c = jnp.broadcast_to(turn_c, c.shape)
    turn_s = jnp.broadcast_to(turn_s, c.shape)

    def rows_in(c, s, offset, keep):
        at = spot + MARGIN - offset * rows
        keep = keep & (at >= 0) & (at < window)
        c = jnp.where(keep, c, 0.0)
        s = jnp.where(keep, s, 0.0)
        return jnp.concatenate([jnp.where(later, s, c), jnp.where(later, c, -s)], axis=0).astype(bf)

    in_own = rows_in(c, s, 0, True)
    sign = -first.astype(jnp.float32)
    in_a = rows_in(c * turn_c - s * (sign * turn_s), s * turn_c + c * (sign * turn_s), first, first_in)
    in_b = rows_in(
        c * turn_c + s * (sign * turn_s), s * turn_c - c * (sign * turn_s), second, second_in
    )

    p = p_ref[...]
    send_b_ref[: 2 * fr] = dot(in_b, p).astype(bf)
    send_a_ref[: 2 * fr] = dot(in_a, p).astype(bf)
    own_ref[...] = dot(in_own, p)
    tops = [phi_ref[i : i + 1, q : q + fc] for i in range(HALO) for q in range(0, cols, fc)]
    lows = [
        phi_ref[rows - HALO + i : rows - HALO + i + 1, q : q + fc]
        for i in range(HALO)
        for q in range(0, cols, fc)
    ]
    tops = jnp.concatenate(tops, axis=0)
    lows = jnp.concatenate(lows, axis=0)
    send_a_ref[2 * fr :] = jnp.where(first > 0, lows, tops).astype(bf)
    send_b_ref[2 * fr :] = jnp.where(second > 0, lows, tops).astype(bf)


def second_kernel(
    strips,
    groups,
    defocus_ref,
    freq_ref,
    phi_ref,
    kernels_hbm,
    psi_hbm,
    target_hbm,
    inner_ref,
    inner_t_ref,
    tall_ref,
    far_ref,
    k_re_ref,
    k_im_ref,
    goal_ref,
    slope_ref,
    kernels_ref,
    psi_ref,
    target_ref,
    sems,
):
    rows, cols = phi_ref.shape
    half = cols // 2
    fr = psi_ref.shape[0]
    load_psi = pltpu.make_async_copy(psi_hbm, psi_ref, sems.at[0])
    load_kernels = pltpu.make_async_copy(kernels_hbm, kernels_ref, sems.at[1])
    load_target = pltpu.make_async_copy(target_hbm, target_ref, sems.at[2])
    load_psi.start()
    load_kernels.start()
    load_target.start()
    window = rows + 2 * MARGIN
    bf = jnp.bfloat16
    place, first, second, first_in, second_in = partners(strips)
    across = freq_ref[0:1, :]
    down = freq_ref[...].T[: 2 * fr, :1]

    inner_ref[...] = interleaved(down, (2 * fr, 2 * rows), 0, fr, MARGIN, window).astype(bf)
    table = interleaved(across, (2 * rows, LANES), 1, fr, MARGIN, window)
    inner_t_ref[...] = table[:, : 2 * fr].astype(bf)

    def rows_from(offset, keep, first_row, number):
        table, spot = rotation(
            across, (2 * number, LANES), number, 1, fr, first_row - offset * rows + MARGIN, window
        )
        keep = keep & (spot >= 0) & (spot < window)
        return jnp.where(keep, table, 0.0)

    tall = rows + 2 * PAD
    for index, (offset, keep) in enumerate(((0, True), (first, first_in), (second, second_in))):
        tall_ref[index] = rows_from(offset, keep, -PAD, tall)[:, : 2 * fr].astype(bf)
    shape = (4 * HALO, LANES)
    index = lax.broadcasted_iota(jnp.int32, shape, 0)
    imag_row = index >= 2 * HALO
    index = jnp.where(imag_row, index - 2 * HALO, index)
    low = index >= HALO
    row = jnp.where(low, index + (rows - HALO), index - HALO)
    imag = lax.broadcasted_iota(jnp.int32, shape, 1) >= fr
    for group, offsets in enumerate(groups.values()):
        total = jnp.zeros(shape, jnp.float32)
        for offset in offsets:
            spot = row - offset * rows + MARGIN
            keep = (spot >= 0) & (spot < window) & (low if offset > 0 else ~low)
            keep = keep & (place - offset >= 0) & (place - offset < strips)
            c, s = turn(across * spot.astype(jnp.float32), float(window))
            total = total + jnp.where(keep, quarter(imag_row, imag, c, s), 0.0)
        far_ref[group] = total[:, : 2 * fr].astype(bf)

    scale = 1.0 / float(window * cols) ** 0.5
    mask = jnp.tanh(phi_ref[...])
    slope_ref[...] = (step_size * scale) * (1.0 - mask * mask)

    load_psi.wait()
    load_kernels.wait()
    middle = (LEVELS - 1) / 2.0
    defocus = (defocus_ref[0].astype(jnp.float32) - middle) * (1.0 / middle)
    turn_c, turn_s = cos_sin(psi_ref[...] * defocus)
    for k in range(kernels_ref.shape[1]):
        k_re_ref[k] = kernels_ref[0, k] * turn_c - kernels_ref[1, k] * turn_s
        k_im_ref[k] = kernels_ref[0, k] * turn_s + kernels_ref[1, k] * turn_c

    load_target.wait()
    goal_ref[:, :half] = target_ref[:, :half].astype(jnp.float32)
    for b in range(half // LANES):
        goal_ref[:, half + b * LANES : half + (b + 1) * LANES] = mirrored(
            target_ref[:, cols - (b + 1) * LANES : cols - b * LANES].astype(jnp.float32)
        )


def main_kernel(
    own_ref,
    from_a_ref,
    from_b_ref,
    goal_ref,
    table_ref,
    inner_ref,
    inner_t_ref,
    k_re_ref,
    k_im_ref,
    out_ref,
    q_ref,
    x_ref,
):
    rows, cols = goal_ref.shape
    half = cols // 2
    count, fr, _ = k_re_ref.shape
    scale = 1.0 / float((rows + 2 * MARGIN) * cols) ** 0.5
    bf = jnp.bfloat16
    f32 = jnp.float32

    spec = scale * (
        own_ref[...] + from_a_ref[: 2 * fr].astype(f32) + from_b_ref[: 2 * fr].astype(f32)
    )
    s_re, s_im = spec[:fr], spec[fr:]
    unit = 16 * count
    for k in range(count):
        k_re, k_im = k_re_ref[k], k_im_ref[k]
        g = jnp.concatenate([k_re * s_re - k_im * s_im, k_re * s_im + k_im * s_re], axis=0)
        q = dot(inner_t_ref[...], g.astype(bf)).astype(bf)
        for r in range(rows // 8):
            q_ref[r * unit + 16 * k : r * unit + 16 * k + 16] = q[16 * r : 16 * r + 16]

    gain = 4.0 * slope_resist / count * scale
    norm = scale * scale / count

    def weight(intensity, goal):
        resist = jax.nn.sigmoid(slope_resist * (norm * intensity - level_resist))
        return gain * (resist - goal) * resist * (1.0 - resist)

    width = min(CHUNK, half)
    for start in range(0, half, width):
        left_half = slice(start, start + width)
        right_half = slice(half + start, half + start + width)
        af = dot(q_ref[...], table_ref[:, left_half])
        db = dot(q_ref[...], table_ref[:, right_half])
        for r in range(rows // 8):

            def parts(k):
                at = r * unit + 16 * k
                return af[at : at + 8], db[at + 8 : at + 16], af[at + 8 : at + 16], db[at : at + 8]

            even = 0.0
            cross = 0.0
            for k in range(count):
                a, b, f, d = parts(k)
                even = even + ((a * a + f * f) + (d * d + b * b))
                cross = cross + (a * b - d * f)
            cross = 2.0 * cross
            here = slice(8 * r, 8 * r + 8)
            w_left = weight(even - cross, goal_ref[here, left_half])
            w_right = weight(even + cross, goal_ref[here, right_half])
            p_w = w_left + w_right
            q_w = w_right - w_left
            for k in range(count):
                a, b, f, d = parts(k)
                at = slice(r * unit + 16 * k, r * unit + 16 * k + 16)
                x_ref[at, left_half] = jnp.concatenate(
                    [p_w * a + q_w * b, p_w * f - q_w * d], axis=0
                ).astype(bf)
                x_ref[at, right_half] = jnp.concatenate(
                    [p_w * d - q_w * f, q_w * a + p_w * b], axis=0
                ).astype(bf)

    q_ref[...] = dot_t(x_ref[...], table_ref[...]).astype(bf)
    y_re = 0.0
    y_im = 0.0
    for k in range(count):
        u = jnp.concatenate(
            [q_ref[r * unit + 16 * k : r * unit + 16 * k + 16] for r in range(rows // 8)], axis=0
        )
        w = scale * dot(inner_ref[...], u)
        w_re, w_im = w[:fr], w[fr:]
        k_re, k_im = k_re_ref[k], k_im_ref[k]
        y_re = y_re + (k_re * w_re + k_im * w_im)
        y_im = y_im + (k_re * w_im - k_im * w_re)
    out_ref[:fr] = y_re.astype(bf)
    out_ref[fr:] = y_im.astype(bf)


def sum_kernel(part_ref, other_ref, far_ref, total_ref, *payload_refs):
    total = part_ref[...].astype(jnp.float32) + other_ref[...].astype(jnp.float32)
    total = total.astype(jnp.bfloat16)
    total_ref[...] = total
    for index, payload_ref in enumerate(payload_refs):
        payload_ref[...] = dot(far_ref[index], total).astype(jnp.bfloat16)


def final_kernel(
    strips,
    phi_ref,
    slope_ref,
    from_a_ref,
    from_b_ref,
    table_ref,
    tall_ref,
    y_own_ref,
    y_a_ref,
    y_b_ref,
    *rest,
):
    payload_refs = rest[:-10]
    out_hbm, halo_ref, out_ref, sems = rest[-10:-6]
    level_ref, level_across, level_both, next_ref, next_across, next_both = rest[-6:]
    place, first, _, _, _ = partners(strips)
    rows, cols = phi_ref.shape
    half = cols // 2
    blocks = cols // LANES
    tall = rows + 2 * PAD
    fc = y_own_ref.shape[1]
    lead = y_own_ref.shape[0]
    bf = jnp.bfloat16
    f32 = jnp.float32
    scale = 1.0 / float((rows + 2 * MARGIN) * cols) ** 0.5

    z = dot(tall_ref[0], y_own_ref[...])
    z = z + dot(tall_ref[1], y_a_ref[...]) + dot(tall_ref[2], y_b_ref[...])
    if payload_refs:
        down = lax.broadcasted_iota(jnp.int32, (2 * tall, 4 * HALO), 0)
        index = lax.broadcasted_iota(jnp.int32, (2 * tall, 4 * HALO), 1)
        imag = index >= 2 * HALO
        index = jnp.where(imag, index - 2 * HALO, index)
        goes = jnp.where(index < HALO, index + (PAD - HALO), index + (PAD + rows - HALO))
        goes = jnp.where(imag, goes + tall, goes)
        place_rows = jnp.where(down == goes, 1.0, 0.0).astype(bf)
        for payload_ref in payload_refs:
            z = z + dot(place_rows, payload_ref[...])
    z = z.astype(bf)
    even = dot(z[:tall], table_ref[:, :half])
    odd = dot(z[tall:], table_ref[:, half:])

    halo_ref[...] = jnp.zeros_like(halo_ref)
    edges_a = from_a_ref[lead:].astype(f32)
    edges_b = from_b_ref[lead:].astype(f32)
    above = jnp.where(first < 0, edges_a, edges_b)
    below = jnp.where(first < 0, edges_b, edges_a)
    per_row = cols // fc
    for i in range(HALO):
        for q in range(per_row):
            here = slice(q * fc, (q + 1) * fc)
            spot = i * per_row + q
            halo_ref[PAD - HALO + i : PAD - HALO + i + 1, here] = above[spot : spot + 1]
            halo_ref[PAD + i : PAD + i + 1, here] = below[spot : spot + 1]
    top_in = place > 0
    low_in = place < strips - 1

    def advance(b, grad):
        here = slice(b * LANES, (b + 1) * LANES)
        level_ref[b, PAD : PAD + rows] = phi_ref[:, here] - slope_ref[:, here] * grad[
            PAD : PAD + rows
        ]
        for inside, edge, to in ((top_in, 0, 0), (low_in, PAD, PAD + rows)):
            phi = halo_ref[edge : edge + PAD, here]
            mask = jnp.tanh(phi)
            slope = (step_size * scale) * (1.0 - mask * mask)
            level_ref[b, to : to + PAD] = jnp.where(
                inside, phi - slope * grad[to : to + PAD], 0.0
            )

    for b in range(half // LANES):
        part = slice(b * LANES, (b + 1) * LANES)
        advance(b, even[:, part] - odd[:, part])
        advance(blocks - 1 - b, mirrored(even[:, part] + odd[:, part]))

    lane = lax.broadcasted_iota(jnp.int32, (8, LANES), 1)
    nothing = jnp.zeros((8, LANES), f32)

    def beside(values):
        ahead = [pltpu.roll(value, LANES - 1, 1) for value in values] + [nothing]
        behind = [nothing] + [pltpu.roll(value, 1, 1) for value in values]
        for b in range(len(values)):
            right = jnp.where(lane == LANES - 1, ahead[b + 1], ahead[b])
            left = jnp.where(lane == 0, behind[b], behind[b + 1])
            yield right - left, right + left

    def sweep(refs, at, b):
        source, across_ref, both_ref = refs
        here = slice(at, at + 8)
        c = source[b, here]
        up, down = source[b, at + 1 : at + 9], source[b, at - 1 : at + 7]
        y = across_ref[b, here]
        crossed = across_ref[b, at + 1 : at + 9] - across_ref[b, at - 1 : at + 7]
        twice = c + c
        x = up - down
        second_x = (up + down) - twice
        second_y = both_ref[b, here] - twice
        x_x = x * x
        y_y = y * y
        numer = second_x * y_y + second_y * x_x - (0.5 * x) * y * crossed
        return c + flow_rate * (numer / (4.0 + x_x + y_y))

    levels = (level_ref, level_across, level_both)
    nexts = (next_ref, next_across, next_both)

    def fill(refs, at, values):
        for b, (difference, total) in enumerate(beside(values)):
            refs[1][b, at : at + 8] = difference
            refs[2][b, at : at + 8] = total

    for at in range(0, tall, 8):
        fill(levels, at, [level_ref[b, at : at + 8] for b in range(blocks)])
    starts = list(range(PAD - 1, PAD + rows - 7, 8))
    if starts[-1] + 8 < PAD + rows + 1:
        starts.append(PAD + rows - 7)
    for at in starts:
        values = [sweep(levels, at, b) for b in range(blocks)]
        if at < PAD or at + 8 > PAD + rows:
            spot = lax.broadcasted_iota(jnp.int32, (8, LANES), 0) + at
            keep = ((spot >= PAD) | top_in) & ((spot < PAD + rows) | low_in)
            values = [jnp.where(keep, value, 0.0) for value in values]
        for b in range(blocks):
            next_ref[b, at : at + 8] = values[b]
        fill(nexts, at, values)
    copies = []
    for index in range(rows // 8):
        here = slice(8 * index, 8 * index + 8)
        for b in range(blocks):
            out_ref[here, b * LANES : (b + 1) * LANES] = sweep(nexts, PAD + 8 * index, b)
        here = pl.ds(8 * index, 8)
        copies.append(pltpu.make_async_copy(out_ref.at[here], out_hbm.at[here], sems.at[index]))
        copies[-1].start()
    for copy in copies:
        copy.wait()


def spec(kind):
    return pl.BlockSpec(memory_space={"v": pltpu.VMEM, "s": pltpu.SMEM, "h": pltpu.HBM}[kind])


def call(kernel, outs, args, kinds=None, out_kinds=None, scratch=(), limit=24, flops=1000000):
    kinds = kinds or "v" * len(args)
    out_kinds = out_kinds or "v" * len(outs)
    args = [
        pltpu.with_memory_space_constraint(arg, pltpu.HBM) if kind == "h" else arg
        for kind, arg in zip(kinds, args)
    ]
    return pl.pallas_call(
        kernel,
        out_shape=outs,
        in_specs=[spec(kind) for kind in kinds],
        out_specs=[spec(kind) for kind in out_kinds],
        scratch_shapes=list(scratch),
        compiler_params=pltpu.CompilerParams(vmem_limit_bytes=limit << 20),
        cost_estimate=pl.CostEstimate(flops=flops, bytes_accessed=4 << 20, transcendentals=0),
    )(*args)


def pair_up(block, first):
    count = lax.axis_size("strip")
    low = range(0 if first else 1, count, 2)
    pairs = [(i, (i + 1) % count) for i in low]
    return lax.ppermute(block, "strip", pairs + [(b, a) for a, b in pairs])


def on_device(phi, target, defocus_ids, kernels, psi, row_freqs, col_freqs):
    rows, cols = phi.shape
    fr, fc = psi.shape
    count = kernels.shape[1]
    strips = lax.axis_size("strip")
    planes = lax.axis_size("focus")
    groups = offset_groups(rows, strips)
    tall = rows + 2 * PAD
    bf = jnp.bfloat16
    f32 = jnp.float32
    shape = jax.ShapeDtypeStruct
    packet = shape((2 * fr + HALO * (cols // fc), fc), bf)
    row_freqs = row_freqs.reshape(1, fr)

    table, s_own, send_a, send_b, phi, freqs = call(
        functools.partial(first_kernel, strips),
        [
            shape((fc, cols), bf),
            shape((2 * fr, fc), f32),
            packet,
            packet,
            shape((rows, cols), f32),
            shape((8, LANES), f32),
        ],
        (phi, row_freqs, col_freqs.reshape(1, fc)),
        kinds="hhh",
        scratch=[
            pltpu.VMEM((rows, cols), bf),
            pltpu.VMEM((2 * rows, fc), bf),
            pltpu.VMEM((1, fr), jnp.int32),
            pltpu.VMEM((1, fc), jnp.int32),
            pltpu.SemaphoreType.DMA((3,)),
        ],
    )
    from_b = pair_up(send_b, False)
    from_a = pair_up(send_a, True)
    inner, inner_t, tall_t, far_t, k_re, k_im, goal, slope = call(
        functools.partial(second_kernel, strips, groups),
        [
            shape((2 * fr, 2 * rows), bf),
            shape((2 * rows, 2 * fr), bf),
            shape((3, 2 * tall, 2 * fr), bf),
            shape((max(1, len(groups)), 4 * HALO, 2 * fr), bf),
            shape((count, fr, fc), f32),
            shape((count, fr, fc), f32),
            shape((rows, cols), f32),
            shape((rows, cols), f32),
        ],
        (defocus_ids, freqs, phi, kernels, psi, target),
        kinds="svvhhh",
        scratch=[
            pltpu.VMEM(kernels.shape, f32),
            pltpu.VMEM(psi.shape, f32),
            pltpu.VMEM(target.shape, jnp.int32),
            pltpu.SemaphoreType.DMA((3,)),
        ],
        flops=4000000000,
    )
    (part,) = call(
        main_kernel,
        [shape((2 * fr, fc), bf)],
        (s_own, from_a, from_b, goal, table, inner, inner_t, k_re, k_im),
        scratch=[
            pltpu.VMEM((count * 2 * rows, fc), bf),
            pltpu.VMEM((count * 2 * rows, cols), bf),
        ],
        flops=4000000000,
    )
    step = 1
    other = jnp.zeros_like(part)
    while step < planes:
        if step > 1:
            part = lax.optimization_barrier(
                (part.astype(f32) + other.astype(f32)).astype(bf)
            )
        other = lax.ppermute(part, "focus", [(i, i ^ step) for i in range(planes)])
        step *= 2
    total, *payloads = call(
        sum_kernel,
        [shape((2 * fr, fc), bf)] + [shape((4 * HALO, fc), bf)] * len(groups),
        (part, other, far_t),
    )
    far = [
        lax.ppermute(payload, "strip", [(i, (i - turn_by) % strips) for i in range(strips)])
        for turn_by, payload in zip(groups, payloads)
    ]
    y_b = pair_up(total, False)
    y_a = pair_up(total, True)
    return call(
        functools.partial(final_kernel, strips),
        [shape((rows, cols), f32)],
        (phi, slope, from_a, from_b, table, tall_t, total, y_a, y_b, *far),
        out_kinds="h",
        scratch=[
            pltpu.VMEM((2 * PAD, cols), f32),
            pltpu.VMEM((rows, cols), f32),
            pltpu.SemaphoreType.DMA((rows // 8,)),
        ]
        + [pltpu.VMEM((cols // LANES, tall, LANES), f32)] * 6,
    )[0]


def solution(mesh):
    return jax.shard_map(
        on_device,
        mesh=mesh,
        in_specs=(
            P(("tile", "strip"), None),
            P(("tile", "strip"), None),
            P(("tile", "focus")),
            P(),
            P(),
            P(),
            P(),
        ),
        out_specs=P(("tile", "strip"), None),
        check_vma=False,
    )
```

```python
import functools

import jax
import jax.numpy as jnp
from jax import lax
from jax.experimental import pallas as pl
from jax.experimental.pallas import tpu as pltpu
from jax.sharding import PartitionSpec as P

MARGIN = 64
LEVELS = 31
SWEEPS = 2
HALO = SWEEPS
LANES = 128
PAD = 8
CHUNK = 256
GROUP = 256

slope_resist = 4.0
level_resist = 0.5
step_size = 1.0
flow_rate = 0.2

SIN_TERMS = (1.0, -1.0 / 6, 1.0 / 120, -1.0 / 5040, 1.0 / 362880, -1.0 / 39916800)
COS_TERMS = (1.0, -0.5, 1.0 / 24, -1.0 / 720, 1.0 / 40320, -1.0 / 3628800, 1.0 / 479001600)


def cos_sin(angle):
    half = 0.5 * angle
    square = half * half
    s = jnp.full_like(half, SIN_TERMS[-1])
    for term in SIN_TERMS[-2::-1]:
        s = s * square + term
    s = s * half
    c = jnp.full_like(half, COS_TERMS[-1])
    for term in COS_TERMS[-2::-1]:
        c = c * square + term
    return 1.0 - 2.0 * s * s, 2.0 * s * c


def turn(product, period):
    rest = product - jnp.round(product * (1.0 / period)) * period
    return cos_sin(rest * (2.0 * jnp.pi / period))


def mirrored(block):
    spots = (LANES - 1) - lax.broadcasted_iota(jnp.int32, block.shape, 1)
    return jnp.take_along_axis(block, spots, axis=1, mode="promise_in_bounds")


def dot(lhs_mat, rhs_mat):
    return jnp.dot(lhs_mat, rhs_mat, preferred_element_type=jnp.float32)


def dot_t(lhs_mat, rhs_mat):
    return lax.dot_general(
        lhs_mat, rhs_mat, (((1,), (1,)), ((), ())), preferred_element_type=jnp.float32
    )


def offset_groups(rows, strips):
    reach = (MARGIN + HALO + rows - 1) // rows
    groups = {}
    for offset in range(-reach, reach + 1):
        if abs(offset) > 1:
            groups.setdefault(offset % strips, []).append(offset)
    return groups


def partners(strips):
    place = lax.axis_index("strip")
    first = jnp.where(place % 2 == 0, 1, -1)
    second = -first

    def inside(offset):
        return (place + offset >= 0) & (place + offset < strips)

    return place, first, second, inside(first), inside(second)


def quarter(second, imag, c, s):
    return jnp.where(second == imag, c, jnp.where(second, s, -s))


def rotation(freqs, shape, length, freq_dim, fr, start, period):
    spot = lax.broadcasted_iota(jnp.int32, shape, 1 - freq_dim)
    second = spot >= length
    spot = jnp.where(second, spot - length, spot) + start
    imag = lax.broadcasted_iota(jnp.int32, shape, freq_dim) >= fr
    c, s = turn(freqs * spot.astype(jnp.float32), float(period))
    return quarter(second, imag, c, s), spot


def interleaved(freqs, shape, freq_dim, fr, start, period):
    index = lax.broadcasted_iota(jnp.int32, shape, 1 - freq_dim)
    spot = ((index >> 4) << 3) + (index & 7) + start
    second = (index & 8) > 0
    imag = lax.broadcasted_iota(jnp.int32, shape, freq_dim) >= fr
    c, s = turn(freqs * spot.astype(jnp.float32), float(period))
    return quarter(second, imag, c, s)


def row_freq_lanes(row_freqs_ref, freq_ref):
    fr = row_freqs_ref.shape[1]
    freqs = jnp.broadcast_to(row_freqs_ref[...].astype(jnp.float32), (8, fr))
    freq_ref[...] = jnp.zeros_like(freq_ref)
    freq_ref[:, 0:fr] = freqs
    freq_ref[:, fr : 2 * fr] = freqs


def first_kernel(
    strips,
    phi_hbm,
    row_freqs_hbm,
    col_freqs_hbm,
    table_ref,
    own_ref,
    send_a_ref,
    send_b_ref,
    phi_ref,
    freq_ref,
    mask_ref,
    row_freqs_ref,
    col_freqs_ref,
    sems,
):
    rows, cols = phi_ref.shape
    half = cols // 2
    fr, fc = row_freqs_ref.shape[1], table_ref.shape[0]
    window = rows + 2 * MARGIN
    bf = jnp.bfloat16
    load_cols = pltpu.make_async_copy(col_freqs_hbm, col_freqs_ref, sems.at[0])
    load_rows = pltpu.make_async_copy(row_freqs_hbm, row_freqs_ref, sems.at[1])
    load_phi = pltpu.make_async_copy(phi_hbm, phi_ref, sems.at[2])
    load_cols.start()
    load_rows.start()
    load_phi.start()
    _, first, second, first_in, second_in = partners(strips)

    load_cols.wait()
    load_rows.wait()
    row_freq_lanes(row_freqs_ref, freq_ref)
    down = freq_ref[...].T[:fr, :1]
    spot = lax.broadcasted_iota(jnp.int32, (fr, 2 * rows), 1)
    later = spot >= rows
    spot = jnp.where(later, spot - rows, spot)
    c, s = turn(down * (spot + MARGIN).astype(jnp.float32), float(window))
    turn_c, turn_s = turn(jnp.broadcast_to(down, c.shape) * float(rows), float(window))

    def rows_in(c, s, offset, keep):
        at = spot + MARGIN - offset * rows
        keep = keep & (at >= 0) & (at < window)
        c = jnp.where(keep, c, 0.0)
        s = jnp.where(keep, s, 0.0)
        return jnp.concatenate([jnp.where(later, s, c), jnp.where(later, c, -s)], axis=0).astype(bf)

    sign = -first.astype(jnp.float32)
    turn_s = sign * turn_s
    in_all = jnp.concatenate(
        [
            rows_in(c * turn_c + s * turn_s, s * turn_c - c * turn_s, second, second_in),
            rows_in(c * turn_c - s * turn_s, s * turn_c + c * turn_s, first, first_in),
            rows_in(c, s, 0, True),
        ],
        axis=0,
    )

    freq_row = jnp.broadcast_to(col_freqs_ref[...].astype(jnp.float32), (8, fc))
    step_row_c, step_row_s = turn(freq_row * float(LANES), float(cols))
    kind = lax.broadcasted_iota(jnp.int32, (8, fc), 0)
    packed = jnp.where(kind == 0, freq_row, jnp.where(kind == 1, step_row_c, step_row_s)).T

    def make_columns(start, number):
        f = packed[start : start + number, 0:1]
        spot = lax.broadcasted_iota(jnp.int32, (number, LANES), 1).astype(jnp.float32)
        c, s = turn(f * (2.0 * spot + 1.0), 2.0 * cols)
        step_c = jnp.broadcast_to(packed[start : start + number, 1:2], (number, LANES))
        step_s = jnp.broadcast_to(packed[start : start + number, 2:3], (number, LANES))
        twice = 2.0 * step_c
        c_old, s_old = c, s
        here = slice(start, start + number)
        for b in range(half // LANES):
            if b == 1:
                c, s = c * step_c - s * step_s, s * step_c + c * step_s
            elif b:
                c, s, c_old, s_old = twice * c - c_old, twice * s - s_old, c, s
            table_ref[here, b * LANES : (b + 1) * LANES] = c.astype(bf)
            table_ref[here, half + b * LANES : half + (b + 1) * LANES] = s.astype(bf)

    def transform(start, number):
        here = slice(start, start + number)
        p_re = dot_t(mask_ref[:, :half], table_ref[here, :half])
        p_im = -dot_t(mask_ref[:, half:], table_ref[here, half:])
        spec = dot(in_all, jnp.concatenate([p_re, p_im], axis=0).astype(bf))
        send_b_ref[: 2 * fr, here] = spec[: 2 * fr].astype(bf)
        send_a_ref[: 2 * fr, here] = spec[2 * fr : 4 * fr].astype(bf)
        own_ref[:, here] = spec[4 * fr :]

    group = min(GROUP, fc)
    piece = min(64, group)
    for start in range(0, fc, group):
        for part in range(start, start + group, piece):
            make_columns(part, piece)
        if start == 0:
            load_phi.wait()
            for b in range(half // LANES):
                left = jnp.tanh(phi_ref[:, b * LANES : (b + 1) * LANES])
                right = mirrored(jnp.tanh(phi_ref[:, cols - (b + 1) * LANES : cols - b * LANES]))
                mask_ref[:, b * LANES : (b + 1) * LANES] = (left + right).astype(bf)
                mask_ref[:, half + b * LANES : half + (b + 1) * LANES] = (left - right).astype(bf)
        transform(start, group)
    tops = [phi_ref[i : i + 1, q : q + fc] for i in range(HALO) for q in range(0, cols, fc)]
    lows = [
        phi_ref[rows - HALO + i : rows - HALO + i + 1, q : q + fc]
        for i in range(HALO)
        for q in range(0, cols, fc)
    ]
    tops = jnp.concatenate(tops, axis=0)
    lows = jnp.concatenate(lows, axis=0)
    send_a_ref[2 * fr :] = jnp.where(first > 0, lows, tops).astype(bf)
    send_b_ref[2 * fr :] = jnp.where(second > 0, lows, tops).astype(bf)


def second_kernel(
    defocus_ref,
    freq_ref,
    kernels_hbm,
    psi_hbm,
    target_hbm,
    inner_ref,
    inner_t_ref,
    k_re_ref,
    k_im_ref,
    goal_ref,
    kernels_ref,
    psi_ref,
    target_ref,
    sems,
):
    rows, cols = target_ref.shape
    half = cols // 2
    fr = psi_ref.shape[0]
    load_psi = pltpu.make_async_copy(psi_hbm, psi_ref, sems.at[0])
    load_kernels = pltpu.make_async_copy(kernels_hbm, kernels_ref, sems.at[1])
    load_target = pltpu.make_async_copy(target_hbm, target_ref, sems.at[2])
    load_psi.start()
    load_kernels.start()
    load_target.start()
    window = rows + 2 * MARGIN
    bf = jnp.bfloat16
    across = freq_ref[0:1, :]
    down = freq_ref[...].T[: 2 * fr, :1]

    inner_ref[...] = interleaved(down, (2 * fr, 2 * rows), 0, fr, MARGIN, window).astype(bf)
    table = interleaved(across, (2 * rows, LANES), 1, fr, MARGIN, window)
    inner_t_ref[...] = table[:, : 2 * fr].astype(bf)

    load_psi.wait()
    middle = (LEVELS - 1) / 2.0
    defocus = (defocus_ref[0].astype(jnp.float32) - middle) * (1.0 / middle)
    turn_c, turn_s = cos_sin(psi_ref[...] * defocus)
    load_kernels.wait()
    for k in range(kernels_ref.shape[1]):
        k_re_ref[k] = kernels_ref[0, k] * turn_c - kernels_ref[1, k] * turn_s
        k_im_ref[k] = kernels_ref[0, k] * turn_s + kernels_ref[1, k] * turn_c

    load_target.wait()
    goal_ref[:, :half] = target_ref[:, :half].astype(jnp.float32)
    for b in range(half // LANES):
        goal_ref[:, half + b * LANES : half + (b + 1) * LANES] = mirrored(
            target_ref[:, cols - (b + 1) * LANES : cols - b * LANES].astype(jnp.float32)
        )


def third_kernel(strips, groups, freq_ref, phi_ref, part_ref, tall_ref, far_ref, slope_ref):
    rows, cols = phi_ref.shape
    fr = part_ref.shape[0] // 2
    window = rows + 2 * MARGIN
    bf = jnp.bfloat16
    place, first, second, first_in, second_in = partners(strips)
    across = freq_ref[0:1, :]

    tall = rows + 2 * PAD
    for index, (offset, keep) in enumerate(((0, True), (first, first_in), (second, second_in))):
        table, spot = rotation(
            across, (2 * tall, LANES), tall, 1, fr, MARGIN - PAD - offset * rows, window
        )
        keep = keep & (spot >= 0) & (spot < window)
        tall_ref[index] = jnp.where(keep, table, 0.0)[:, : 2 * fr].astype(bf)
    shape = (4 * HALO, LANES)
    index = lax.broadcasted_iota(jnp.int32, shape, 0)
    imag_row = index >= 2 * HALO
    index = jnp.where(imag_row, index - 2 * HALO, index)
    low = index >= HALO
    row = jnp.where(low, index + (rows - HALO), index - HALO)
    imag = lax.broadcasted_iota(jnp.int32, shape, 1) >= fr
    for group, offsets in enumerate(groups.values()):
        total = jnp.zeros(shape, jnp.float32)
        for offset in offsets:
            spot = row - offset * rows + MARGIN
            keep = (spot >= 0) & (spot < window) & (low if offset > 0 else ~low)
            keep = keep & (place - offset >= 0) & (place - offset < strips)
            c, s = turn(across * spot.astype(jnp.float32), float(window))
            total = total + jnp.where(keep, quarter(imag_row, imag, c, s), 0.0)
        far_ref[group] = total[:, : 2 * fr].astype(bf)

    scale = 1.0 / float(window * cols) ** 0.5
    mask = jnp.tanh(phi_ref[...])
    slope_ref[...] = (step_size * scale) * (1.0 - mask * mask)


def main_kernel(
    own_ref,
    from_a_ref,
    from_b_ref,
    goal_ref,
    table_ref,
    inner_ref,
    inner_t_ref,
    k_re_ref,
    k_im_ref,
    out_ref,
    q_ref,
    x_ref,
):
    rows, cols = goal_ref.shape
    half = cols // 2
    count, fr, _ = k_re_ref.shape
    scale = 1.0 / float((rows + 2 * MARGIN) * cols) ** 0.5
    bf = jnp.bfloat16
    f32 = jnp.float32

    spec = scale * (
        own_ref[...] + from_a_ref[: 2 * fr].astype(f32) + from_b_ref[: 2 * fr].astype(f32)
    )
    s_re, s_im = spec[:fr], spec[fr:]
    unit = 16 * count
    for k in range(count):
        k_re, k_im = k_re_ref[k], k_im_ref[k]
        g = jnp.concatenate([k_re * s_re - k_im * s_im, k_re * s_im + k_im * s_re], axis=0)
        q = dot(inner_t_ref[...], g.astype(bf)).astype(bf)
        for r in range(rows // 8):
            q_ref[r * unit + 16 * k : r * unit + 16 * k + 16] = q[16 * r : 16 * r + 16]

    gain = 4.0 * slope_resist / count * scale
    norm = scale * scale / count

    def weight(intensity, goal):
        resist = jax.nn.sigmoid(slope_resist * (norm * intensity - level_resist))
        return gain * (resist - goal) * resist * (1.0 - resist)

    width = min(CHUNK, half)
    for start in range(0, half, width):
        left_half = slice(start, start + width)
        right_half = slice(half + start, half + start + width)
        af = dot(q_ref[...], table_ref[:, left_half])
        db = dot(q_ref[...], table_ref[:, right_half])
        for r in range(rows // 8):

            def parts(k):
                at = r * unit + 16 * k
                return af[at : at + 8], db[at + 8 : at + 16], af[at + 8 : at + 16], db[at : at + 8]

            even = 0.0
            cross = 0.0
            for k in range(count):
                a, b, f, d = parts(k)
                even = even + ((a * a + f * f) + (d * d + b * b))
                cross = cross + (a * b - d * f)
            cross = 2.0 * cross
            here = slice(8 * r, 8 * r + 8)
            w_left = weight(even - cross, goal_ref[here, left_half])
            w_right = weight(even + cross, goal_ref[here, right_half])
            p_w = w_left + w_right
            q_w = w_right - w_left
            for k in range(count):
                a, b, f, d = parts(k)
                at = slice(r * unit + 16 * k, r * unit + 16 * k + 16)
                x_ref[at, left_half] = jnp.concatenate(
                    [p_w * a + q_w * b, p_w * f - q_w * d], axis=0
                ).astype(bf)
                x_ref[at, right_half] = jnp.concatenate(
                    [p_w * d - q_w * f, q_w * a + p_w * b], axis=0
                ).astype(bf)

    q_ref[...] = dot_t(x_ref[...], table_ref[...]).astype(bf)
    y_re = 0.0
    y_im = 0.0
    for k in range(count):
        u = jnp.concatenate(
            [q_ref[r * unit + 16 * k : r * unit + 16 * k + 16] for r in range(rows // 8)], axis=0
        )
        w = scale * dot(inner_ref[...], u)
        w_re, w_im = w[:fr], w[fr:]
        k_re, k_im = k_re_ref[k], k_im_ref[k]
        y_re = y_re + (k_re * w_re + k_im * w_im)
        y_im = y_im + (k_re * w_im - k_im * w_re)
    out_ref[:fr] = y_re.astype(bf)
    out_ref[fr:] = y_im.astype(bf)


def sum_kernel(part_ref, other_ref, far_ref, total_ref, *payload_refs):
    total = part_ref[...].astype(jnp.float32) + other_ref[...].astype(jnp.float32)
    total = total.astype(jnp.bfloat16)
    total_ref[...] = total
    for index, payload_ref in enumerate(payload_refs):
        payload_ref[...] = dot(far_ref[index], total).astype(jnp.bfloat16)


def final_kernel(
    strips,
    phi_ref,
    slope_ref,
    from_a_ref,
    from_b_ref,
    table_ref,
    tall_ref,
    y_own_ref,
    y_a_ref,
    y_b_ref,
    *rest,
):
    payload_refs = rest[:-10]
    out_hbm, halo_ref, out_ref, sems = rest[-10:-6]
    level_ref, level_across, level_both, next_ref, next_across, next_both = rest[-6:]
    place, first, _, _, _ = partners(strips)
    rows, cols = phi_ref.shape
    half = cols // 2
    blocks = cols // LANES
    tall = rows + 2 * PAD
    fc = y_own_ref.shape[1]
    lead = y_own_ref.shape[0]
    bf = jnp.bfloat16
    f32 = jnp.float32
    scale = 1.0 / float((rows + 2 * MARGIN) * cols) ** 0.5

    z = dot(tall_ref[0], y_own_ref[...])
    z = z + dot(tall_ref[1], y_a_ref[...]) + dot(tall_ref[2], y_b_ref[...])
    if payload_refs:
        down = lax.broadcasted_iota(jnp.int32, (2 * tall, 4 * HALO), 0)
        index = lax.broadcasted_iota(jnp.int32, (2 * tall, 4 * HALO), 1)
        imag = index >= 2 * HALO
        index = jnp.where(imag, index - 2 * HALO, index)
        goes = jnp.where(index < HALO, index + (PAD - HALO), index + (PAD + rows - HALO))
        goes = jnp.where(imag, goes + tall, goes)
        place_rows = jnp.where(down == goes, 1.0, 0.0).astype(bf)
        for payload_ref in payload_refs:
            z = z + dot(place_rows, payload_ref[...])
    z = z.astype(bf)
    even = dot(z[:tall], table_ref[:, :half])
    odd = dot(z[tall:], table_ref[:, half:])

    halo_ref[...] = jnp.zeros_like(halo_ref)
    edges_a = from_a_ref[lead:].astype(f32)
    edges_b = from_b_ref[lead:].astype(f32)
    above = jnp.where(first < 0, edges_a, edges_b)
    below = jnp.where(first < 0, edges_b, edges_a)
    per_row = cols // fc
    for i in range(HALO):
        for q in range(per_row):
            here = slice(q * fc, (q + 1) * fc)
            spot = i * per_row + q
            halo_ref[PAD - HALO + i : PAD - HALO + i + 1, here] = above[spot : spot + 1]
            halo_ref[PAD + i : PAD + i + 1, here] = below[spot : spot + 1]
    top_in = place > 0
    low_in = place < strips - 1

    def advance(b, grad):
        here = slice(b * LANES, (b + 1) * LANES)
        level_ref[b, PAD : PAD + rows] = phi_ref[:, here] - slope_ref[:, here] * grad[
            PAD : PAD + rows
        ]
        for inside, edge, to in ((top_in, 0, 0), (low_in, PAD, PAD + rows)):
            phi = halo_ref[edge : edge + PAD, here]
            mask = jnp.tanh(phi)
            slope = (step_size * scale) * (1.0 - mask * mask)
            level_ref[b, to : to + PAD] = jnp.where(
                inside, phi - slope * grad[to : to + PAD], 0.0
            )

    for b in range(half // LANES):
        part = slice(b * LANES, (b + 1) * LANES)
        advance(b, even[:, part] - odd[:, part])
        advance(blocks - 1 - b, mirrored(even[:, part] + odd[:, part]))

    lane = lax.broadcasted_iota(jnp.int32, (8, LANES), 1)
    nothing = jnp.zeros((8, LANES), f32)

    def beside(values):
        ahead = [pltpu.roll(value, LANES - 1, 1) for value in values] + [nothing]
        behind = [nothing] + [pltpu.roll(value, 1, 1) for value in values]
        for b in range(len(values)):
            right = jnp.where(lane == LANES - 1, ahead[b + 1], ahead[b])
            left = jnp.where(lane == 0, behind[b], behind[b + 1])
            yield right - left, right + left

    def sweep(refs, at, b):
        source, across_ref, both_ref = refs
        here = slice(at, at + 8)
        c = source[b, here]
        up, down = source[b, at + 1 : at + 9], source[b, at - 1 : at + 7]
        y = across_ref[b, here]
        crossed = across_ref[b, at + 1 : at + 9] - across_ref[b, at - 1 : at + 7]
        twice = c + c
        x = up - down
        second_x = (up + down) - twice
        second_y = both_ref[b, here] - twice
        x_x = x * x
        y_y = y * y
        numer = second_x * y_y + second_y * x_x - (0.5 * x) * y * crossed
        return c + flow_rate * (numer / (4.0 + x_x + y_y))

    levels = (level_ref, level_across, level_both)
    nexts = (next_ref, next_across, next_both)

    def fill(refs, at, values):
        for b, (difference, total) in enumerate(beside(values)):
            refs[1][b, at : at + 8] = difference
            refs[2][b, at : at + 8] = total

    for at in range(0, tall, 8):
        fill(levels, at, [level_ref[b, at : at + 8] for b in range(blocks)])
    starts = list(range(PAD - 1, PAD + rows - 7, 8))
    if starts[-1] + 8 < PAD + rows + 1:
        starts.append(PAD + rows - 7)
    for at in starts:
        values = [sweep(levels, at, b) for b in range(blocks)]
        if at < PAD or at + 8 > PAD + rows:
            spot = lax.broadcasted_iota(jnp.int32, (8, LANES), 0) + at
            keep = ((spot >= PAD) | top_in) & ((spot < PAD + rows) | low_in)
            values = [jnp.where(keep, value, 0.0) for value in values]
        for b in range(blocks):
            next_ref[b, at : at + 8] = values[b]
        fill(nexts, at, values)
    copies = []
    for index in range(rows // 8):
        here = slice(8 * index, 8 * index + 8)
        for b in range(blocks):
            out_ref[here, b * LANES : (b + 1) * LANES] = sweep(nexts, PAD + 8 * index, b)
        here = pl.ds(8 * index, 8)
        copies.append(pltpu.make_async_copy(out_ref.at[here], out_hbm.at[here], sems.at[index]))
        copies[-1].start()
    for copy in copies:
        copy.wait()


def spec(kind):
    return pl.BlockSpec(memory_space={"v": pltpu.VMEM, "s": pltpu.SMEM, "h": pltpu.HBM}[kind])


def call(kernel, outs, args, kinds=None, out_kinds=None, scratch=(), limit=24, flops=1000000):
    kinds = kinds or "v" * len(args)
    out_kinds = out_kinds or "v" * len(outs)
    args = [
        pltpu.with_memory_space_constraint(arg, pltpu.HBM) if kind == "h" else arg
        for kind, arg in zip(kinds, args)
    ]
    return pl.pallas_call(
        kernel,
        out_shape=outs,
        in_specs=[spec(kind) for kind in kinds],
        out_specs=[spec(kind) for kind in out_kinds],
        scratch_shapes=list(scratch),
        compiler_params=pltpu.CompilerParams(vmem_limit_bytes=limit << 20),
        cost_estimate=pl.CostEstimate(flops=flops, bytes_accessed=4 << 20, transcendentals=0),
    )(*args)


def pair_up(block, first):
    strips, planes = lax.axis_size("strip"), lax.axis_size("focus")
    moves = []
    for strip in range(strips):
        up = (strip % 2 == 0) == first
        partner = strip + 1 if up else strip - 1
        for plane in range(planes):
            here = strip * planes + plane
            if 0 <= partner < strips:
                moves.append((here, partner * planes + plane))
            else:
                moves.append((here, strip * planes + (plane ^ 1 if planes > 1 else plane)))
    return lax.ppermute(block, ("strip", "focus"), moves)


def on_device(phi, target, defocus_ids, kernels, psi, row_freqs, col_freqs):
    rows, cols = phi.shape
    fr, fc = psi.shape
    count = kernels.shape[1]
    strips = lax.axis_size("strip")
    planes = lax.axis_size("focus")
    groups = offset_groups(rows, strips)
    tall = rows + 2 * PAD
    bf = jnp.bfloat16
    f32 = jnp.float32
    shape = jax.ShapeDtypeStruct
    packet = shape((2 * fr + HALO * (cols // fc), fc), bf)
    row_freqs = row_freqs.reshape(1, fr)

    table, s_own, send_a, send_b, phi, freqs = call(
        functools.partial(first_kernel, strips),
        [
            shape((fc, cols), bf),
            shape((2 * fr, fc), f32),
            packet,
            packet,
            shape((rows, cols), f32),
            shape((8, LANES), f32),
        ],
        (phi, row_freqs, col_freqs.reshape(1, fc)),
        kinds="hhh",
        scratch=[
            pltpu.VMEM((rows, cols), bf),
            pltpu.VMEM((1, fr), jnp.int32),
            pltpu.VMEM((1, fc), jnp.int32),
            pltpu.SemaphoreType.DMA((3,)),
        ],
    )
    from_b = pair_up(send_b, False)
    from_a = pair_up(send_a, True)
    inner, inner_t, k_re, k_im, goal = call(
        second_kernel,
        [
            shape((2 * fr, 2 * rows), bf),
            shape((2 * rows, 2 * fr), bf),
            shape((count, fr, fc), f32),
            shape((count, fr, fc), f32),
            shape((rows, cols), f32),
        ],
        (defocus_ids, freqs, kernels, psi, target),
        kinds="svhhh",
        scratch=[
            pltpu.VMEM(kernels.shape, f32),
            pltpu.VMEM(psi.shape, f32),
            pltpu.VMEM(target.shape, jnp.int32),
            pltpu.SemaphoreType.DMA((3,)),
        ],
        flops=4000000000,
    )
    (part,) = call(
        main_kernel,
        [shape((2 * fr, fc), bf)],
        (s_own, from_a, from_b, goal, table, inner, inner_t, k_re, k_im),
        scratch=[
            pltpu.VMEM((count * 2 * rows, fc), bf),
            pltpu.VMEM((count * 2 * rows, cols), bf),
        ],
        flops=4000000000,
    )
    tall_t, far_t, slope = call(
        functools.partial(third_kernel, strips, groups),
        [
            shape((3, 2 * tall, 2 * fr), bf),
            shape((max(1, len(groups)), 4 * HALO, 2 * fr), bf),
            shape((rows, cols), f32),
        ],
        (freqs, phi, part),
        flops=2000000000,
    )
    step = 1
    other = jnp.zeros_like(part)
    while step < planes:
        if step > 1:
            part = lax.optimization_barrier(
                (part.astype(f32) + other.astype(f32)).astype(bf)
            )
        other = lax.ppermute(part, "focus", [(i, i ^ step) for i in range(planes)])
        step *= 2
    total, *payloads = call(
        sum_kernel,
        [shape((2 * fr, fc), bf)] + [shape((4 * HALO, fc), bf)] * len(groups),
        (part, other, far_t),
    )
    far = [
        lax.ppermute(payload, "strip", [(i, (i - turn_by) % strips) for i in range(strips)])
        for turn_by, payload in zip(groups, payloads)
    ]
    y_b = pair_up(total, False)
    y_a = pair_up(total, True)
    return call(
        functools.partial(final_kernel, strips),
        [shape((rows, cols), f32)],
        (phi, slope, from_a, from_b, table, tall_t, total, y_a, y_b, *far),
        out_kinds="h",
        scratch=[
            pltpu.VMEM((2 * PAD, cols), f32),
            pltpu.VMEM((rows, cols), f32),
            pltpu.SemaphoreType.DMA((rows // 8,)),
        ]
        + [pltpu.VMEM((cols // LANES, tall, LANES), f32)] * 6,
    )[0]


def solution(mesh):
    return jax.shard_map(
        on_device,
        mesh=mesh,
        in_specs=(
            P(("tile", "strip"), None),
            P(("tile", "strip"), None),
            P(("tile", "focus")),
            P(),
            P(),
            P(),
            P(),
        ),
        out_specs=P(("tile", "strip"), None),
        check_vma=False,
    )
```

```python
import functools

import jax
import jax.numpy as jnp
from jax import lax
from jax.experimental import pallas as pl
from jax.experimental.pallas import tpu as pltpu
from jax.sharding import PartitionSpec as P

MARGIN = 64
LEVELS = 31
SWEEPS = 2
HALO = SWEEPS
LANES = 128
PAD = 8
CHUNK = 256
GROUPS = (4, 4)

slope_resist = 4.0
level_resist = 0.5
step_size = 1.0
flow_rate = 0.2

SIN_TERMS = (3.1415926401307073, -5.167710083507878, 2.550077523214199, -0.5982912856179897, 0.07765766030124945)
COS_TERMS = (0.9999999532476078, -4.934792830619626, 4.0584113528622625, -1.3318765680789622, 0.2196896110945085)


def cos_sin(t):
    square = t * t
    s = SIN_TERMS[-1] * square + SIN_TERMS[-2]
    for term in SIN_TERMS[-3::-1]:
        s = s * square + term
    s = s * t
    c = COS_TERMS[-1] * square + COS_TERMS[-2]
    for term in COS_TERMS[-3::-1]:
        c = c * square + term
    twice = s + s
    return 1.0 - twice * s, twice * c


def turn(product, period):
    if float(period).is_integer() and int(period) & (int(period) - 1) == 0:
        t = product * (1.0 / period)
        return cos_sin(t - jnp.round(t))
    rest = product - jnp.round(product * (1.0 / period)) * period
    return cos_sin(rest * (1.0 / period))


def mirrored(block):
    spots = (LANES - 1) - lax.broadcasted_iota(jnp.int32, block.shape, 1)
    return jnp.take_along_axis(block, spots, axis=1, mode="promise_in_bounds")


def dot(lhs_mat, rhs_mat):
    return jnp.dot(lhs_mat, rhs_mat, preferred_element_type=jnp.float32)


def dot_t(lhs_mat, rhs_mat):
    return lax.dot_general(
        lhs_mat, rhs_mat, (((1,), (1,)), ((), ())), preferred_element_type=jnp.float32
    )


def offset_groups(rows, strips):
    reach = (MARGIN + HALO + rows - 1) // rows
    groups = {}
    for offset in range(-reach, reach + 1):
        if abs(offset) > 1:
            groups.setdefault(offset % strips, []).append(offset)
    return groups


def partners(strips):
    place = lax.axis_index("strip")
    first = jnp.where(place % 2 == 0, 1, -1)
    second = -first

    def inside(offset):
        return (place + offset >= 0) & (place + offset < strips)

    return place, first, second, inside(first), inside(second)


def quarter(second, imag, c, s):
    return jnp.where(second == imag, c, jnp.where(second, s, -s))


def rotation(freqs, shape, length, freq_dim, fr, start, period):
    spot = lax.broadcasted_iota(jnp.int32, shape, 1 - freq_dim)
    second = spot >= length
    spot = jnp.where(second, spot - length, spot) + start
    imag = lax.broadcasted_iota(jnp.int32, shape, freq_dim) >= fr
    c, s = turn(freqs * spot.astype(jnp.float32), float(period))
    return quarter(second, imag, c, s), spot


def interleaved(freqs, shape, freq_dim, fr, start, period):
    index = lax.broadcasted_iota(jnp.int32, shape, 1 - freq_dim)
    spot = ((index >> 4) << 3) + (index & 7) + start
    second = (index & 8) > 0
    imag = lax.broadcasted_iota(jnp.int32, shape, freq_dim) >= fr
    c, s = turn(freqs * spot.astype(jnp.float32), float(period))
    return quarter(second, imag, c, s)


def row_freq_lanes(row_freqs_ref, freq_ref):
    fr = row_freqs_ref.shape[1]
    freqs = jnp.broadcast_to(row_freqs_ref[...].astype(jnp.float32), (8, fr))
    freq_ref[...] = jnp.zeros_like(freq_ref)
    freq_ref[:, 0:fr] = freqs
    freq_ref[:, fr : 2 * fr] = freqs


def first_kernel(
    strips,
    phi_hbm,
    row_freqs_hbm,
    col_freqs_hbm,
    table_ref,
    own_ref,
    send_a_ref,
    send_b_ref,
    phi_ref,
    freq_ref,
    mask_ref,
    row_freqs_ref,
    col_freqs_ref,
    sems,
):
    rows, cols = phi_ref.shape
    half = cols // 2
    fr, fc = row_freqs_ref.shape[1], table_ref.shape[0]
    window = rows + 2 * MARGIN
    bf = jnp.bfloat16
    load_cols = pltpu.make_async_copy(col_freqs_hbm, col_freqs_ref, sems.at[0])
    load_rows = pltpu.make_async_copy(row_freqs_hbm, row_freqs_ref, sems.at[1])
    load_phi = pltpu.make_async_copy(phi_hbm, phi_ref, sems.at[2])
    load_cols.start()
    load_rows.start()
    load_phi.start()
    _, first, second, first_in, second_in = partners(strips)

    load_cols.wait()
    load_rows.wait()
    row_freq_lanes(row_freqs_ref, freq_ref)
    down = freq_ref[...].T[:fr, :1]
    spot = lax.broadcasted_iota(jnp.int32, (fr, 2 * rows), 1)
    later = spot >= rows
    spot = jnp.where(later, spot - rows, spot)
    c, s = turn(down * (spot + MARGIN).astype(jnp.float32), float(window))
    turn_c, turn_s = turn(jnp.broadcast_to(down, c.shape) * float(rows), float(window))

    def rows_in(c, s, offset, keep):
        at = spot + MARGIN - offset * rows
        keep = keep & (at >= 0) & (at < window)
        c = jnp.where(keep, c, 0.0)
        s = jnp.where(keep, s, 0.0)
        return jnp.concatenate([jnp.where(later, s, c), jnp.where(later, c, -s)], axis=0).astype(bf)

    sign = -first.astype(jnp.float32)
    turn_s = sign * turn_s
    in_all = jnp.concatenate(
        [
            rows_in(c * turn_c + s * turn_s, s * turn_c - c * turn_s, second, second_in),
            rows_in(c * turn_c - s * turn_s, s * turn_c + c * turn_s, first, first_in),
            rows_in(c, s, 0, True),
        ],
        axis=0,
    )

    freq_row = jnp.broadcast_to(col_freqs_ref[...].astype(jnp.float32), (8, fc))
    step_row_c, step_row_s = turn(freq_row * float(LANES), float(cols))
    kind = lax.broadcasted_iota(jnp.int32, (8, fc), 0)
    packed = jnp.where(kind == 0, freq_row, jnp.where(kind == 1, step_row_c, step_row_s)).T

    def make_columns(start, number):
        f = packed[start : start + number, 0:1]
        spot = lax.broadcasted_iota(jnp.int32, (number, LANES), 1).astype(jnp.float32)
        c, s = turn(f * (2.0 * spot + 1.0), 2.0 * cols)
        step_c = jnp.broadcast_to(packed[start : start + number, 1:2], (number, LANES))
        step_s = jnp.broadcast_to(packed[start : start + number, 2:3], (number, LANES))
        twice = 2.0 * step_c
        c_old, s_old = c, s
        here = slice(start, start + number)
        for b in range(half // LANES):
            if b == 1:
                c, s = c * step_c - s * step_s, s * step_c + c * step_s
            elif b:
                c, s, c_old, s_old = twice * c - c_old, twice * s - s_old, c, s
            table_ref[here, b * LANES : (b + 1) * LANES] = c.astype(bf)
            table_ref[here, half + b * LANES : half + (b + 1) * LANES] = s.astype(bf)

    def transform(start, number):
        here = slice(start, start + number)
        p_re = dot_t(mask_ref[:, :half], table_ref[here, :half])
        p_im = -dot_t(mask_ref[:, half:], table_ref[here, half:])
        spec = dot(in_all, jnp.concatenate([p_re, p_im], axis=0).astype(bf))
        send_b_ref[: 2 * fr, here] = spec[: 2 * fr].astype(bf)
        send_a_ref[: 2 * fr, here] = spec[2 * fr : 4 * fr].astype(bf)
        own_ref[:, here] = spec[4 * fr :]

    piece = 64
    start = 0
    for share in GROUPS:
        group = fc * share // 8
        for part in range(start, start + group, piece):
            make_columns(part, piece)
        if start == 0:
            load_phi.wait()
            for b in range(half // LANES):
                left = jnp.tanh(phi_ref[:, b * LANES : (b + 1) * LANES])
                right = mirrored(jnp.tanh(phi_ref[:, cols - (b + 1) * LANES : cols - b * LANES]))
                mask_ref[:, b * LANES : (b + 1) * LANES] = (left + right).astype(bf)
                mask_ref[:, half + b * LANES : half + (b + 1) * LANES] = (left - right).astype(bf)
        transform(start, group)
        start += group
    tops = [phi_ref[i : i + 1, q : q + fc] for i in range(HALO) for q in range(0, cols, fc)]
    lows = [
        phi_ref[rows - HALO + i : rows - HALO + i + 1, q : q + fc]
        for i in range(HALO)
        for q in range(0, cols, fc)
    ]
    tops = jnp.concatenate(tops, axis=0)
    lows = jnp.concatenate(lows, axis=0)
    send_a_ref[2 * fr :] = jnp.where(first > 0, lows, tops).astype(bf)
    send_b_ref[2 * fr :] = jnp.where(second > 0, lows, tops).astype(bf)


def second_kernel(
    defocus_ref,
    freq_ref,
    kernels_hbm,
    psi_hbm,
    target_hbm,
    inner_ref,
    inner_t_ref,
    k_re_ref,
    k_im_ref,
    goal_ref,
    kernels_ref,
    psi_ref,
    target_ref,
    sems,
):
    rows, cols = target_ref.shape
    half = cols // 2
    fr = psi_ref.shape[0]
    load_psi = pltpu.make_async_copy(psi_hbm, psi_ref, sems.at[0])
    load_kernels = pltpu.make_async_copy(kernels_hbm, kernels_ref, sems.at[1])
    load_target = pltpu.make_async_copy(target_hbm, target_ref, sems.at[2])
    load_psi.start()
    load_kernels.start()
    load_target.start()
    window = rows + 2 * MARGIN
    bf = jnp.bfloat16
    across = freq_ref[0:1, :]
    down = freq_ref[...].T[: 2 * fr, :1]

    inner_ref[...] = interleaved(down, (2 * fr, 2 * rows), 0, fr, MARGIN, window).astype(bf)
    table = interleaved(across, (2 * rows, LANES), 1, fr, MARGIN, window)
    inner_t_ref[...] = table[:, : 2 * fr].astype(bf)

    load_psi.wait()
    middle = (LEVELS - 1) / 2.0
    defocus = (defocus_ref[0].astype(jnp.float32) - middle) * (1.0 / middle)
    turn_c, turn_s = cos_sin(psi_ref[...] * (defocus * (0.5 / jnp.pi)))
    load_kernels.wait()
    for k in range(kernels_ref.shape[1]):
        k_re_ref[k] = kernels_ref[0, k] * turn_c - kernels_ref[1, k] * turn_s
        k_im_ref[k] = kernels_ref[0, k] * turn_s + kernels_ref[1, k] * turn_c

    load_target.wait()
    goal_ref[:, :half] = target_ref[:, :half].astype(jnp.float32)
    for b in range(half // LANES):
        goal_ref[:, half + b * LANES : half + (b + 1) * LANES] = mirrored(
            target_ref[:, cols - (b + 1) * LANES : cols - b * LANES].astype(jnp.float32)
        )


def third_kernel(
    strips,
    groups,
    freq_ref,
    phi_ref,
    from_a_ref,
    from_b_ref,
    part_ref,
    tall_ref,
    far_ref,
    slope_ref,
    halo_ref,
    halo_slope_ref,
):
    rows, cols = phi_ref.shape
    fr, fc = part_ref.shape[0] // 2, part_ref.shape[1]
    window = rows + 2 * MARGIN
    bf = jnp.bfloat16
    place, first, second, first_in, second_in = partners(strips)
    across = freq_ref[0:1, :]

    tall = rows + 2 * PAD
    for index, (offset, keep) in enumerate(((0, True), (first, first_in), (second, second_in))):
        table, spot = rotation(
            across, (2 * tall, LANES), tall, 1, fr, MARGIN - PAD - offset * rows, window
        )
        keep = keep & (spot >= 0) & (spot < window)
        tall_ref[index] = jnp.where(keep, table, 0.0)[:, : 2 * fr].astype(bf)
    shape = (4 * HALO, LANES)
    index = lax.broadcasted_iota(jnp.int32, shape, 0)
    imag_row = index >= 2 * HALO
    index = jnp.where(imag_row, index - 2 * HALO, index)
    low = index >= HALO
    row = jnp.where(low, index + (rows - HALO), index - HALO)
    imag = lax.broadcasted_iota(jnp.int32, shape, 1) >= fr
    for group, offsets in enumerate(groups.values()):
        total = jnp.zeros(shape, jnp.float32)
        for offset in offsets:
            spot = row - offset * rows + MARGIN
            keep = (spot >= 0) & (spot < window) & (low if offset > 0 else ~low)
            keep = keep & (place - offset >= 0) & (place - offset < strips)
            c, s = turn(across * spot.astype(jnp.float32), float(window))
            total = total + jnp.where(keep, quarter(imag_row, imag, c, s), 0.0)
        far_ref[group] = total[:, : 2 * fr].astype(bf)

    scale = 1.0 / float(window * cols) ** 0.5
    mask = jnp.tanh(phi_ref[...])
    slope_ref[...] = (step_size * scale) * (1.0 - mask * mask)

    halo_ref[...] = jnp.zeros_like(halo_ref)
    edges_a = from_a_ref[2 * fr :].astype(jnp.float32)
    edges_b = from_b_ref[2 * fr :].astype(jnp.float32)
    top_in = (place > 0).astype(jnp.float32)
    low_in = (place < strips - 1).astype(jnp.float32)
    above = jnp.where(first < 0, edges_a, edges_b) * top_in
    below = jnp.where(first < 0, edges_b, edges_a) * low_in
    per_row = cols // fc
    for i in range(HALO):
        for q in range(per_row):
            here = slice(q * fc, (q + 1) * fc)
            spot = i * per_row + q
            halo_ref[PAD - HALO + i : PAD - HALO + i + 1, here] = above[spot : spot + 1]
            halo_ref[PAD + i : PAD + i + 1, here] = below[spot : spot + 1]
    for edge, inside in ((0, top_in), (PAD, low_in)):
        mask = jnp.tanh(halo_ref[edge : edge + PAD])
        halo_slope_ref[edge : edge + PAD] = (step_size * scale) * inside * (1.0 - mask * mask)


def own_kernel(tall_ref, y_ref, z_ref):
    z_ref[...] = dot(tall_ref[0], y_ref[...])


def main_kernel(
    own_ref,
    from_a_ref,
    from_b_ref,
    goal_ref,
    table_ref,
    inner_ref,
    inner_t_ref,
    k_re_ref,
    k_im_ref,
    out_ref,
    q_ref,
    x_ref,
):
    rows, cols = goal_ref.shape
    half = cols // 2
    count, fr, _ = k_re_ref.shape
    scale = 1.0 / float((rows + 2 * MARGIN) * cols) ** 0.5
    bf = jnp.bfloat16
    f32 = jnp.float32

    spec = scale * (
        own_ref[...] + from_a_ref[: 2 * fr].astype(f32) + from_b_ref[: 2 * fr].astype(f32)
    )
    s_re, s_im = spec[:fr], spec[fr:]
    unit = 16 * count
    for k in range(count):
        k_re, k_im = k_re_ref[k], k_im_ref[k]
        g = jnp.concatenate([k_re * s_re - k_im * s_im, k_re * s_im + k_im * s_re], axis=0)
        q = dot(inner_t_ref[...], g.astype(bf)).astype(bf)
        for r in range(rows // 8):
            q_ref[r * unit + 16 * k : r * unit + 16 * k + 16] = q[16 * r : 16 * r + 16]

    gain = 4.0 * slope_resist / count * scale
    norm = scale * scale / count

    def weight(intensity, goal):
        resist = jax.nn.sigmoid(slope_resist * (norm * intensity - level_resist))
        return gain * (resist - goal) * resist * (1.0 - resist)

    width = min(CHUNK, half)
    for start in range(0, half, width):
        left_half = slice(start, start + width)
        right_half = slice(half + start, half + start + width)
        af = dot(q_ref[...], table_ref[:, left_half])
        db = dot(q_ref[...], table_ref[:, right_half])
        for r in range(rows // 8):

            def parts(k):
                at = r * unit + 16 * k
                return af[at : at + 8], db[at + 8 : at + 16], af[at + 8 : at + 16], db[at : at + 8]

            even = 0.0
            cross = 0.0
            for k in range(count):
                a, b, f, d = parts(k)
                even = even + ((a * a + f * f) + (d * d + b * b))
                cross = cross + (a * b - d * f)
            cross = 2.0 * cross
            here = slice(8 * r, 8 * r + 8)
            w_left = weight(even - cross, goal_ref[here, left_half])
            w_right = weight(even + cross, goal_ref[here, right_half])
            p_w = w_left + w_right
            q_w = w_right - w_left
            for k in range(count):
                a, b, f, d = parts(k)
                at = slice(r * unit + 16 * k, r * unit + 16 * k + 16)
                x_ref[at, left_half] = jnp.concatenate(
                    [p_w * a + q_w * b, p_w * f - q_w * d], axis=0
                ).astype(bf)
                x_ref[at, right_half] = jnp.concatenate(
                    [p_w * d - q_w * f, q_w * a + p_w * b], axis=0
                ).astype(bf)

    q_ref[...] = dot_t(x_ref[...], table_ref[...]).astype(bf)
    y_re = 0.0
    y_im = 0.0
    for k in range(count):
        u = jnp.concatenate(
            [q_ref[r * unit + 16 * k : r * unit + 16 * k + 16] for r in range(rows // 8)], axis=0
        )
        w = scale * dot(inner_ref[...], u)
        w_re, w_im = w[:fr], w[fr:]
        k_re, k_im = k_re_ref[k], k_im_ref[k]
        y_re = y_re + (k_re * w_re + k_im * w_im)
        y_im = y_im + (k_re * w_im - k_im * w_re)
    out_ref[:fr] = y_re.astype(bf)
    out_ref[fr:] = y_im.astype(bf)


def sum_kernel(part_ref, other_ref, far_ref, total_ref, *payload_refs):
    total = part_ref[...].astype(jnp.float32) + other_ref[...].astype(jnp.float32)
    total = total.astype(jnp.bfloat16)
    total_ref[...] = total
    for index, payload_ref in enumerate(payload_refs):
        payload_ref[...] = dot(far_ref[index], total).astype(jnp.bfloat16)


def final_kernel(
    strips,
    phi_ref,
    slope_ref,
    halo_ref,
    halo_slope_ref,
    table_ref,
    tall_ref,
    z_own_ref,
    y_a_ref,
    y_b_ref,
    *rest,
):
    payload_refs = rest[:-9]
    out_hbm, out_ref, sems = rest[-9:-6]
    level_ref, level_across, level_both, next_ref, next_across, next_both = rest[-6:]
    place, _, _, _, _ = partners(strips)
    rows, cols = phi_ref.shape
    half = cols // 2
    blocks = cols // LANES
    tall = rows + 2 * PAD
    bf = jnp.bfloat16
    f32 = jnp.float32

    z = z_own_ref[...] + dot(tall_ref[1], y_a_ref[...]) + dot(tall_ref[2], y_b_ref[...])
    if payload_refs:
        down = lax.broadcasted_iota(jnp.int32, (2 * tall, 4 * HALO), 0)
        index = lax.broadcasted_iota(jnp.int32, (2 * tall, 4 * HALO), 1)
        imag = index >= 2 * HALO
        index = jnp.where(imag, index - 2 * HALO, index)
        goes = jnp.where(index < HALO, index + (PAD - HALO), index + (PAD + rows - HALO))
        goes = jnp.where(imag, goes + tall, goes)
        place_rows = jnp.where(down == goes, 1.0, 0.0).astype(bf)
        for payload_ref in payload_refs:
            z = z + dot(place_rows, payload_ref[...])
    z = z.astype(bf)
    even = dot(z[:tall], table_ref[:, :half])
    odd = dot(z[tall:], table_ref[:, half:])

    top_in = place > 0
    low_in = place < strips - 1

    def advance(b, grad):
        here = slice(b * LANES, (b + 1) * LANES)
        level_ref[b, PAD : PAD + rows] = phi_ref[:, here] - slope_ref[:, here] * grad[
            PAD : PAD + rows
        ]
        for edge, to in ((0, 0), (PAD, PAD + rows)):
            step = halo_slope_ref[edge : edge + PAD, here] * grad[to : to + PAD]
            level_ref[b, to : to + PAD] = halo_ref[edge : edge + PAD, here] - step

    for b in range(half // LANES):
        part = slice(b * LANES, (b + 1) * LANES)
        advance(b, even[:, part] - odd[:, part])
        advance(blocks - 1 - b, mirrored(even[:, part] + odd[:, part]))

    lane = lax.broadcasted_iota(jnp.int32, (8, LANES), 1)
    nothing = jnp.zeros((8, LANES), f32)

    def beside(values):
        ahead = [pltpu.roll(value, LANES - 1, 1) for value in values] + [nothing]
        behind = [nothing] + [pltpu.roll(value, 1, 1) for value in values]
        for b in range(len(values)):
            right = jnp.where(lane == LANES - 1, ahead[b + 1], ahead[b])
            left = jnp.where(lane == 0, behind[b], behind[b + 1])
            yield right - left, right + left

    def sweep(refs, at, b):
        source, across_ref, both_ref = refs
        here = slice(at, at + 8)
        c = source[b, here]
        up, down = source[b, at + 1 : at + 9], source[b, at - 1 : at + 7]
        y = across_ref[b, here]
        crossed = across_ref[b, at + 1 : at + 9] - across_ref[b, at - 1 : at + 7]
        twice = c + c
        x = up - down
        second_x = (up + down) - twice
        second_y = both_ref[b, here] - twice
        x_x = x * x
        y_y = y * y
        numer = second_x * y_y + second_y * x_x - (0.5 * x) * y * crossed
        return c + flow_rate * (numer / (4.0 + x_x + y_y))

    levels = (level_ref, level_across, level_both)
    nexts = (next_ref, next_across, next_both)

    def fill(refs, at, values):
        for b, (difference, total) in enumerate(beside(values)):
            refs[1][b, at : at + 8] = difference
            refs[2][b, at : at + 8] = total

    def cover(first_row, end):
        starts = list(range(first_row, end - 7, 8))
        return starts if starts[-1] + 8 >= end else starts + [end - 8]

    for at in cover(PAD - 2, PAD + rows + 2):
        fill(levels, at, [level_ref[b, at : at + 8] for b in range(blocks)])
    for at in cover(PAD - 1, PAD + rows + 1):
        values = [sweep(levels, at, b) for b in range(blocks)]
        if at < PAD or at + 8 > PAD + rows:
            spot = lax.broadcasted_iota(jnp.int32, (8, LANES), 0) + at
            keep = ((spot >= PAD) | top_in) & ((spot < PAD + rows) | low_in)
            values = [jnp.where(keep, value, 0.0) for value in values]
        for b in range(blocks):
            next_ref[b, at : at + 8] = values[b]
        fill(nexts, at, values)
    copies = []
    for index in range(rows // 8):
        here = slice(8 * index, 8 * index + 8)
        for b in range(blocks):
            out_ref[here, b * LANES : (b + 1) * LANES] = sweep(nexts, PAD + 8 * index, b)
        here = pl.ds(8 * index, 8)
        copies.append(pltpu.make_async_copy(out_ref.at[here], out_hbm.at[here], sems.at[index]))
        copies[-1].start()
    for copy in copies:
        copy.wait()


def spec(kind):
    return pl.BlockSpec(memory_space={"v": pltpu.VMEM, "s": pltpu.SMEM, "h": pltpu.HBM}[kind])


def call(kernel, outs, args, kinds=None, out_kinds=None, scratch=(), limit=24, flops=1000000):
    kinds = kinds or "v" * len(args)
    out_kinds = out_kinds or "v" * len(outs)
    args = [
        pltpu.with_memory_space_constraint(arg, pltpu.HBM) if kind == "h" else arg
        for kind, arg in zip(kinds, args)
    ]
    return pl.pallas_call(
        kernel,
        out_shape=outs,
        in_specs=[spec(kind) for kind in kinds],
        out_specs=[spec(kind) for kind in out_kinds],
        scratch_shapes=list(scratch),
        compiler_params=pltpu.CompilerParams(vmem_limit_bytes=limit << 20),
        cost_estimate=pl.CostEstimate(flops=flops, bytes_accessed=4 << 20, transcendentals=0),
    )(*args)


def pair_up(block, first):
    strips, planes = lax.axis_size("strip"), lax.axis_size("focus")
    moves = []
    for strip in range(strips):
        up = (strip % 2 == 0) == first
        partner = strip + 1 if up else strip - 1
        for plane in range(planes):
            here = strip * planes + plane
            if 0 <= partner < strips:
                moves.append((here, partner * planes + plane))
            else:
                moves.append((here, strip * planes + (plane ^ 1 if planes > 1 else plane)))
    return lax.ppermute(block, ("strip", "focus"), moves)


def on_device(phi, target, defocus_ids, kernels, psi, row_freqs, col_freqs):
    rows, cols = phi.shape
    fr, fc = psi.shape
    count = kernels.shape[1]
    strips = lax.axis_size("strip")
    planes = lax.axis_size("focus")
    groups = offset_groups(rows, strips)
    tall = rows + 2 * PAD
    bf = jnp.bfloat16
    f32 = jnp.float32
    shape = jax.ShapeDtypeStruct
    packet = shape((2 * fr + HALO * (cols // fc), fc), bf)
    row_freqs = row_freqs.reshape(1, fr)

    table, s_own, send_a, send_b, phi, freqs = call(
        functools.partial(first_kernel, strips),
        [
            shape((fc, cols), bf),
            shape((2 * fr, fc), f32),
            packet,
            packet,
            shape((rows, cols), f32),
            shape((8, LANES), f32),
        ],
        (phi, row_freqs, col_freqs.reshape(1, fc)),
        kinds="hhh",
        scratch=[
            pltpu.VMEM((rows, cols), bf),
            pltpu.VMEM((1, fr), jnp.int32),
            pltpu.VMEM((1, fc), jnp.int32),
            pltpu.SemaphoreType.DMA((3,)),
        ],
    )
    from_b = pair_up(send_b, False)
    from_a = pair_up(send_a, True)
    inner, inner_t, k_re, k_im, goal = call(
        second_kernel,
        [
            shape((2 * fr, 2 * rows), bf),
            shape((2 * rows, 2 * fr), bf),
            shape((count, fr, fc), f32),
            shape((count, fr, fc), f32),
            shape((rows, cols), f32),
        ],
        (defocus_ids, freqs, kernels, psi, target),
        kinds="svhhh",
        scratch=[
            pltpu.VMEM(kernels.shape, f32),
            pltpu.VMEM(psi.shape, f32),
            pltpu.VMEM(target.shape, jnp.int32),
            pltpu.SemaphoreType.DMA((3,)),
        ],
        flops=4000000000,
    )
    (part,) = call(
        main_kernel,
        [shape((2 * fr, fc), bf)],
        (s_own, from_a, from_b, goal, table, inner, inner_t, k_re, k_im),
        scratch=[
            pltpu.VMEM((count * 2 * rows, fc), bf),
            pltpu.VMEM((count * 2 * rows, cols), bf),
        ],
        flops=4000000000,
    )
    tall_t, far_t, slope, halo, halo_slope = call(
        functools.partial(third_kernel, strips, groups),
        [
            shape((3, 2 * tall, 2 * fr), bf),
            shape((max(1, len(groups)), 4 * HALO, 2 * fr), bf),
            shape((rows, cols), f32),
            shape((2 * PAD, cols), f32),
            shape((2 * PAD, cols), f32),
        ],
        (freqs, phi, from_a, from_b, part),
        flops=2000000000,
    )
    step = 1
    other = jnp.zeros_like(part)
    while step < planes:
        if step > 1:
            part = lax.optimization_barrier(
                (part.astype(f32) + other.astype(f32)).astype(bf)
            )
        other = lax.ppermute(part, "focus", [(i, i ^ step) for i in range(planes)])
        step *= 2
    total, *payloads = call(
        sum_kernel,
        [shape((2 * fr, fc), bf)] + [shape((4 * HALO, fc), bf)] * len(groups),
        (part, other, far_t),
    )
    far = [
        lax.ppermute(payload, "strip", [(i, (i - turn_by) % strips) for i in range(strips)])
        for turn_by, payload in zip(groups, payloads)
    ]
    y_b = pair_up(total, False)
    y_a = pair_up(total, True)
    (z_own,) = call(own_kernel, [shape((2 * tall, fc), f32)], (tall_t, total), flops=2000000000)
    return call(
        functools.partial(final_kernel, strips),
        [shape((rows, cols), f32)],
        (phi, slope, halo, halo_slope, table, tall_t, z_own, y_a, y_b, *far),
        out_kinds="h",
        scratch=[
            pltpu.VMEM((rows, cols), f32),
            pltpu.SemaphoreType.DMA((rows // 8,)),
        ]
        + [pltpu.VMEM((cols // LANES, tall, LANES), f32)] * 6,
    )[0]


def solution(mesh):
    return jax.shard_map(
        on_device,
        mesh=mesh,
        in_specs=(
            P(("tile", "strip"), None),
            P(("tile", "strip"), None),
            P(("tile", "focus")),
            P(),
            P(),
            P(),
            P(),
        ),
        out_specs=P(("tile", "strip"), None),
        check_vma=False,
    )
```

```python
import functools

import jax
import jax.numpy as jnp
from jax import lax
from jax.experimental import pallas as pl
from jax.experimental.pallas import tpu as pltpu
from jax.sharding import PartitionSpec as P

MARGIN = 64
LEVELS = 31
SWEEPS = 2
HALO = SWEEPS
LANES = 128
PAD = 8
CHUNK = 256
GROUPS = (4, 4)

slope_resist = 4.0
level_resist = 0.5
step_size = 1.0
flow_rate = 0.2

SIN_TERMS = (3.1415926401307073, -5.167710083507878, 2.550077523214199, -0.5982912856179897, 0.07765766030124945)
COS_TERMS = (0.9999999532476078, -4.934792830619626, 4.0584113528622625, -1.3318765680789622, 0.2196896110945085)


def cos_sin(t):
    square = t * t
    s = SIN_TERMS[-1] * square + SIN_TERMS[-2]
    for term in SIN_TERMS[-3::-1]:
        s = s * square + term
    s = s * t
    c = COS_TERMS[-1] * square + COS_TERMS[-2]
    for term in COS_TERMS[-3::-1]:
        c = c * square + term
    twice = s + s
    return 1.0 - twice * s, twice * c


def turn(product, period):
    if float(period).is_integer() and int(period) & (int(period) - 1) == 0:
        t = product * (1.0 / period)
        return cos_sin(t - jnp.round(t))
    rest = product - jnp.round(product * (1.0 / period)) * period
    return cos_sin(rest * (1.0 / period))


def mirrored(block):
    spots = (LANES - 1) - lax.broadcasted_iota(jnp.int32, block.shape, 1)
    return jnp.take_along_axis(block, spots, axis=1, mode="promise_in_bounds")


def dot(lhs_mat, rhs_mat):
    return jnp.dot(lhs_mat, rhs_mat, preferred_element_type=jnp.float32)


def dot_t(lhs_mat, rhs_mat):
    return lax.dot_general(
        lhs_mat, rhs_mat, (((1,), (1,)), ((), ())), preferred_element_type=jnp.float32
    )


def offset_groups(rows, strips):
    reach = (MARGIN + HALO + rows - 1) // rows
    groups = {}
    for offset in range(-reach, reach + 1):
        if abs(offset) > 1:
            groups.setdefault(offset % strips, []).append(offset)
    return groups


def partners(strips):
    place = lax.axis_index("strip")
    first = jnp.where(place % 2 == 0, 1, -1)
    second = -first

    def inside(offset):
        return (place + offset >= 0) & (place + offset < strips)

    return place, first, second, inside(first), inside(second)


def quarter(second, imag, c, s):
    return jnp.where(second == imag, c, jnp.where(second, s, -s))


def rotation(freqs, shape, length, freq_dim, fr, start, period):
    spot = lax.broadcasted_iota(jnp.int32, shape, 1 - freq_dim)
    second = spot >= length
    spot = jnp.where(second, spot - length, spot) + start
    imag = lax.broadcasted_iota(jnp.int32, shape, freq_dim) >= fr
    c, s = turn(freqs * spot.astype(jnp.float32), float(period))
    return quarter(second, imag, c, s), spot


def interleaved(freqs, shape, freq_dim, fr, start, period):
    index = lax.broadcasted_iota(jnp.int32, shape, 1 - freq_dim)
    spot = ((index >> 4) << 3) + (index & 7) + start
    second = (index & 8) > 0
    imag = lax.broadcasted_iota(jnp.int32, shape, freq_dim) >= fr
    c, s = turn(freqs * spot.astype(jnp.float32), float(period))
    return quarter(second, imag, c, s)


def row_freq_lanes(row_freqs_ref, freq_ref):
    fr = row_freqs_ref.shape[1]
    freqs = jnp.broadcast_to(row_freqs_ref[...].astype(jnp.float32), (8, fr))
    freq_ref[...] = jnp.zeros_like(freq_ref)
    freq_ref[:, 0:fr] = freqs
    freq_ref[:, fr : 2 * fr] = freqs


def first_kernel(
    strips,
    phi_hbm,
    row_freqs_hbm,
    col_freqs_hbm,
    table_ref,
    own_ref,
    send_a_ref,
    send_b_ref,
    phi_ref,
    freq_ref,
    mask_ref,
    row_freqs_ref,
    col_freqs_ref,
    sems,
):
    rows, cols = phi_ref.shape
    half = cols // 2
    fr, fc = row_freqs_ref.shape[1], table_ref.shape[0]
    window = rows + 2 * MARGIN
    bf = jnp.bfloat16
    load_cols = pltpu.make_async_copy(col_freqs_hbm, col_freqs_ref, sems.at[0])
    load_rows = pltpu.make_async_copy(row_freqs_hbm, row_freqs_ref, sems.at[1])
    load_phi = pltpu.make_async_copy(phi_hbm, phi_ref, sems.at[2])
    load_cols.start()
    load_rows.start()
    load_phi.start()
    _, first, second, first_in, second_in = partners(strips)

    load_cols.wait()
    load_rows.wait()
    row_freq_lanes(row_freqs_ref, freq_ref)
    down = freq_ref[...].T[:fr, :1]
    spot = lax.broadcasted_iota(jnp.int32, (fr, 2 * rows), 1)
    later = spot >= rows
    spot = jnp.where(later, spot - rows, spot)
    c, s = turn(down * (spot + MARGIN).astype(jnp.float32), float(window))
    turn_c, turn_s = turn(jnp.broadcast_to(down, c.shape) * float(rows), float(window))

    def rows_in(c, s, offset, keep):
        at = spot + MARGIN - offset * rows
        keep = keep & (at >= 0) & (at < window)
        c = jnp.where(keep, c, 0.0)
        s = jnp.where(keep, s, 0.0)
        return jnp.concatenate([jnp.where(later, s, c), jnp.where(later, c, -s)], axis=0).astype(bf)

    sign = -first.astype(jnp.float32)
    turn_s = sign * turn_s
    in_all = jnp.concatenate(
        [
            rows_in(c * turn_c + s * turn_s, s * turn_c - c * turn_s, second, second_in),
            rows_in(c * turn_c - s * turn_s, s * turn_c + c * turn_s, first, first_in),
            rows_in(c, s, 0, True),
        ],
        axis=0,
    )

    freq_row = jnp.broadcast_to(col_freqs_ref[...].astype(jnp.float32), (8, fc))
    step_row_c, step_row_s = turn(freq_row * float(LANES), float(cols))
    kind = lax.broadcasted_iota(jnp.int32, (8, fc), 0)
    packed = jnp.where(kind == 0, freq_row, jnp.where(kind == 1, step_row_c, step_row_s)).T

    def make_columns(start, number):
        f = packed[start : start + number, 0:1]
        spot = lax.broadcasted_iota(jnp.int32, (number, LANES), 1).astype(jnp.float32)
        c, s = turn(f * (2.0 * spot + 1.0), 2.0 * cols)
        step_c = jnp.broadcast_to(packed[start : start + number, 1:2], (number, LANES))
        step_s = jnp.broadcast_to(packed[start : start + number, 2:3], (number, LANES))
        twice = 2.0 * step_c
        c_old, s_old = c, s
        here = slice(start, start + number)
        for b in range(half // LANES):
            if b == 1:
                c, s = c * step_c - s * step_s, s * step_c + c * step_s
            elif b:
                c, s, c_old, s_old = twice * c - c_old, twice * s - s_old, c, s
            table_ref[here, b * LANES : (b + 1) * LANES] = c.astype(bf)
            table_ref[here, half + b * LANES : half + (b + 1) * LANES] = s.astype(bf)

    def transform(start, number):
        here = slice(start, start + number)
        p_re = dot_t(mask_ref[:, :half], table_ref[here, :half])
        p_im = -dot_t(mask_ref[:, half:], table_ref[here, half:])
        spec = dot(in_all, jnp.concatenate([p_re, p_im], axis=0).astype(bf))
        send_b_ref[: 2 * fr, here] = spec[: 2 * fr].astype(bf)
        send_a_ref[: 2 * fr, here] = spec[2 * fr : 4 * fr].astype(bf)
        own_ref[:, here] = spec[4 * fr :]

    piece = 64
    start = 0
    for share in GROUPS:
        group = fc * share // 8
        for part in range(start, start + group, piece):
            make_columns(part, piece)
        if start == 0:
            load_phi.wait()
            for b in range(half // LANES):
                left = jnp.tanh(phi_ref[:, b * LANES : (b + 1) * LANES])
                right = mirrored(jnp.tanh(phi_ref[:, cols - (b + 1) * LANES : cols - b * LANES]))
                mask_ref[:, b * LANES : (b + 1) * LANES] = (left + right).astype(bf)
                mask_ref[:, half + b * LANES : half + (b + 1) * LANES] = (left - right).astype(bf)
        transform(start, group)
        start += group
    tops = [phi_ref[i : i + 1, q : q + fc] for i in range(HALO) for q in range(0, cols, fc)]
    lows = [
        phi_ref[rows - HALO + i : rows - HALO + i + 1, q : q + fc]
        for i in range(HALO)
        for q in range(0, cols, fc)
    ]
    tops = jnp.concatenate(tops, axis=0)
    lows = jnp.concatenate(lows, axis=0)
    send_a_ref[2 * fr :] = jnp.where(first > 0, lows, tops).astype(bf)
    send_b_ref[2 * fr :] = jnp.where(second > 0, lows, tops).astype(bf)


def defocus_kernel(defocus_ref, after_ref, out_ref):
    middle = (LEVELS - 1) / 2.0
    defocus = (defocus_ref[0].astype(jnp.float32) - middle) * (1.0 / middle)
    out_ref[...] = jnp.full(out_ref.shape, defocus, jnp.float32)


def kernels_at(defocus_ref, psi_ref, kernels_ref, k_re_ref, k_im_ref):
    cycles = psi_ref[...] * (defocus_ref[0:1, 0:1] * (0.5 / jnp.pi))
    turn_c, turn_s = cos_sin(cycles)
    for k in range(kernels_ref.shape[1]):
        k_re_ref[k] = kernels_ref[0, k] * turn_c - kernels_ref[1, k] * turn_s
        k_im_ref[k] = kernels_ref[0, k] * turn_s + kernels_ref[1, k] * turn_c


def second_kernel(
    defocus_ref,
    freq_ref,
    kernels_hbm,
    psi_hbm,
    target_hbm,
    inner_ref,
    inner_t_ref,
    k_re_ref,
    k_im_ref,
    goal_ref,
    kernels_ref,
    psi_ref,
    target_ref,
    sems,
):
    rows, cols = target_ref.shape
    half = cols // 2
    fr = psi_ref.shape[0]
    load_psi = pltpu.make_async_copy(psi_hbm, psi_ref, sems.at[0])
    load_kernels = pltpu.make_async_copy(kernels_hbm, kernels_ref, sems.at[1])
    load_target = pltpu.make_async_copy(target_hbm, target_ref, sems.at[2])
    load_psi.start()
    load_kernels.start()
    load_target.start()
    window = rows + 2 * MARGIN
    bf = jnp.bfloat16
    across = freq_ref[0:1, :]
    down = freq_ref[...].T[: 2 * fr, :1]

    inner_ref[...] = interleaved(down, (2 * fr, 2 * rows), 0, fr, MARGIN, window).astype(bf)
    table = interleaved(across, (2 * rows, LANES), 1, fr, MARGIN, window)
    inner_t_ref[...] = table[:, : 2 * fr].astype(bf)

    load_psi.wait()
    load_kernels.wait()
    kernels_at(defocus_ref, psi_ref, kernels_ref, k_re_ref, k_im_ref)

    load_target.wait()
    goal_ref[:, :half] = target_ref[:, :half].astype(jnp.float32)
    for b in range(half // LANES):
        goal_ref[:, half + b * LANES : half + (b + 1) * LANES] = mirrored(
            target_ref[:, cols - (b + 1) * LANES : cols - b * LANES].astype(jnp.float32)
        )


def third_kernel(
    strips,
    groups,
    freq_ref,
    phi_ref,
    from_a_ref,
    from_b_ref,
    part_ref,
    tall_ref,
    far_ref,
    slope_ref,
    halo_ref,
    halo_slope_ref,
):
    rows, cols = phi_ref.shape
    fr, fc = part_ref.shape[0] // 2, part_ref.shape[1]
    window = rows + 2 * MARGIN
    bf = jnp.bfloat16
    place, first, second, first_in, second_in = partners(strips)
    across = freq_ref[0:1, :]

    tall = rows + 2 * PAD
    for index, (offset, keep) in enumerate(((0, True), (first, first_in), (second, second_in))):
        table, spot = rotation(
            across, (2 * tall, LANES), tall, 1, fr, MARGIN - PAD - offset * rows, window
        )
        keep = keep & (spot >= 0) & (spot < window)
        tall_ref[index] = jnp.where(keep, table, 0.0)[:, : 2 * fr].astype(bf)
    shape = (4 * HALO, LANES)
    index = lax.broadcasted_iota(jnp.int32, shape, 0)
    imag_row = index >= 2 * HALO
    index = jnp.where(imag_row, index - 2 * HALO, index)
    low = index >= HALO
    row = jnp.where(low, index + (rows - HALO), index - HALO)
    imag = lax.broadcasted_iota(jnp.int32, shape, 1) >= fr
    for group, offsets in enumerate(groups.values()):
        total = jnp.zeros(shape, jnp.float32)
        for offset in offsets:
            spot = row - offset * rows + MARGIN
            keep = (spot >= 0) & (spot < window) & (low if offset > 0 else ~low)
            keep = keep & (place - offset >= 0) & (place - offset < strips)
            c, s = turn(across * spot.astype(jnp.float32), float(window))
            total = total + jnp.where(keep, quarter(imag_row, imag, c, s), 0.0)
        far_ref[group] = total[:, : 2 * fr].astype(bf)

    scale = 1.0 / float(window * cols) ** 0.5
    mask = jnp.tanh(phi_ref[...])
    slope_ref[...] = (step_size * scale) * (1.0 - mask * mask)

    halo_ref[...] = jnp.zeros_like(halo_ref)
    edges_a = from_a_ref[2 * fr :].astype(jnp.float32)
    edges_b = from_b_ref[2 * fr :].astype(jnp.float32)
    top_in = (place > 0).astype(jnp.float32)
    low_in = (place < strips - 1).astype(jnp.float32)
    above = jnp.where(first < 0, edges_a, edges_b) * top_in
    below = jnp.where(first < 0, edges_b, edges_a) * low_in
    per_row = cols // fc
    for i in range(HALO):
        for q in range(per_row):
            here = slice(q * fc, (q + 1) * fc)
            spot = i * per_row + q
            halo_ref[PAD - HALO + i : PAD - HALO + i + 1, here] = above[spot : spot + 1]
            halo_ref[PAD + i : PAD + i + 1, here] = below[spot : spot + 1]
    for edge, inside in ((0, top_in), (PAD, low_in)):
        mask = jnp.tanh(halo_ref[edge : edge + PAD])
        halo_slope_ref[edge : edge + PAD] = (step_size * scale) * inside * (1.0 - mask * mask)


def own_kernel(tall_ref, y_ref, z_ref):
    z_ref[...] = dot(tall_ref[0], y_ref[...])


def main_kernel(
    own_ref,
    from_a_ref,
    from_b_ref,
    goal_ref,
    table_ref,
    inner_ref,
    inner_t_ref,
    k_re_ref,
    k_im_ref,
    *rest,
):
    rows, cols = goal_ref.shape
    half = cols // 2
    count, fr, _ = k_re_ref.shape
    scale = 1.0 / float((rows + 2 * MARGIN) * cols) ** 0.5
    bf = jnp.bfloat16
    f32 = jnp.float32
    if len(rest) == 3:
        out_ref, q_ref, x_ref = rest
        planes = [(k_re_ref, k_im_ref, q_ref, x_ref)]
    else:
        other_ref, psi_ref, kernels_ref, out_ref = rest[:4]
        q_ref, x_ref, q2_ref, x2_ref, k2_re_ref, k2_im_ref = rest[4:]
        kernels_at(other_ref, psi_ref, kernels_ref, k2_re_ref, k2_im_ref)
        planes = [(k_re_ref, k_im_ref, q_ref, x_ref), (k2_re_ref, k2_im_ref, q2_ref, x2_ref)]

    spec = scale * (
        own_ref[...] + from_a_ref[: 2 * fr].astype(f32) + from_b_ref[: 2 * fr].astype(f32)
    )
    s_re, s_im = spec[:fr], spec[fr:]
    unit = 16 * count
    gain = 4.0 * slope_resist / count * scale
    norm = scale * scale / count
    width = min(CHUNK, half)

    def weight(intensity, goal):
        resist = jax.nn.sigmoid(slope_resist * (norm * intensity - level_resist))
        return gain * (resist - goal) * resist * (1.0 - resist)

    def fields(k_re_ref, k_im_ref, q_ref):
        for k in range(count):
            k_re, k_im = k_re_ref[k], k_im_ref[k]
            g = jnp.concatenate([k_re * s_re - k_im * s_im, k_re * s_im + k_im * s_re], axis=0)
            q = dot(inner_t_ref[...], g.astype(bf)).astype(bf)
            for r in range(rows // 8):
                q_ref[r * unit + 16 * k : r * unit + 16 * k + 16] = q[16 * r : 16 * r + 16]

    def weighted(q_ref, x_ref, start):
        left_half = slice(start, start + width)
        right_half = slice(half + start, half + start + width)
        af = dot(q_ref[...], table_ref[:, left_half])
        db = dot(q_ref[...], table_ref[:, right_half])
        for r in range(rows // 8):

            def parts(k):
                at = r * unit + 16 * k
                return af[at : at + 8], db[at + 8 : at + 16], af[at + 8 : at + 16], db[at : at + 8]

            even = 0.0
            cross = 0.0
            for k in range(count):
                a, b, f, d = parts(k)
                even = even + ((a * a + f * f) + (d * d + b * b))
                cross = cross + (a * b - d * f)
            cross = 2.0 * cross
            here = slice(8 * r, 8 * r + 8)
            w_left = weight(even - cross, goal_ref[here, left_half])
            w_right = weight(even + cross, goal_ref[here, right_half])
            p_w = w_left + w_right
            q_w = w_right - w_left
            for k in range(count):
                a, b, f, d = parts(k)
                at = slice(r * unit + 16 * k, r * unit + 16 * k + 16)
                x_ref[at, left_half] = jnp.concatenate(
                    [p_w * a + q_w * b, p_w * f - q_w * d], axis=0
                ).astype(bf)
                x_ref[at, right_half] = jnp.concatenate(
                    [p_w * d - q_w * f, q_w * a + p_w * b], axis=0
                ).astype(bf)

    def adjoint(k_re_ref, k_im_ref, q_ref, x_ref):
        q_ref[...] = dot_t(x_ref[...], table_ref[...]).astype(bf)
        y_re = 0.0
        y_im = 0.0
        for k in range(count):
            u = jnp.concatenate(
                [q_ref[r * unit + 16 * k : r * unit + 16 * k + 16] for r in range(rows // 8)],
                axis=0,
            )
            w = scale * dot(inner_ref[...], u)
            w_re, w_im = w[:fr], w[fr:]
            k_re, k_im = k_re_ref[k], k_im_ref[k]
            y_re = y_re + (k_re * w_re + k_im * w_im)
            y_im = y_im + (k_re * w_im - k_im * w_re)
        return y_re, y_im

    for k_re_ref, k_im_ref, q_ref, x_ref in planes:
        fields(k_re_ref, k_im_ref, q_ref)
    for _, _, q_ref, x_ref in planes:
        for start in range(0, half, width):
            weighted(q_ref, x_ref, start)
    y_re = 0.0
    y_im = 0.0
    for plane in planes:
        part_re, part_im = adjoint(*plane)
        y_re = y_re + part_re
        y_im = y_im + part_im
    out_ref[:fr] = y_re.astype(bf)
    out_ref[fr:] = y_im.astype(bf)


def sum_kernel(part_ref, other_ref, far_ref, total_ref, *payload_refs):
    total = part_ref[...].astype(jnp.float32) + other_ref[...].astype(jnp.float32)
    total = total.astype(jnp.bfloat16)
    total_ref[...] = total
    for index, payload_ref in enumerate(payload_refs):
        payload_ref[...] = dot(far_ref[index], total).astype(jnp.bfloat16)


def final_kernel(
    strips,
    phi_ref,
    slope_ref,
    halo_ref,
    halo_slope_ref,
    table_ref,
    tall_ref,
    z_own_ref,
    y_a_ref,
    y_b_ref,
    *rest,
):
    payload_refs = rest[:-9]
    out_hbm, out_ref, sems = rest[-9:-6]
    level_ref, level_across, level_both, next_ref, next_across, next_both = rest[-6:]
    place, _, _, _, _ = partners(strips)
    rows, cols = phi_ref.shape
    half = cols // 2
    blocks = cols // LANES
    tall = rows + 2 * PAD
    bf = jnp.bfloat16
    f32 = jnp.float32

    z = z_own_ref[...] + dot(tall_ref[1], y_a_ref[...]) + dot(tall_ref[2], y_b_ref[...])
    if payload_refs:
        down = lax.broadcasted_iota(jnp.int32, (2 * tall, 4 * HALO), 0)
        index = lax.broadcasted_iota(jnp.int32, (2 * tall, 4 * HALO), 1)
        imag = index >= 2 * HALO
        index = jnp.where(imag, index - 2 * HALO, index)
        goes = jnp.where(index < HALO, index + (PAD - HALO), index + (PAD + rows - HALO))
        goes = jnp.where(imag, goes + tall, goes)
        place_rows = jnp.where(down == goes, 1.0, 0.0).astype(bf)
        for payload_ref in payload_refs:
            z = z + dot(place_rows, payload_ref[...])
    z = z.astype(bf)
    even = dot(z[:tall], table_ref[:, :half])
    odd = dot(z[tall:], table_ref[:, half:])

    top_in = place > 0
    low_in = place < strips - 1

    def advance(b, grad):
        here = slice(b * LANES, (b + 1) * LANES)
        level_ref[b, PAD : PAD + rows] = phi_ref[:, here] - slope_ref[:, here] * grad[
            PAD : PAD + rows
        ]
        for edge, to in ((0, 0), (PAD, PAD + rows)):
            step = halo_slope_ref[edge : edge + PAD, here] * grad[to : to + PAD]
            level_ref[b, to : to + PAD] = halo_ref[edge : edge + PAD, here] - step

    for b in range(half // LANES):
        part = slice(b * LANES, (b + 1) * LANES)
        advance(b, even[:, part] - odd[:, part])
        advance(blocks - 1 - b, mirrored(even[:, part] + odd[:, part]))

    lane = lax.broadcasted_iota(jnp.int32, (8, LANES), 1)
    nothing = jnp.zeros((8, LANES), f32)

    def beside(values):
        ahead = [pltpu.roll(value, LANES - 1, 1) for value in values] + [nothing]
        behind = [nothing] + [pltpu.roll(value, 1, 1) for value in values]
        for b in range(len(values)):
            right = jnp.where(lane == LANES - 1, ahead[b + 1], ahead[b])
            left = jnp.where(lane == 0, behind[b], behind[b + 1])
            yield right - left, right + left

    def sweep(refs, at, b):
        source, across_ref, both_ref = refs
        here = slice(at, at + 8)
        c = source[b, here]
        up, down = source[b, at + 1 : at + 9], source[b, at - 1 : at + 7]
        y = across_ref[b, here]
        crossed = across_ref[b, at + 1 : at + 9] - across_ref[b, at - 1 : at + 7]
        twice = c + c
        x = up - down
        second_x = (up + down) - twice
        second_y = both_ref[b, here] - twice
        x_x = x * x
        y_y = y * y
        numer = second_x * y_y + second_y * x_x - (0.5 * x) * y * crossed
        return c + flow_rate * (numer / (4.0 + x_x + y_y))

    levels = (level_ref, level_across, level_both)
    nexts = (next_ref, next_across, next_both)

    def fill(refs, at, values):
        for b, (difference, total) in enumerate(beside(values)):
            refs[1][b, at : at + 8] = difference
            refs[2][b, at : at + 8] = total

    def cover(first_row, end):
        starts = list(range(first_row, end - 7, 8))
        return starts if starts[-1] + 8 >= end else starts + [end - 8]

    for at in cover(PAD - 2, PAD + rows + 2):
        fill(levels, at, [level_ref[b, at : at + 8] for b in range(blocks)])
    for at in cover(PAD - 1, PAD + rows + 1):
        values = [sweep(levels, at, b) for b in range(blocks)]
        if at < PAD or at + 8 > PAD + rows:
            spot = lax.broadcasted_iota(jnp.int32, (8, LANES), 0) + at
            keep = ((spot >= PAD) | top_in) & ((spot < PAD + rows) | low_in)
            values = [jnp.where(keep, value, 0.0) for value in values]
        for b in range(blocks):
            next_ref[b, at : at + 8] = values[b]
        fill(nexts, at, values)
    copies = []
    for index in range(rows // 8):
        here = slice(8 * index, 8 * index + 8)
        for b in range(blocks):
            out_ref[here, b * LANES : (b + 1) * LANES] = sweep(nexts, PAD + 8 * index, b)
        here = pl.ds(8 * index, 8)
        copies.append(pltpu.make_async_copy(out_ref.at[here], out_hbm.at[here], sems.at[index]))
        copies[-1].start()
    for copy in copies:
        copy.wait()


def spec(kind):
    return pl.BlockSpec(memory_space={"v": pltpu.VMEM, "s": pltpu.SMEM, "h": pltpu.HBM}[kind])


def call(kernel, outs, args, kinds=None, out_kinds=None, scratch=(), limit=24, flops=1000000):
    kinds = kinds or "v" * len(args)
    out_kinds = out_kinds or "v" * len(outs)
    args = [
        pltpu.with_memory_space_constraint(arg, pltpu.HBM) if kind == "h" else arg
        for kind, arg in zip(kinds, args)
    ]
    return pl.pallas_call(
        kernel,
        out_shape=outs,
        in_specs=[spec(kind) for kind in kinds],
        out_specs=[spec(kind) for kind in out_kinds],
        scratch_shapes=list(scratch),
        compiler_params=pltpu.CompilerParams(vmem_limit_bytes=limit << 20),
        cost_estimate=pl.CostEstimate(flops=flops, bytes_accessed=4 << 20, transcendentals=0),
    )(*args)


def pair_up(block, first):
    strips, planes = lax.axis_size("strip"), lax.axis_size("focus")
    moves = []
    for strip in range(strips):
        up = (strip % 2 == 0) == first
        partner = strip + 1 if up else strip - 1
        for plane in range(planes):
            here = strip * planes + plane
            if 0 <= partner < strips:
                moves.append((here, partner * planes + plane))
            else:
                moves.append((here, strip * planes + (plane ^ 1 if planes > 1 else plane)))
    return lax.ppermute(block, ("strip", "focus"), moves)


def on_device(phi, target, defocus_ids, kernels, psi, row_freqs, col_freqs):
    rows, cols = phi.shape
    fr, fc = psi.shape
    count = kernels.shape[1]
    strips = lax.axis_size("strip")
    planes = lax.axis_size("focus")
    groups = offset_groups(rows, strips)
    tall = rows + 2 * PAD
    bf = jnp.bfloat16
    f32 = jnp.float32
    shape = jax.ShapeDtypeStruct
    packet = shape((2 * fr + HALO * (cols // fc), fc), bf)
    row_freqs = row_freqs.reshape(1, fr)

    table, s_own, send_a, send_b, phi, freqs = call(
        functools.partial(first_kernel, strips),
        [
            shape((fc, cols), bf),
            shape((2 * fr, fc), f32),
            packet,
            packet,
            shape((rows, cols), f32),
            shape((8, LANES), f32),
        ],
        (phi, row_freqs, col_freqs.reshape(1, fc)),
        kinds="hhh",
        scratch=[
            pltpu.VMEM((rows, cols), bf),
            pltpu.VMEM((1, fr), jnp.int32),
            pltpu.VMEM((1, fc), jnp.int32),
            pltpu.SemaphoreType.DMA((3,)),
        ],
    )
    (defocus,) = call(
        defocus_kernel, [shape((8, LANES), f32)], (defocus_ids, freqs), kinds="sv"
    )
    paired = planes > 1
    from_b = pair_up(send_b, False)
    from_a = pair_up(send_a, True)
    if paired:
        swap = [(i, i ^ (planes // 2)) for i in range(planes)]
        other_defocus = lax.ppermute(defocus, "focus", swap)
    inner, inner_t, k_re, k_im, goal, kernels_v, psi_v = call(
        second_kernel,
        [
            shape((2 * fr, 2 * rows), bf),
            shape((2 * rows, 2 * fr), bf),
            shape((count, fr, fc), f32),
            shape((count, fr, fc), f32),
            shape((rows, cols), f32),
            shape(kernels.shape, f32),
            shape(psi.shape, f32),
        ],
        (defocus, freqs, kernels, psi, target),
        kinds="vvhhh",
        scratch=[
            pltpu.VMEM(target.shape, jnp.int32),
            pltpu.SemaphoreType.DMA((3,)),
        ],
        flops=4000000000,
    )
    scratch = [
        pltpu.VMEM((count * 2 * rows, fc), bf),
        pltpu.VMEM((count * 2 * rows, cols), bf),
    ]
    (part,) = call(
        main_kernel,
        [shape((2 * fr, fc), bf)],
        (s_own, from_a, from_b, goal, table, inner, inner_t, k_re, k_im)
        + ((other_defocus, psi_v, kernels_v) if paired else ()),
        scratch=scratch * 2 + [pltpu.VMEM((count, fr, fc), f32)] * 2 if paired else scratch,
        limit=40,
        flops=4000000000,
    )
    tall_t, far_t, slope, halo, halo_slope = call(
        functools.partial(third_kernel, strips, groups),
        [
            shape((3, 2 * tall, 2 * fr), bf),
            shape((max(1, len(groups)), 4 * HALO, 2 * fr), bf),
            shape((rows, cols), f32),
            shape((2 * PAD, cols), f32),
            shape((2 * PAD, cols), f32),
        ],
        (freqs, phi, from_a, from_b, part),
        flops=2000000000,
    )
    step = 1
    other = jnp.zeros_like(part)
    while step < planes // 2:
        if step > 1:
            part = lax.optimization_barrier(
                (part.astype(f32) + other.astype(f32)).astype(bf)
            )
        other = lax.ppermute(part, "focus", [(i, i ^ step) for i in range(planes)])
        step *= 2
    total, *payloads = call(
        sum_kernel,
        [shape((2 * fr, fc), bf)] + [shape((4 * HALO, fc), bf)] * len(groups),
        (part, other, far_t),
    )
    far = [
        lax.ppermute(payload, "strip", [(i, (i - turn_by) % strips) for i in range(strips)])
        for turn_by, payload in zip(groups, payloads)
    ]
    y_b = pair_up(total, False)
    y_a = pair_up(total, True)
    (z_own,) = call(own_kernel, [shape((2 * tall, fc), f32)], (tall_t, total), flops=2000000000)
    return call(
        functools.partial(final_kernel, strips),
        [shape((rows, cols), f32)],
        (phi, slope, halo, halo_slope, table, tall_t, z_own, y_a, y_b, *far),
        out_kinds="h",
        scratch=[
            pltpu.VMEM((rows, cols), f32),
            pltpu.SemaphoreType.DMA((rows // 8,)),
        ]
        + [pltpu.VMEM((cols // LANES, tall, LANES), f32)] * 6,
    )[0]


def solution(mesh):
    return jax.shard_map(
        on_device,
        mesh=mesh,
        in_specs=(
            P(("tile", "strip"), None),
            P(("tile", "strip"), None),
            P(("tile", "focus")),
            P(),
            P(),
            P(),
            P(),
        ),
        out_specs=P(("tile", "strip"), None),
        check_vma=False,
    )
```

```python
import functools

import jax
import jax.numpy as jnp
from jax import lax
from jax.experimental import pallas as pl
from jax.experimental.pallas import tpu as pltpu
from jax.sharding import PartitionSpec as P

MARGIN = 64
LEVELS = 31
SWEEPS = 2
HALO = SWEEPS
LANES = 128
PAD = 8
CHUNK = 256
GROUPS = (4, 4)

slope_resist = 4.0
level_resist = 0.5
step_size = 1.0
flow_rate = 0.2

SIN_TERMS = (3.1415926401307073, -5.167710083507878, 2.550077523214199, -0.5982912856179897, 0.07765766030124945)
COS_TERMS = (0.9999999532476078, -4.934792830619626, 4.0584113528622625, -1.3318765680789622, 0.2196896110945085)


def cos_sin(t):
    square = t * t
    s = SIN_TERMS[-1] * square + SIN_TERMS[-2]
    for term in SIN_TERMS[-3::-1]:
        s = s * square + term
    s = s * t
    c = COS_TERMS[-1] * square + COS_TERMS[-2]
    for term in COS_TERMS[-3::-1]:
        c = c * square + term
    twice = s + s
    return 1.0 - twice * s, twice * c


def turn(product, period):
    if float(period).is_integer() and int(period) & (int(period) - 1) == 0:
        t = product * (1.0 / period)
        return cos_sin(t - jnp.round(t))
    rest = product - jnp.round(product * (1.0 / period)) * period
    return cos_sin(rest * (1.0 / period))


def mirrored(block):
    spots = (LANES - 1) - lax.broadcasted_iota(jnp.int32, block.shape, 1)
    return jnp.take_along_axis(block, spots, axis=1, mode="promise_in_bounds")


def dot(lhs_mat, rhs_mat):
    return jnp.dot(lhs_mat, rhs_mat, preferred_element_type=jnp.float32)


def dot_t(lhs_mat, rhs_mat):
    return lax.dot_general(
        lhs_mat, rhs_mat, (((1,), (1,)), ((), ())), preferred_element_type=jnp.float32
    )


def offset_groups(rows, strips):
    reach = (MARGIN + HALO + rows - 1) // rows
    groups = {}
    for offset in range(-reach, reach + 1):
        if abs(offset) > 1:
            groups.setdefault(offset % strips, []).append(offset)
    return groups


def partners(strips):
    place = lax.axis_index("strip")
    first = jnp.where(place % 2 == 0, 1, -1)
    second = -first

    def inside(offset):
        return (place + offset >= 0) & (place + offset < strips)

    return place, first, second, inside(first), inside(second)


def quarter(second, imag, c, s):
    return jnp.where(second == imag, c, jnp.where(second, s, -s))


def rotation(freqs, shape, length, freq_dim, fr, start, period):
    spot = lax.broadcasted_iota(jnp.int32, shape, 1 - freq_dim)
    second = spot >= length
    spot = jnp.where(second, spot - length, spot) + start
    imag = lax.broadcasted_iota(jnp.int32, shape, freq_dim) >= fr
    c, s = turn(freqs * spot.astype(jnp.float32), float(period))
    return quarter(second, imag, c, s), spot


def interleaved(freqs, shape, freq_dim, fr, start, period):
    index = lax.broadcasted_iota(jnp.int32, shape, 1 - freq_dim)
    spot = ((index >> 4) << 3) + (index & 7) + start
    second = (index & 8) > 0
    imag = lax.broadcasted_iota(jnp.int32, shape, freq_dim) >= fr
    c, s = turn(freqs * spot.astype(jnp.float32), float(period))
    return quarter(second, imag, c, s)


def row_freq_lanes(row_freqs_ref, freq_ref):
    fr = row_freqs_ref.shape[1]
    freqs = jnp.broadcast_to(row_freqs_ref[...].astype(jnp.float32), (8, fr))
    freq_ref[...] = jnp.zeros_like(freq_ref)
    freq_ref[:, 0:fr] = freqs
    freq_ref[:, fr : 2 * fr] = freqs


def first_kernel(
    strips,
    phi_hbm,
    row_freqs_hbm,
    col_freqs_hbm,
    table_ref,
    own_ref,
    send_a_ref,
    send_b_ref,
    phi_ref,
    freq_ref,
    mask_ref,
    row_freqs_ref,
    col_freqs_ref,
    sems,
):
    rows, cols = phi_ref.shape
    half = cols // 2
    fr, fc = row_freqs_ref.shape[1], table_ref.shape[0]
    window = rows + 2 * MARGIN
    bf = jnp.bfloat16
    load_cols = pltpu.make_async_copy(col_freqs_hbm, col_freqs_ref, sems.at[0])
    load_rows = pltpu.make_async_copy(row_freqs_hbm, row_freqs_ref, sems.at[1])
    load_phi = pltpu.make_async_copy(phi_hbm, phi_ref, sems.at[2])
    load_cols.start()
    load_rows.start()
    load_phi.start()
    _, first, second, first_in, second_in = partners(strips)

    load_cols.wait()
    load_rows.wait()
    row_freq_lanes(row_freqs_ref, freq_ref)
    down = freq_ref[...].T[:fr, :1]
    spot = lax.broadcasted_iota(jnp.int32, (fr, 2 * rows), 1)
    later = spot >= rows
    spot = jnp.where(later, spot - rows, spot)
    c, s = turn(down * (spot + MARGIN).astype(jnp.float32), float(window))
    turn_c, turn_s = turn(jnp.broadcast_to(down, c.shape) * float(rows), float(window))

    def rows_in(c, s, offset, keep):
        at = spot + MARGIN - offset * rows
        keep = keep & (at >= 0) & (at < window)
        c = jnp.where(keep, c, 0.0)
        s = jnp.where(keep, s, 0.0)
        return jnp.concatenate([jnp.where(later, s, c), jnp.where(later, c, -s)], axis=0).astype(bf)

    sign = -first.astype(jnp.float32)
    turn_s = sign * turn_s
    in_all = jnp.concatenate(
        [
            rows_in(c * turn_c + s * turn_s, s * turn_c - c * turn_s, second, second_in),
            rows_in(c * turn_c - s * turn_s, s * turn_c + c * turn_s, first, first_in),
            rows_in(c, s, 0, True),
        ],
        axis=0,
    )

    freq_row = jnp.broadcast_to(col_freqs_ref[...].astype(jnp.float32), (8, fc))
    step_row_c, step_row_s = turn(freq_row * float(LANES), float(cols))
    kind = lax.broadcasted_iota(jnp.int32, (8, fc), 0)
    packed = jnp.where(kind == 0, freq_row, jnp.where(kind == 1, step_row_c, step_row_s)).T

    def make_columns(start, number):
        f = packed[start : start + number, 0:1]
        spot = lax.broadcasted_iota(jnp.int32, (number, LANES), 1).astype(jnp.float32)
        c, s = turn(f * (2.0 * spot + 1.0), 2.0 * cols)
        step_c = jnp.broadcast_to(packed[start : start + number, 1:2], (number, LANES))
        step_s = jnp.broadcast_to(packed[start : start + number, 2:3], (number, LANES))
        twice = 2.0 * step_c
        c_old, s_old = c, s
        here = slice(start, start + number)
        for b in range(half // LANES):
            if b == 1:
                c, s = c * step_c - s * step_s, s * step_c + c * step_s
            elif b:
                c, s, c_old, s_old = twice * c - c_old, twice * s - s_old, c, s
            table_ref[here, b * LANES : (b + 1) * LANES] = c.astype(bf)
            table_ref[here, half + b * LANES : half + (b + 1) * LANES] = s.astype(bf)

    def transform(start, number):
        here = slice(start, start + number)
        p_re = dot_t(mask_ref[:, :half], table_ref[here, :half])
        p_im = -dot_t(mask_ref[:, half:], table_ref[here, half:])
        spec = dot(in_all, jnp.concatenate([p_re, p_im], axis=0).astype(bf))
        send_b_ref[: 2 * fr, here] = spec[: 2 * fr].astype(bf)
        send_a_ref[: 2 * fr, here] = spec[2 * fr : 4 * fr].astype(bf)
        own_ref[:, here] = spec[4 * fr :]

    piece = 64
    start = 0
    for share in GROUPS:
        group = fc * share // 8
        for part in range(start, start + group, piece):
            make_columns(part, piece)
        if start == 0:
            load_phi.wait()
            for b in range(half // LANES):
                left = jnp.tanh(phi_ref[:, b * LANES : (b + 1) * LANES])
                right = mirrored(jnp.tanh(phi_ref[:, cols - (b + 1) * LANES : cols - b * LANES]))
                mask_ref[:, b * LANES : (b + 1) * LANES] = (left + right).astype(bf)
                mask_ref[:, half + b * LANES : half + (b + 1) * LANES] = (left - right).astype(bf)
        transform(start, group)
        start += group
    tops = [phi_ref[i : i + 1, q : q + fc] for i in range(HALO) for q in range(0, cols, fc)]
    lows = [
        phi_ref[rows - HALO + i : rows - HALO + i + 1, q : q + fc]
        for i in range(HALO)
        for q in range(0, cols, fc)
    ]
    tops = jnp.concatenate(tops, axis=0)
    lows = jnp.concatenate(lows, axis=0)
    send_a_ref[2 * fr :] = jnp.where(first > 0, lows, tops).astype(bf)
    send_b_ref[2 * fr :] = jnp.where(second > 0, lows, tops).astype(bf)


def defocus_kernel(defocus_ref, after_ref, out_ref):
    middle = (LEVELS - 1) / 2.0
    defocus = (defocus_ref[0].astype(jnp.float32) - middle) * (1.0 / middle)
    out_ref[...] = jnp.full(out_ref.shape, defocus, jnp.float32)


def kernels_at(defocus_ref, psi_ref, kernels_ref, k_re_ref, k_im_ref):
    cycles = psi_ref[...] * (defocus_ref[0:1, 0:1] * (0.5 / jnp.pi))
    turn_c, turn_s = cos_sin(cycles)
    for k in range(kernels_ref.shape[1]):
        k_re_ref[k] = kernels_ref[0, k] * turn_c - kernels_ref[1, k] * turn_s
        k_im_ref[k] = kernels_ref[0, k] * turn_s + kernels_ref[1, k] * turn_c


def second_kernel(
    defocus_ref,
    freq_ref,
    kernels_hbm,
    psi_hbm,
    target_hbm,
    inner_ref,
    inner_t_ref,
    k_re_ref,
    k_im_ref,
    goal_ref,
    kernels_ref,
    psi_ref,
    target_ref,
    sems,
):
    rows, cols = target_ref.shape
    half = cols // 2
    fr = psi_ref.shape[0]
    load_psi = pltpu.make_async_copy(psi_hbm, psi_ref, sems.at[0])
    load_kernels = pltpu.make_async_copy(kernels_hbm, kernels_ref, sems.at[1])
    load_target = pltpu.make_async_copy(target_hbm, target_ref, sems.at[2])
    load_psi.start()
    load_kernels.start()
    load_target.start()
    window = rows + 2 * MARGIN
    bf = jnp.bfloat16
    across = freq_ref[0:1, :]
    down = freq_ref[...].T[: 2 * fr, :1]

    inner_ref[...] = interleaved(down, (2 * fr, 2 * rows), 0, fr, MARGIN, window).astype(bf)
    table = interleaved(across, (2 * rows, LANES), 1, fr, MARGIN, window)
    inner_t_ref[...] = table[:, : 2 * fr].astype(bf)

    load_psi.wait()
    load_kernels.wait()
    kernels_at(defocus_ref, psi_ref, kernels_ref, k_re_ref, k_im_ref)

    load_target.wait()
    goal_ref[:, :half] = target_ref[:, :half].astype(jnp.float32)
    for b in range(half // LANES):
        goal_ref[:, half + b * LANES : half + (b + 1) * LANES] = mirrored(
            target_ref[:, cols - (b + 1) * LANES : cols - b * LANES].astype(jnp.float32)
        )


def third_kernel(
    strips,
    groups,
    freq_ref,
    phi_ref,
    from_a_ref,
    from_b_ref,
    part_ref,
    tall_ref,
    far_ref,
    slope_ref,
    halo_ref,
    halo_slope_ref,
):
    rows, cols = phi_ref.shape
    fr, fc = part_ref.shape[0] // 2, part_ref.shape[1]
    window = rows + 2 * MARGIN
    bf = jnp.bfloat16
    place, first, second, first_in, second_in = partners(strips)
    across = freq_ref[0:1, :]

    tall = rows + 2 * PAD
    for index, (offset, keep) in enumerate(((0, True), (first, first_in), (second, second_in))):
        table, spot = rotation(
            across, (2 * tall, LANES), tall, 1, fr, MARGIN - PAD - offset * rows, window
        )
        keep = keep & (spot >= 0) & (spot < window)
        tall_ref[index] = jnp.where(keep, table, 0.0)[:, : 2 * fr].astype(bf)
    shape = (4 * HALO, LANES)
    index = lax.broadcasted_iota(jnp.int32, shape, 0)
    imag_row = index >= 2 * HALO
    index = jnp.where(imag_row, index - 2 * HALO, index)
    low = index >= HALO
    row = jnp.where(low, index + (rows - HALO), index - HALO)
    imag = lax.broadcasted_iota(jnp.int32, shape, 1) >= fr
    for group, offsets in enumerate(groups.values()):
        total = jnp.zeros(shape, jnp.float32)
        for offset in offsets:
            spot = row - offset * rows + MARGIN
            keep = (spot >= 0) & (spot < window) & (low if offset > 0 else ~low)
            keep = keep & (place - offset >= 0) & (place - offset < strips)
            c, s = turn(across * spot.astype(jnp.float32), float(window))
            total = total + jnp.where(keep, quarter(imag_row, imag, c, s), 0.0)
        far_ref[group] = total[:, : 2 * fr].astype(bf)

    scale = 1.0 / float(window * cols) ** 0.5
    mask = jnp.tanh(phi_ref[...])
    slope_ref[...] = (step_size * scale) * (1.0 - mask * mask)

    halo_ref[...] = jnp.zeros_like(halo_ref)
    edges_a = from_a_ref[2 * fr :].astype(jnp.float32)
    edges_b = from_b_ref[2 * fr :].astype(jnp.float32)
    top_in = (place > 0).astype(jnp.float32)
    low_in = (place < strips - 1).astype(jnp.float32)
    above = jnp.where(first < 0, edges_a, edges_b) * top_in
    below = jnp.where(first < 0, edges_b, edges_a) * low_in
    per_row = cols // fc
    for i in range(HALO):
        for q in range(per_row):
            here = slice(q * fc, (q + 1) * fc)
            spot = i * per_row + q
            halo_ref[PAD - HALO + i : PAD - HALO + i + 1, here] = above[spot : spot + 1]
            halo_ref[PAD + i : PAD + i + 1, here] = below[spot : spot + 1]
    for edge, inside in ((0, top_in), (PAD, low_in)):
        mask = jnp.tanh(halo_ref[edge : edge + PAD])
        halo_slope_ref[edge : edge + PAD] = (step_size * scale) * inside * (1.0 - mask * mask)


def own_kernel(tall_ref, y_ref, z_ref):
    z_ref[...] = dot(tall_ref[0], y_ref[...])


def main_kernel(
    own_ref,
    from_a_ref,
    from_b_ref,
    goal_ref,
    table_ref,
    inner_ref,
    inner_t_ref,
    *rest,
):
    rows, cols = goal_ref.shape
    half = cols // 2
    if len(rest) == 5:
        base_refs, (k_re_ref, k_im_ref, out_ref, q_ref, x_ref) = (), rest
    else:
        base_refs, (defocus_ref, psi_ref, kernels_ref) = rest[:1], rest[1:4]
        out_ref, q_ref, x_ref, k_re_ref, k_im_ref = rest[4:]
        kernels_at(defocus_ref, psi_ref, kernels_ref, k_re_ref, k_im_ref)
    count, fr, _ = k_re_ref.shape
    scale = 1.0 / float((rows + 2 * MARGIN) * cols) ** 0.5
    bf = jnp.bfloat16
    f32 = jnp.float32

    spec = scale * (
        own_ref[...] + from_a_ref[: 2 * fr].astype(f32) + from_b_ref[: 2 * fr].astype(f32)
    )
    s_re, s_im = spec[:fr], spec[fr:]
    unit = 16 * count
    gain = 4.0 * slope_resist / count * scale
    norm = scale * scale / count
    width = min(CHUNK, half)

    def weight(intensity, goal):
        resist = jax.nn.sigmoid(slope_resist * (norm * intensity - level_resist))
        return gain * (resist - goal) * resist * (1.0 - resist)

    def fields(k_re_ref, k_im_ref, q_ref):
        for k in range(count):
            k_re, k_im = k_re_ref[k], k_im_ref[k]
            g = jnp.concatenate([k_re * s_re - k_im * s_im, k_re * s_im + k_im * s_re], axis=0)
            q = dot(inner_t_ref[...], g.astype(bf)).astype(bf)
            for r in range(rows // 8):
                q_ref[r * unit + 16 * k : r * unit + 16 * k + 16] = q[16 * r : 16 * r + 16]

    def weighted(q_ref, x_ref, start):
        left_half = slice(start, start + width)
        right_half = slice(half + start, half + start + width)
        af = dot(q_ref[...], table_ref[:, left_half])
        db = dot(q_ref[...], table_ref[:, right_half])
        for r in range(rows // 8):

            def parts(k):
                at = r * unit + 16 * k
                return af[at : at + 8], db[at + 8 : at + 16], af[at + 8 : at + 16], db[at : at + 8]

            even = 0.0
            cross = 0.0
            for k in range(count):
                a, b, f, d = parts(k)
                even = even + ((a * a + f * f) + (d * d + b * b))
                cross = cross + (a * b - d * f)
            cross = 2.0 * cross
            here = slice(8 * r, 8 * r + 8)
            w_left = weight(even - cross, goal_ref[here, left_half])
            w_right = weight(even + cross, goal_ref[here, right_half])
            p_w = w_left + w_right
            q_w = w_right - w_left
            for k in range(count):
                a, b, f, d = parts(k)
                at = slice(r * unit + 16 * k, r * unit + 16 * k + 16)
                x_ref[at, left_half] = jnp.concatenate(
                    [p_w * a + q_w * b, p_w * f - q_w * d], axis=0
                ).astype(bf)
                x_ref[at, right_half] = jnp.concatenate(
                    [p_w * d - q_w * f, q_w * a + p_w * b], axis=0
                ).astype(bf)

    def adjoint(k_re_ref, k_im_ref, q_ref, x_ref):
        q_ref[...] = dot_t(x_ref[...], table_ref[...]).astype(bf)
        y_re = 0.0
        y_im = 0.0
        for k in range(count):
            u = jnp.concatenate(
                [q_ref[r * unit + 16 * k : r * unit + 16 * k + 16] for r in range(rows // 8)],
                axis=0,
            )
            w = scale * dot(inner_ref[...], u)
            w_re, w_im = w[:fr], w[fr:]
            k_re, k_im = k_re_ref[k], k_im_ref[k]
            y_re = y_re + (k_re * w_re + k_im * w_im)
            y_im = y_im + (k_re * w_im - k_im * w_re)
        return y_re, y_im

    fields(k_re_ref, k_im_ref, q_ref)
    for start in range(0, half, width):
        weighted(q_ref, x_ref, start)
    y_re, y_im = adjoint(k_re_ref, k_im_ref, q_ref, x_ref)
    for base_ref in base_refs:
        y_re = y_re + base_ref[:fr]
        y_im = y_im + base_ref[fr:]
    out_ref[:fr] = y_re.astype(out_ref.dtype)
    out_ref[fr:] = y_im.astype(out_ref.dtype)


def sum_kernel(part_ref, other_ref, far_ref, total_ref, *payload_refs):
    total = part_ref[...].astype(jnp.float32) + other_ref[...].astype(jnp.float32)
    total = total.astype(jnp.bfloat16)
    total_ref[...] = total
    for index, payload_ref in enumerate(payload_refs):
        payload_ref[...] = dot(far_ref[index], total).astype(jnp.bfloat16)


def final_kernel(
    strips,
    phi_ref,
    slope_ref,
    halo_ref,
    halo_slope_ref,
    table_ref,
    tall_ref,
    z_own_ref,
    y_a_ref,
    y_b_ref,
    *rest,
):
    payload_refs = rest[:-9]
    out_hbm, out_ref, sems = rest[-9:-6]
    level_ref, level_across, level_both, next_ref, next_across, next_both = rest[-6:]
    place, _, _, _, _ = partners(strips)
    rows, cols = phi_ref.shape
    half = cols // 2
    blocks = cols // LANES
    tall = rows + 2 * PAD
    bf = jnp.bfloat16
    f32 = jnp.float32

    z = z_own_ref[...] + dot(tall_ref[1], y_a_ref[...]) + dot(tall_ref[2], y_b_ref[...])
    if payload_refs:
        down = lax.broadcasted_iota(jnp.int32, (2 * tall, 4 * HALO), 0)
        index = lax.broadcasted_iota(jnp.int32, (2 * tall, 4 * HALO), 1)
        imag = index >= 2 * HALO
        index = jnp.where(imag, index - 2 * HALO, index)
        goes = jnp.where(index < HALO, index + (PAD - HALO), index + (PAD + rows - HALO))
        goes = jnp.where(imag, goes + tall, goes)
        place_rows = jnp.where(down == goes, 1.0, 0.0).astype(bf)
        for payload_ref in payload_refs:
            z = z + dot(place_rows, payload_ref[...])
    z = z.astype(bf)
    even = dot(z[:tall], table_ref[:, :half])
    odd = dot(z[tall:], table_ref[:, half:])

    top_in = place > 0
    low_in = place < strips - 1

    def advance(b, grad):
        here = slice(b * LANES, (b + 1) * LANES)
        level_ref[b, PAD : PAD + rows] = phi_ref[:, here] - slope_ref[:, here] * grad[
            PAD : PAD + rows
        ]
        for edge, to in ((0, 0), (PAD, PAD + rows)):
            step = halo_slope_ref[edge : edge + PAD, here] * grad[to : to + PAD]
            level_ref[b, to : to + PAD] = halo_ref[edge : edge + PAD, here] - step

    for b in range(half // LANES):
        part = slice(b * LANES, (b + 1) * LANES)
        advance(b, even[:, part] - odd[:, part])
        advance(blocks - 1 - b, mirrored(even[:, part] + odd[:, part]))

    lane = lax.broadcasted_iota(jnp.int32, (8, LANES), 1)
    nothing = jnp.zeros((8, LANES), f32)

    def beside(values):
        ahead = [pltpu.roll(value, LANES - 1, 1) for value in values] + [nothing]
        behind = [nothing] + [pltpu.roll(value, 1, 1) for value in values]
        for b in range(len(values)):
            right = jnp.where(lane == LANES - 1, ahead[b + 1], ahead[b])
            left = jnp.where(lane == 0, behind[b], behind[b + 1])
            yield right - left, right + left

    def sweep(refs, at, b):
        source, across_ref, both_ref = refs
        here = slice(at, at + 8)
        c = source[b, here]
        up, down = source[b, at + 1 : at + 9], source[b, at - 1 : at + 7]
        y = across_ref[b, here]
        crossed = across_ref[b, at + 1 : at + 9] - across_ref[b, at - 1 : at + 7]
        twice = c + c
        x = up - down
        second_x = (up + down) - twice
        second_y = both_ref[b, here] - twice
        x_x = x * x
        y_y = y * y
        numer = second_x * y_y + second_y * x_x - (0.5 * x) * y * crossed
        return c + flow_rate * (numer / (4.0 + x_x + y_y))

    levels = (level_ref, level_across, level_both)
    nexts = (next_ref, next_across, next_both)

    def fill(refs, at, values):
        for b, (difference, total) in enumerate(beside(values)):
            refs[1][b, at : at + 8] = difference
            refs[2][b, at : at + 8] = total

    def cover(first_row, end):
        starts = list(range(first_row, end - 7, 8))
        return starts if starts[-1] + 8 >= end else starts + [end - 8]

    for at in cover(PAD - 2, PAD + rows + 2):
        fill(levels, at, [level_ref[b, at : at + 8] for b in range(blocks)])
    for at in cover(PAD - 1, PAD + rows + 1):
        values = [sweep(levels, at, b) for b in range(blocks)]
        if at < PAD or at + 8 > PAD + rows:
            spot = lax.broadcasted_iota(jnp.int32, (8, LANES), 0) + at
            keep = ((spot >= PAD) | top_in) & ((spot < PAD + rows) | low_in)
            values = [jnp.where(keep, value, 0.0) for value in values]
        for b in range(blocks):
            next_ref[b, at : at + 8] = values[b]
        fill(nexts, at, values)
    copies = []
    for index in range(rows // 8):
        here = slice(8 * index, 8 * index + 8)
        for b in range(blocks):
            out_ref[here, b * LANES : (b + 1) * LANES] = sweep(nexts, PAD + 8 * index, b)
        here = pl.ds(8 * index, 8)
        copies.append(pltpu.make_async_copy(out_ref.at[here], out_hbm.at[here], sems.at[index]))
        copies[-1].start()
    for copy in copies:
        copy.wait()


def spec(kind):
    return pl.BlockSpec(memory_space={"v": pltpu.VMEM, "s": pltpu.SMEM, "h": pltpu.HBM}[kind])


def call(kernel, outs, args, kinds=None, out_kinds=None, scratch=(), limit=24, flops=1000000):
    kinds = kinds or "v" * len(args)
    out_kinds = out_kinds or "v" * len(outs)
    args = [
        pltpu.with_memory_space_constraint(arg, pltpu.HBM) if kind == "h" else arg
        for kind, arg in zip(kinds, args)
    ]
    return pl.pallas_call(
        kernel,
        out_shape=outs,
        in_specs=[spec(kind) for kind in kinds],
        out_specs=[spec(kind) for kind in out_kinds],
        scratch_shapes=list(scratch),
        compiler_params=pltpu.CompilerParams(vmem_limit_bytes=limit << 20),
        cost_estimate=pl.CostEstimate(flops=flops, bytes_accessed=4 << 20, transcendentals=0),
    )(*args)


def pair_up(block, first):
    strips, planes = lax.axis_size("strip"), lax.axis_size("focus")
    moves = []
    for strip in range(strips):
        up = (strip % 2 == 0) == first
        partner = strip + 1 if up else strip - 1
        for plane in range(planes):
            here = strip * planes + plane
            if 0 <= partner < strips:
                moves.append((here, partner * planes + plane))
            else:
                moves.append((here, strip * planes + (plane ^ 1 if planes > 1 else plane)))
    return lax.ppermute(block, ("strip", "focus"), moves)


def on_device(phi, target, defocus_ids, kernels, psi, row_freqs, col_freqs):
    rows, cols = phi.shape
    fr, fc = psi.shape
    count = kernels.shape[1]
    strips = lax.axis_size("strip")
    planes = lax.axis_size("focus")
    groups = offset_groups(rows, strips)
    tall = rows + 2 * PAD
    bf = jnp.bfloat16
    f32 = jnp.float32
    shape = jax.ShapeDtypeStruct
    packet = shape((2 * fr + HALO * (cols // fc), fc), bf)
    row_freqs = row_freqs.reshape(1, fr)

    table, s_own, send_a, send_b, phi, freqs = call(
        functools.partial(first_kernel, strips),
        [
            shape((fc, cols), bf),
            shape((2 * fr, fc), f32),
            packet,
            packet,
            shape((rows, cols), f32),
            shape((8, LANES), f32),
        ],
        (phi, row_freqs, col_freqs.reshape(1, fc)),
        kinds="hhh",
        scratch=[
            pltpu.VMEM((rows, cols), bf),
            pltpu.VMEM((1, fr), jnp.int32),
            pltpu.VMEM((1, fc), jnp.int32),
            pltpu.SemaphoreType.DMA((3,)),
        ],
    )
    (defocus,) = call(
        defocus_kernel, [shape((8, LANES), f32)], (defocus_ids, freqs), kinds="sv"
    )
    paired = planes > 1
    from_b = pair_up(send_b, False)
    from_a = pair_up(send_a, True)
    if paired:
        swap = [(i, i ^ (planes // 2)) for i in range(planes)]
        other_defocus = lax.ppermute(defocus, "focus", swap)
    inner, inner_t, k_re, k_im, goal, kernels_v, psi_v = call(
        second_kernel,
        [
            shape((2 * fr, 2 * rows), bf),
            shape((2 * rows, 2 * fr), bf),
            shape((count, fr, fc), f32),
            shape((count, fr, fc), f32),
            shape((rows, cols), f32),
            shape(kernels.shape, f32),
            shape(psi.shape, f32),
        ],
        (defocus, freqs, kernels, psi, target),
        kinds="vvhhh",
        scratch=[
            pltpu.VMEM(target.shape, jnp.int32),
            pltpu.SemaphoreType.DMA((3,)),
        ],
        flops=4000000000,
    )
    scratch = [
        pltpu.VMEM((count * 2 * rows, fc), bf),
        pltpu.VMEM((count * 2 * rows, cols), bf),
    ]
    common = (s_own, from_a, from_b, goal, table, inner, inner_t)
    (part,) = call(
        main_kernel,
        [shape((2 * fr, fc), f32 if paired else bf)],
        common + (k_re, k_im),
        scratch=scratch,
        flops=4000000000,
    )
    if paired:
        (part,) = call(
            main_kernel,
            [shape((2 * fr, fc), bf)],
            common + (part, other_defocus, psi_v, kernels_v),
            scratch=scratch + [pltpu.VMEM((count, fr, fc), f32)] * 2,
            flops=4000000000,
        )
    tall_t, far_t, slope, halo, halo_slope = call(
        functools.partial(third_kernel, strips, groups),
        [
            shape((3, 2 * tall, 2 * fr), bf),
            shape((max(1, len(groups)), 4 * HALO, 2 * fr), bf),
            shape((rows, cols), f32),
            shape((2 * PAD, cols), f32),
            shape((2 * PAD, cols), f32),
        ],
        (freqs, phi, from_a, from_b, part),
        flops=2000000000,
    )
    step = 1
    other = jnp.zeros_like(part)
    while step < planes // 2:
        if step > 1:
            part = lax.optimization_barrier(
                (part.astype(f32) + other.astype(f32)).astype(bf)
            )
        other = lax.ppermute(part, "focus", [(i, i ^ step) for i in range(planes)])
        step *= 2
    total, *payloads = call(
        sum_kernel,
        [shape((2 * fr, fc), bf)] + [shape((4 * HALO, fc), bf)] * len(groups),
        (part, other, far_t),
    )
    far = [
        lax.ppermute(payload, "strip", [(i, (i - turn_by) % strips) for i in range(strips)])
        for turn_by, payload in zip(groups, payloads)
    ]
    y_b = pair_up(total, False)
    y_a = pair_up(total, True)
    (z_own,) = call(own_kernel, [shape((2 * tall, fc), f32)], (tall_t, total), flops=2000000000)
    return call(
        functools.partial(final_kernel, strips),
        [shape((rows, cols), f32)],
        (phi, slope, halo, halo_slope, table, tall_t, z_own, y_a, y_b, *far),
        out_kinds="h",
        scratch=[
            pltpu.VMEM((rows, cols), f32),
            pltpu.SemaphoreType.DMA((rows // 8,)),
        ]
        + [pltpu.VMEM((cols // LANES, tall, LANES), f32)] * 6,
    )[0]


def solution(mesh):
    return jax.shard_map(
        on_device,
        mesh=mesh,
        in_specs=(
            P(("tile", "strip"), None),
            P(("tile", "strip"), None),
            P(("tile", "focus")),
            P(),
            P(),
            P(),
            P(),
        ),
        out_specs=P(("tile", "strip"), None),
        check_vma=False,
    )
```

```python
import functools

import jax
import jax.numpy as jnp
from jax import lax
from jax.experimental import pallas as pl
from jax.experimental.pallas import tpu as pltpu
from jax.sharding import PartitionSpec as P

MARGIN = 64
LEVELS = 31
SWEEPS = 2
HALO = SWEEPS
LANES = 128
PAD = 8
CHUNK = 256
GROUPS = (4, 4)

slope_resist = 4.0
level_resist = 0.5
step_size = 1.0
flow_rate = 0.2

SIN_TERMS = (3.1415926401307073, -5.167710083507878, 2.550077523214199, -0.5982912856179897, 0.07765766030124945)
COS_TERMS = (0.9999999532476078, -4.934792830619626, 4.0584113528622625, -1.3318765680789622, 0.2196896110945085)


def cos_sin(t):
    square = t * t
    s = SIN_TERMS[-1] * square + SIN_TERMS[-2]
    for term in SIN_TERMS[-3::-1]:
        s = s * square + term
    s = s * t
    c = COS_TERMS[-1] * square + COS_TERMS[-2]
    for term in COS_TERMS[-3::-1]:
        c = c * square + term
    twice = s + s
    return 1.0 - twice * s, twice * c


def turn(product, period):
    if float(period).is_integer() and int(period) & (int(period) - 1) == 0:
        t = product * (1.0 / period)
        return cos_sin(t - jnp.round(t))
    rest = product - jnp.round(product * (1.0 / period)) * period
    return cos_sin(rest * (1.0 / period))


def mirrored(block):
    spots = (LANES - 1) - lax.broadcasted_iota(jnp.int32, block.shape, 1)
    return jnp.take_along_axis(block, spots, axis=1, mode="promise_in_bounds")


def dot(lhs_mat, rhs_mat):
    return jnp.dot(lhs_mat, rhs_mat, preferred_element_type=jnp.float32)


def dot_t(lhs_mat, rhs_mat):
    return lax.dot_general(
        lhs_mat, rhs_mat, (((1,), (1,)), ((), ())), preferred_element_type=jnp.float32
    )


def offset_groups(rows, strips):
    reach = (MARGIN + HALO + rows - 1) // rows
    groups = {}
    for offset in range(-reach, reach + 1):
        if abs(offset) > 1:
            groups.setdefault(offset % strips, []).append(offset)
    return groups


def partners(strips):
    place = lax.axis_index("strip")
    first = jnp.where(place % 2 == 0, 1, -1)
    second = -first

    def inside(offset):
        return (place + offset >= 0) & (place + offset < strips)

    return place, first, second, inside(first), inside(second)


def quarter(second, imag, c, s):
    return jnp.where(second == imag, c, jnp.where(second, s, -s))


def rotation(freqs, shape, length, freq_dim, fr, start, period):
    spot = lax.broadcasted_iota(jnp.int32, shape, 1 - freq_dim)
    second = spot >= length
    spot = jnp.where(second, spot - length, spot) + start
    imag = lax.broadcasted_iota(jnp.int32, shape, freq_dim) >= fr
    c, s = turn(freqs * spot.astype(jnp.float32), float(period))
    return quarter(second, imag, c, s), spot


def interleaved(freqs, shape, freq_dim, fr, start, period):
    index = lax.broadcasted_iota(jnp.int32, shape, 1 - freq_dim)
    spot = ((index >> 4) << 3) + (index & 7) + start
    second = (index & 8) > 0
    imag = lax.broadcasted_iota(jnp.int32, shape, freq_dim) >= fr
    c, s = turn(freqs * spot.astype(jnp.float32), float(period))
    return quarter(second, imag, c, s)


def row_freq_lanes(row_freqs_ref, freq_ref):
    fr = row_freqs_ref.shape[1]
    freqs = jnp.broadcast_to(row_freqs_ref[...].astype(jnp.float32), (8, fr))
    freq_ref[...] = jnp.zeros_like(freq_ref)
    freq_ref[:, 0:fr] = freqs
    freq_ref[:, fr : 2 * fr] = freqs


def first_kernel(
    strips,
    phi_hbm,
    row_freqs_hbm,
    col_freqs_hbm,
    kernels_hbm,
    psi_hbm,
    target_hbm,
    table_ref,
    own_ref,
    send_a_ref,
    send_b_ref,
    phi_ref,
    freq_ref,
    kernels_ref,
    psi_ref,
    target_ref,
    mask_ref,
    row_freqs_ref,
    col_freqs_ref,
    sems,
):
    rows, cols = phi_ref.shape
    half = cols // 2
    fr, fc = row_freqs_ref.shape[1], table_ref.shape[0]
    window = rows + 2 * MARGIN
    bf = jnp.bfloat16
    load_cols = pltpu.make_async_copy(col_freqs_hbm, col_freqs_ref, sems.at[0])
    load_rows = pltpu.make_async_copy(row_freqs_hbm, row_freqs_ref, sems.at[1])
    load_phi = pltpu.make_async_copy(phi_hbm, phi_ref, sems.at[2])
    load_cols.start()
    load_rows.start()
    load_phi.start()
    later_loads = [
        pltpu.make_async_copy(psi_hbm, psi_ref, sems.at[3]),
        pltpu.make_async_copy(kernels_hbm, kernels_ref, sems.at[4]),
        pltpu.make_async_copy(target_hbm, target_ref, sems.at[5]),
    ]
    for load in later_loads:
        load.start()
    _, first, second, first_in, second_in = partners(strips)

    load_cols.wait()
    load_rows.wait()
    row_freq_lanes(row_freqs_ref, freq_ref)
    down = freq_ref[...].T[:fr, :1]
    spot = lax.broadcasted_iota(jnp.int32, (fr, 2 * rows), 1)
    later = spot >= rows
    spot = jnp.where(later, spot - rows, spot)
    c, s = turn(down * (spot + MARGIN).astype(jnp.float32), float(window))
    turn_c, turn_s = turn(jnp.broadcast_to(down, c.shape) * float(rows), float(window))

    def rows_in(c, s, offset, keep):
        at = spot + MARGIN - offset * rows
        keep = keep & (at >= 0) & (at < window)
        c = jnp.where(keep, c, 0.0)
        s = jnp.where(keep, s, 0.0)
        return jnp.concatenate([jnp.where(later, s, c), jnp.where(later, c, -s)], axis=0).astype(bf)

    sign = -first.astype(jnp.float32)
    turn_s = sign * turn_s
    in_all = jnp.concatenate(
        [
            rows_in(c * turn_c + s * turn_s, s * turn_c - c * turn_s, second, second_in),
            rows_in(c * turn_c - s * turn_s, s * turn_c + c * turn_s, first, first_in),
            rows_in(c, s, 0, True),
        ],
        axis=0,
    )

    freq_row = jnp.broadcast_to(col_freqs_ref[...].astype(jnp.float32), (8, fc))
    step_row_c, step_row_s = turn(freq_row * float(LANES), float(cols))
    kind = lax.broadcasted_iota(jnp.int32, (8, fc), 0)
    packed = jnp.where(kind == 0, freq_row, jnp.where(kind == 1, step_row_c, step_row_s)).T

    def make_columns(start, number):
        f = packed[start : start + number, 0:1]
        spot = lax.broadcasted_iota(jnp.int32, (number, LANES), 1).astype(jnp.float32)
        c, s = turn(f * (2.0 * spot + 1.0), 2.0 * cols)
        step_c = jnp.broadcast_to(packed[start : start + number, 1:2], (number, LANES))
        step_s = jnp.broadcast_to(packed[start : start + number, 2:3], (number, LANES))
        twice = 2.0 * step_c
        c_old, s_old = c, s
        here = slice(start, start + number)
        for b in range(half // LANES):
            if b == 1:
                c, s = c * step_c - s * step_s, s * step_c + c * step_s
            elif b:
                c, s, c_old, s_old = twice * c - c_old, twice * s - s_old, c, s
            table_ref[here, b * LANES : (b + 1) * LANES] = c.astype(bf)
            table_ref[here, half + b * LANES : half + (b + 1) * LANES] = s.astype(bf)

    def transform(start, number):
        here = slice(start, start + number)
        p_re = dot_t(mask_ref[:, :half], table_ref[here, :half])
        p_im = -dot_t(mask_ref[:, half:], table_ref[here, half:])
        spec = dot(in_all, jnp.concatenate([p_re, p_im], axis=0).astype(bf))
        send_b_ref[: 2 * fr, here] = spec[: 2 * fr].astype(bf)
        send_a_ref[: 2 * fr, here] = spec[2 * fr : 4 * fr].astype(bf)
        own_ref[:, here] = spec[4 * fr :]

    piece = 64
    start = 0
    for share in GROUPS:
        group = fc * share // 8
        for part in range(start, start + group, piece):
            make_columns(part, piece)
        if start == 0:
            load_phi.wait()
            for b in range(half // LANES):
                left = jnp.tanh(phi_ref[:, b * LANES : (b + 1) * LANES])
                right = mirrored(jnp.tanh(phi_ref[:, cols - (b + 1) * LANES : cols - b * LANES]))
                mask_ref[:, b * LANES : (b + 1) * LANES] = (left + right).astype(bf)
                mask_ref[:, half + b * LANES : half + (b + 1) * LANES] = (left - right).astype(bf)
        transform(start, group)
        start += group
    tops = [phi_ref[i : i + 1, q : q + fc] for i in range(HALO) for q in range(0, cols, fc)]
    lows = [
        phi_ref[rows - HALO + i : rows - HALO + i + 1, q : q + fc]
        for i in range(HALO)
        for q in range(0, cols, fc)
    ]
    tops = jnp.concatenate(tops, axis=0)
    lows = jnp.concatenate(lows, axis=0)
    send_a_ref[2 * fr :] = jnp.where(first > 0, lows, tops).astype(bf)
    send_b_ref[2 * fr :] = jnp.where(second > 0, lows, tops).astype(bf)
    for load in later_loads:
        load.wait()


def defocus_kernel(defocus_ref, after_ref, out_ref):
    middle = (LEVELS - 1) / 2.0
    defocus = (defocus_ref[0].astype(jnp.float32) - middle) * (1.0 / middle)
    out_ref[...] = jnp.full(out_ref.shape, defocus, jnp.float32)


def kernels_at(defocus_ref, psi_ref, kernels_ref, k_re_ref, k_im_ref):
    cycles = psi_ref[...] * (defocus_ref[0:1, 0:1] * (0.5 / jnp.pi))
    turn_c, turn_s = cos_sin(cycles)
    for k in range(kernels_ref.shape[1]):
        k_re_ref[k] = kernels_ref[0, k] * turn_c - kernels_ref[1, k] * turn_s
        k_im_ref[k] = kernels_ref[0, k] * turn_s + kernels_ref[1, k] * turn_c


def second_kernel(
    defocus_ref,
    freq_ref,
    kernels_ref,
    psi_ref,
    target_ref,
    inner_ref,
    inner_t_ref,
    k_re_ref,
    k_im_ref,
    goal_ref,
):
    rows, cols = target_ref.shape
    half = cols // 2
    fr = psi_ref.shape[0]
    window = rows + 2 * MARGIN
    bf = jnp.bfloat16
    across = freq_ref[0:1, :]
    down = freq_ref[...].T[: 2 * fr, :1]

    inner_ref[...] = interleaved(down, (2 * fr, 2 * rows), 0, fr, MARGIN, window).astype(bf)
    table = interleaved(across, (2 * rows, LANES), 1, fr, MARGIN, window)
    inner_t_ref[...] = table[:, : 2 * fr].astype(bf)

    kernels_at(defocus_ref, psi_ref, kernels_ref, k_re_ref, k_im_ref)

    goal_ref[:, :half] = target_ref[:, :half].astype(jnp.float32)
    for b in range(half // LANES):
        goal_ref[:, half + b * LANES : half + (b + 1) * LANES] = mirrored(
            target_ref[:, cols - (b + 1) * LANES : cols - b * LANES].astype(jnp.float32)
        )


def third_kernel(
    strips,
    groups,
    freq_ref,
    phi_ref,
    from_a_ref,
    from_b_ref,
    part_ref,
    tall_ref,
    far_ref,
    slope_ref,
    halo_ref,
    halo_slope_ref,
):
    rows, cols = phi_ref.shape
    fr, fc = part_ref.shape[0] // 2, part_ref.shape[1]
    window = rows + 2 * MARGIN
    bf = jnp.bfloat16
    place, first, second, first_in, second_in = partners(strips)
    across = freq_ref[0:1, :]

    tall = rows + 2 * PAD
    for index, (offset, keep) in enumerate(((0, True), (first, first_in), (second, second_in))):
        table, spot = rotation(
            across, (2 * tall, LANES), tall, 1, fr, MARGIN - PAD - offset * rows, window
        )
        keep = keep & (spot >= 0) & (spot < window)
        tall_ref[index] = jnp.where(keep, table, 0.0)[:, : 2 * fr].astype(bf)
    shape = (4 * HALO, LANES)
    index = lax.broadcasted_iota(jnp.int32, shape, 0)
    imag_row = index >= 2 * HALO
    index = jnp.where(imag_row, index - 2 * HALO, index)
    low = index >= HALO
    row = jnp.where(low, index + (rows - HALO), index - HALO)
    imag = lax.broadcasted_iota(jnp.int32, shape, 1) >= fr
    for group, offsets in enumerate(groups.values()):
        total = jnp.zeros(shape, jnp.float32)
        for offset in offsets:
            spot = row - offset * rows + MARGIN
            keep = (spot >= 0) & (spot < window) & (low if offset > 0 else ~low)
            keep = keep & (place - offset >= 0) & (place - offset < strips)
            c, s = turn(across * spot.astype(jnp.float32), float(window))
            total = total + jnp.where(keep, quarter(imag_row, imag, c, s), 0.0)
        far_ref[group] = total[:, : 2 * fr].astype(bf)

    scale = 1.0 / float(window * cols) ** 0.5
    mask = jnp.tanh(phi_ref[...])
    slope_ref[...] = (step_size * scale) * (1.0 - mask * mask)

    halo_ref[...] = jnp.zeros_like(halo_ref)
    edges_a = from_a_ref[2 * fr :].astype(jnp.float32)
    edges_b = from_b_ref[2 * fr :].astype(jnp.float32)
    top_in = (place > 0).astype(jnp.float32)
    low_in = (place < strips - 1).astype(jnp.float32)
    above = jnp.where(first < 0, edges_a, edges_b) * top_in
    below = jnp.where(first < 0, edges_b, edges_a) * low_in
    per_row = cols // fc
    for i in range(HALO):
        for q in range(per_row):
            here = slice(q * fc, (q + 1) * fc)
            spot = i * per_row + q
            halo_ref[PAD - HALO + i : PAD - HALO + i + 1, here] = above[spot : spot + 1]
            halo_ref[PAD + i : PAD + i + 1, here] = below[spot : spot + 1]
    for edge, inside in ((0, top_in), (PAD, low_in)):
        mask = jnp.tanh(halo_ref[edge : edge + PAD])
        halo_slope_ref[edge : edge + PAD] = (step_size * scale) * inside * (1.0 - mask * mask)


def own_kernel(tall_ref, y_ref, z_ref):
    z_ref[...] = dot(tall_ref[0], y_ref[...])


def main_kernel(
    own_ref,
    from_a_ref,
    from_b_ref,
    goal_ref,
    table_ref,
    inner_ref,
    inner_t_ref,
    *rest,
):
    rows, cols = goal_ref.shape
    half = cols // 2
    if len(rest) == 5:
        base_refs, (k_re_ref, k_im_ref, out_ref, q_ref, x_ref) = (), rest
    else:
        base_refs, (defocus_ref, psi_ref, kernels_ref) = rest[:1], rest[1:4]
        out_ref, q_ref, x_ref, k_re_ref, k_im_ref = rest[4:]
        kernels_at(defocus_ref, psi_ref, kernels_ref, k_re_ref, k_im_ref)
    count, fr, _ = k_re_ref.shape
    scale = 1.0 / float((rows + 2 * MARGIN) * cols) ** 0.5
    bf = jnp.bfloat16
    f32 = jnp.float32

    spec = scale * (
        own_ref[...] + from_a_ref[: 2 * fr].astype(f32) + from_b_ref[: 2 * fr].astype(f32)
    )
    s_re, s_im = spec[:fr], spec[fr:]
    unit = 16 * count
    gain = 4.0 * slope_resist / count * scale
    norm = scale * scale / count
    width = min(CHUNK, half)

    def weight(intensity, goal):
        resist = jax.nn.sigmoid(slope_resist * (norm * intensity - level_resist))
        return gain * (resist - goal) * resist * (1.0 - resist)

    def fields(k_re_ref, k_im_ref, q_ref):
        for k in range(count):
            k_re, k_im = k_re_ref[k], k_im_ref[k]
            g = jnp.concatenate([k_re * s_re - k_im * s_im, k_re * s_im + k_im * s_re], axis=0)
            q = dot(inner_t_ref[...], g.astype(bf)).astype(bf)
            for r in range(rows // 8):
                q_ref[r * unit + 16 * k : r * unit + 16 * k + 16] = q[16 * r : 16 * r + 16]

    def weighted(q_ref, x_ref, start):
        left_half = slice(start, start + width)
        right_half = slice(half + start, half + start + width)
        af = dot(q_ref[...], table_ref[:, left_half])
        db = dot(q_ref[...], table_ref[:, right_half])
        for r in range(rows // 8):

            def parts(k):
                at = r * unit + 16 * k
                return af[at : at + 8], db[at + 8 : at + 16], af[at + 8 : at + 16], db[at : at + 8]

            even = 0.0
            cross = 0.0
            for k in range(count):
                a, b, f, d = parts(k)
                even = even + ((a * a + f * f) + (d * d + b * b))
                cross = cross + (a * b - d * f)
            cross = 2.0 * cross
            here = slice(8 * r, 8 * r + 8)
            w_left = weight(even - cross, goal_ref[here, left_half])
            w_right = weight(even + cross, goal_ref[here, right_half])
            p_w = w_left + w_right
            q_w = w_right - w_left
            for k in range(count):
                a, b, f, d = parts(k)
                at = slice(r * unit + 16 * k, r * unit + 16 * k + 16)
                x_ref[at, left_half] = jnp.concatenate(
                    [p_w * a + q_w * b, p_w * f - q_w * d], axis=0
                ).astype(bf)
                x_ref[at, right_half] = jnp.concatenate(
                    [p_w * d - q_w * f, q_w * a + p_w * b], axis=0
                ).astype(bf)

    def adjoint(k_re_ref, k_im_ref, q_ref, x_ref):
        q_ref[...] = dot_t(x_ref[...], table_ref[...]).astype(bf)
        y_re = 0.0
        y_im = 0.0
        for k in range(count):
            u = jnp.concatenate(
                [q_ref[r * unit + 16 * k : r * unit + 16 * k + 16] for r in range(rows // 8)],
                axis=0,
            )
            w = scale * dot(inner_ref[...], u)
            w_re, w_im = w[:fr], w[fr:]
            k_re, k_im = k_re_ref[k], k_im_ref[k]
            y_re = y_re + (k_re * w_re + k_im * w_im)
            y_im = y_im + (k_re * w_im - k_im * w_re)
        return y_re, y_im

    fields(k_re_ref, k_im_ref, q_ref)
    for start in range(0, half, width):
        weighted(q_ref, x_ref, start)
    y_re, y_im = adjoint(k_re_ref, k_im_ref, q_ref, x_ref)
    for base_ref in base_refs:
        y_re = y_re + base_ref[:fr]
        y_im = y_im + base_ref[fr:]
    out_ref[:fr] = y_re.astype(out_ref.dtype)
    out_ref[fr:] = y_im.astype(out_ref.dtype)


def sum_kernel(part_ref, other_ref, far_ref, total_ref, *payload_refs):
    total = part_ref[...].astype(jnp.float32) + other_ref[...].astype(jnp.float32)
    total = total.astype(jnp.bfloat16)
    total_ref[...] = total
    for index, payload_ref in enumerate(payload_refs):
        payload_ref[...] = dot(far_ref[index], total).astype(jnp.bfloat16)


def final_kernel(
    strips,
    phi_ref,
    slope_ref,
    halo_ref,
    halo_slope_ref,
    table_ref,
    tall_ref,
    z_own_ref,
    y_a_ref,
    y_b_ref,
    *rest,
):
    payload_refs = rest[:-9]
    out_hbm, out_ref, sems = rest[-9:-6]
    level_ref, level_across, level_both, next_ref, next_across, next_both = rest[-6:]
    place, _, _, _, _ = partners(strips)
    rows, cols = phi_ref.shape
    half = cols // 2
    blocks = cols // LANES
    tall = rows + 2 * PAD
    bf = jnp.bfloat16
    f32 = jnp.float32

    z = z_own_ref[...] + dot(tall_ref[1], y_a_ref[...]) + dot(tall_ref[2], y_b_ref[...])
    if payload_refs:
        down = lax.broadcasted_iota(jnp.int32, (2 * tall, 4 * HALO), 0)
        index = lax.broadcasted_iota(jnp.int32, (2 * tall, 4 * HALO), 1)
        imag = index >= 2 * HALO
        index = jnp.where(imag, index - 2 * HALO, index)
        goes = jnp.where(index < HALO, index + (PAD - HALO), index + (PAD + rows - HALO))
        goes = jnp.where(imag, goes + tall, goes)
        place_rows = jnp.where(down == goes, 1.0, 0.0).astype(bf)
        for payload_ref in payload_refs:
            z = z + dot(place_rows, payload_ref[...])
    z = z.astype(bf)
    even = dot(z[:tall], table_ref[:, :half])
    odd = dot(z[tall:], table_ref[:, half:])

    top_in = place > 0
    low_in = place < strips - 1

    def advance(b, grad):
        here = slice(b * LANES, (b + 1) * LANES)
        level_ref[b, PAD : PAD + rows] = phi_ref[:, here] - slope_ref[:, here] * grad[
            PAD : PAD + rows
        ]
        for edge, to in ((0, 0), (PAD, PAD + rows)):
            step = halo_slope_ref[edge : edge + PAD, here] * grad[to : to + PAD]
            level_ref[b, to : to + PAD] = halo_ref[edge : edge + PAD, here] - step

    for b in range(half // LANES):
        part = slice(b * LANES, (b + 1) * LANES)
        advance(b, even[:, part] - odd[:, part])
        advance(blocks - 1 - b, mirrored(even[:, part] + odd[:, part]))

    lane = lax.broadcasted_iota(jnp.int32, (8, LANES), 1)
    nothing = jnp.zeros((8, LANES), f32)

    def beside(values):
        ahead = [pltpu.roll(value, LANES - 1, 1) for value in values] + [nothing]
        behind = [nothing] + [pltpu.roll(value, 1, 1) for value in values]
        for b in range(len(values)):
            right = jnp.where(lane == LANES - 1, ahead[b + 1], ahead[b])
            left = jnp.where(lane == 0, behind[b], behind[b + 1])
            yield right - left, right + left

    def sweep(refs, at, b):
        source, across_ref, both_ref = refs
        here = slice(at, at + 8)
        c = source[b, here]
        up, down = source[b, at + 1 : at + 9], source[b, at - 1 : at + 7]
        y = across_ref[b, here]
        crossed = across_ref[b, at + 1 : at + 9] - across_ref[b, at - 1 : at + 7]
        twice = c + c
        x = up - down
        second_x = (up + down) - twice
        second_y = both_ref[b, here] - twice
        x_x = x * x
        y_y = y * y
        numer = second_x * y_y + second_y * x_x - (0.5 * x) * y * crossed
        return c + flow_rate * (numer / (4.0 + x_x + y_y))

    levels = (level_ref, level_across, level_both)
    nexts = (next_ref, next_across, next_both)

    def fill(refs, at, values):
        for b, (difference, total) in enumerate(beside(values)):
            refs[1][b, at : at + 8] = difference
            refs[2][b, at : at + 8] = total

    def cover(first_row, end):
        starts = list(range(first_row, end - 7, 8))
        return starts if starts[-1] + 8 >= end else starts + [end - 8]

    for at in cover(PAD - 2, PAD + rows + 2):
        fill(levels, at, [level_ref[b, at : at + 8] for b in range(blocks)])
    for at in cover(PAD - 1, PAD + rows + 1):
        values = [sweep(levels, at, b) for b in range(blocks)]
        if at < PAD or at + 8 > PAD + rows:
            spot = lax.broadcasted_iota(jnp.int32, (8, LANES), 0) + at
            keep = ((spot >= PAD) | top_in) & ((spot < PAD + rows) | low_in)
            values = [jnp.where(keep, value, 0.0) for value in values]
        for b in range(blocks):
            next_ref[b, at : at + 8] = values[b]
        fill(nexts, at, values)
    copies = []
    for index in range(rows // 8):
        here = slice(8 * index, 8 * index + 8)
        for b in range(blocks):
            out_ref[here, b * LANES : (b + 1) * LANES] = sweep(nexts, PAD + 8 * index, b)
        here = pl.ds(8 * index, 8)
        copies.append(pltpu.make_async_copy(out_ref.at[here], out_hbm.at[here], sems.at[index]))
        copies[-1].start()
    for copy in copies:
        copy.wait()


def spec(kind):
    return pl.BlockSpec(memory_space={"v": pltpu.VMEM, "s": pltpu.SMEM, "h": pltpu.HBM}[kind])


def call(kernel, outs, args, kinds=None, out_kinds=None, scratch=(), limit=24, flops=1000000):
    kinds = kinds or "v" * len(args)
    out_kinds = out_kinds or "v" * len(outs)
    args = [
        pltpu.with_memory_space_constraint(arg, pltpu.HBM) if kind == "h" else arg
        for kind, arg in zip(kinds, args)
    ]
    return pl.pallas_call(
        kernel,
        out_shape=outs,
        in_specs=[spec(kind) for kind in kinds],
        out_specs=[spec(kind) for kind in out_kinds],
        scratch_shapes=list(scratch),
        compiler_params=pltpu.CompilerParams(vmem_limit_bytes=limit << 20),
        cost_estimate=pl.CostEstimate(flops=flops, bytes_accessed=4 << 20, transcendentals=0),
    )(*args)


def pair_up(block, first):
    strips, planes = lax.axis_size("strip"), lax.axis_size("focus")
    moves = []
    for strip in range(strips):
        up = (strip % 2 == 0) == first
        partner = strip + 1 if up else strip - 1
        for plane in range(planes):
            here = strip * planes + plane
            if 0 <= partner < strips:
                moves.append((here, partner * planes + plane))
            else:
                moves.append((here, strip * planes + (plane ^ 1 if planes > 1 else plane)))
    return lax.ppermute(block, ("strip", "focus"), moves)


def on_device(phi, target, defocus_ids, kernels, psi, row_freqs, col_freqs):
    rows, cols = phi.shape
    fr, fc = psi.shape
    count = kernels.shape[1]
    strips = lax.axis_size("strip")
    planes = lax.axis_size("focus")
    groups = offset_groups(rows, strips)
    tall = rows + 2 * PAD
    bf = jnp.bfloat16
    f32 = jnp.float32
    shape = jax.ShapeDtypeStruct
    packet = shape((2 * fr + HALO * (cols // fc), fc), bf)
    row_freqs = row_freqs.reshape(1, fr)

    table, s_own, send_a, send_b, phi, freqs, kernels_v, psi_v, target_v = call(
        functools.partial(first_kernel, strips),
        [
            shape((fc, cols), bf),
            shape((2 * fr, fc), f32),
            packet,
            packet,
            shape((rows, cols), f32),
            shape((8, LANES), f32),
            shape(kernels.shape, f32),
            shape(psi.shape, f32),
            shape(target.shape, jnp.int32),
        ],
        (phi, row_freqs, col_freqs.reshape(1, fc), kernels, psi, target),
        kinds="hhhhhh",
        scratch=[
            pltpu.VMEM((rows, cols), bf),
            pltpu.VMEM((1, fr), jnp.int32),
            pltpu.VMEM((1, fc), jnp.int32),
            pltpu.SemaphoreType.DMA((6,)),
        ],
    )
    (defocus,) = call(
        defocus_kernel, [shape((8, LANES), f32)], (defocus_ids, freqs), kinds="sv"
    )
    paired = planes > 1
    from_b = pair_up(send_b, False)
    from_a = pair_up(send_a, True)
    if paired:
        swap = [(i, i ^ (planes // 2)) for i in range(planes)]
        other_defocus = lax.ppermute(defocus, "focus", swap)
    inner, inner_t, k_re, k_im, goal = call(
        second_kernel,
        [
            shape((2 * fr, 2 * rows), bf),
            shape((2 * rows, 2 * fr), bf),
            shape((count, fr, fc), f32),
            shape((count, fr, fc), f32),
            shape((rows, cols), f32),
        ],
        (defocus, freqs, kernels_v, psi_v, target_v),
        flops=4000000000,
    )
    scratch = [
        pltpu.VMEM((count * 2 * rows, fc), bf),
        pltpu.VMEM((count * 2 * rows, cols), bf),
    ]
    common = (s_own, from_a, from_b, goal, table, inner, inner_t)
    (part,) = call(
        main_kernel,
        [shape((2 * fr, fc), f32 if paired else bf)],
        common + (k_re, k_im),
        scratch=scratch,
        flops=4000000000,
    )
    if paired:
        (part,) = call(
            main_kernel,
            [shape((2 * fr, fc), bf)],
            common + (part, other_defocus, psi_v, kernels_v),
            scratch=scratch + [pltpu.VMEM((count, fr, fc), f32)] * 2,
            flops=4000000000,
        )
    tall_t, far_t, slope, halo, halo_slope = call(
        functools.partial(third_kernel, strips, groups),
        [
            shape((3, 2 * tall, 2 * fr), bf),
            shape((max(1, len(groups)), 4 * HALO, 2 * fr), bf),
            shape((rows, cols), f32),
            shape((2 * PAD, cols), f32),
            shape((2 * PAD, cols), f32),
        ],
        (freqs, phi, from_a, from_b, part),
        flops=2000000000,
    )
    step = 1
    other = jnp.zeros_like(part)
    while step < planes // 2:
        if step > 1:
            part = lax.optimization_barrier(
                (part.astype(f32) + other.astype(f32)).astype(bf)
            )
        other = lax.ppermute(part, "focus", [(i, i ^ step) for i in range(planes)])
        step *= 2
    total, *payloads = call(
        sum_kernel,
        [shape((2 * fr, fc), bf)] + [shape((4 * HALO, fc), bf)] * len(groups),
        (part, other, far_t),
    )
    y_b = pair_up(total, False)
    y_a = pair_up(total, True)
    far = [
        lax.ppermute(payload, "strip", [(i, (i - turn_by) % strips) for i in range(strips)])
        for turn_by, payload in zip(groups, payloads)
    ]
    (z_own,) = call(own_kernel, [shape((2 * tall, fc), f32)], (tall_t, total), flops=2000000000)
    return call(
        functools.partial(final_kernel, strips),
        [shape((rows, cols), f32)],
        (phi, slope, halo, halo_slope, table, tall_t, z_own, y_a, y_b, *far),
        out_kinds="h",
        scratch=[
            pltpu.VMEM((rows, cols), f32),
            pltpu.SemaphoreType.DMA((rows // 8,)),
        ]
        + [pltpu.VMEM((cols // LANES, tall, LANES), f32)] * 6,
    )[0]


def solution(mesh):
    return jax.shard_map(
        on_device,
        mesh=mesh,
        in_specs=(
            P(("tile", "strip"), None),
            P(("tile", "strip"), None),
            P(("tile", "focus")),
            P(),
            P(),
            P(),
            P(),
        ),
        out_specs=P(("tile", "strip"), None),
        check_vma=False,
    )
```

```python
import functools

import jax
import jax.numpy as jnp
from jax import lax
from jax.experimental import pallas as pl
from jax.experimental.pallas import tpu as pltpu
from jax.sharding import PartitionSpec as P

MARGIN = 64
LEVELS = 31
SWEEPS = 2
HALO = SWEEPS
LANES = 128
PAD = 8
CHUNK = 256
GROUPS = (4, 4)

slope_resist = 4.0
level_resist = 0.5
step_size = 1.0
flow_rate = 0.2

SIN_TERMS = (3.1415926401307073, -5.167710083507878, 2.550077523214199, -0.5982912856179897, 0.07765766030124945)
COS_TERMS = (0.9999999532476078, -4.934792830619626, 4.0584113528622625, -1.3318765680789622, 0.2196896110945085)


def cos_sin(t):
    square = t * t
    s = SIN_TERMS[-1] * square + SIN_TERMS[-2]
    for term in SIN_TERMS[-3::-1]:
        s = s * square + term
    s = s * t
    c = COS_TERMS[-1] * square + COS_TERMS[-2]
    for term in COS_TERMS[-3::-1]:
        c = c * square + term
    twice = s + s
    return 1.0 - twice * s, twice * c


def turn(product, period):
    if float(period).is_integer() and int(period) & (int(period) - 1) == 0:
        t = product * (1.0 / period)
        return cos_sin(t - jnp.round(t))
    rest = product - jnp.round(product * (1.0 / period)) * period
    return cos_sin(rest * (1.0 / period))


def mirrored(block):
    spots = (LANES - 1) - lax.broadcasted_iota(jnp.int32, block.shape, 1)
    return jnp.take_along_axis(block, spots, axis=1, mode="promise_in_bounds")


def dot(lhs_mat, rhs_mat):
    return jnp.dot(lhs_mat, rhs_mat, preferred_element_type=jnp.float32)


def dot_t(lhs_mat, rhs_mat):
    return lax.dot_general(
        lhs_mat, rhs_mat, (((1,), (1,)), ((), ())), preferred_element_type=jnp.float32
    )


def offset_groups(rows, strips):
    reach = (MARGIN + HALO + rows - 1) // rows
    groups = {}
    for offset in range(-reach, reach + 1):
        if abs(offset) > 1:
            groups.setdefault(offset % strips, []).append(offset)
    return groups


def partners(strips):
    place = lax.axis_index("strip")
    first = jnp.where(place % 2 == 0, 1, -1)
    second = -first

    def inside(offset):
        return (place + offset >= 0) & (place + offset < strips)

    return place, first, second, inside(first), inside(second)


def quarter(second, imag, c, s):
    return jnp.where(second == imag, c, jnp.where(second, s, -s))


def rotation(freqs, shape, length, freq_dim, fr, start, period):
    spot = lax.broadcasted_iota(jnp.int32, shape, 1 - freq_dim)
    second = spot >= length
    spot = jnp.where(second, spot - length, spot) + start
    imag = lax.broadcasted_iota(jnp.int32, shape, freq_dim) >= fr
    c, s = turn(freqs * spot.astype(jnp.float32), float(period))
    return quarter(second, imag, c, s), spot


def interleaved(freqs, shape, freq_dim, fr, start, period):
    index = lax.broadcasted_iota(jnp.int32, shape, 1 - freq_dim)
    spot = ((index >> 4) << 3) + (index & 7) + start
    second = (index & 8) > 0
    imag = lax.broadcasted_iota(jnp.int32, shape, freq_dim) >= fr
    c, s = turn(freqs * spot.astype(jnp.float32), float(period))
    return quarter(second, imag, c, s)


def row_freq_lanes(row_freqs_ref, freq_ref):
    fr = row_freqs_ref.shape[1]
    freqs = jnp.broadcast_to(row_freqs_ref[...].astype(jnp.float32), (8, fr))
    freq_ref[...] = jnp.zeros_like(freq_ref)
    freq_ref[:, 0:fr] = freqs
    freq_ref[:, fr : 2 * fr] = freqs


def first_kernel(
    strips,
    phi_hbm,
    row_freqs_hbm,
    col_freqs_hbm,
    kernels_hbm,
    psi_hbm,
    target_hbm,
    table_ref,
    own_ref,
    send_a_ref,
    send_b_ref,
    phi_ref,
    freq_ref,
    kernels_ref,
    psi_ref,
    target_ref,
    mask_ref,
    row_freqs_ref,
    col_freqs_ref,
    sems,
):
    rows, cols = phi_ref.shape
    half = cols // 2
    fr, fc = row_freqs_ref.shape[1], table_ref.shape[0]
    window = rows + 2 * MARGIN
    bf = jnp.bfloat16
    load_cols = pltpu.make_async_copy(col_freqs_hbm, col_freqs_ref, sems.at[0])
    load_rows = pltpu.make_async_copy(row_freqs_hbm, row_freqs_ref, sems.at[1])
    load_phi = pltpu.make_async_copy(phi_hbm, phi_ref, sems.at[2])
    load_cols.start()
    load_rows.start()
    load_phi.start()
    later_loads = [
        pltpu.make_async_copy(psi_hbm, psi_ref, sems.at[3]),
        pltpu.make_async_copy(kernels_hbm, kernels_ref, sems.at[4]),
        pltpu.make_async_copy(target_hbm, target_ref, sems.at[5]),
    ]
    for load in later_loads:
        load.start()
    _, first, second, first_in, second_in = partners(strips)

    load_cols.wait()
    load_rows.wait()
    row_freq_lanes(row_freqs_ref, freq_ref)
    down = freq_ref[...].T[:fr, :1]
    spot = lax.broadcasted_iota(jnp.int32, (fr, 2 * rows), 1)
    later = spot >= rows
    spot = jnp.where(later, spot - rows, spot)
    c, s = turn(down * (spot + MARGIN).astype(jnp.float32), float(window))
    turn_c, turn_s = turn(jnp.broadcast_to(down, c.shape) * float(rows), float(window))

    def rows_in(c, s, offset, keep):
        at = spot + MARGIN - offset * rows
        keep = keep & (at >= 0) & (at < window)
        c = jnp.where(keep, c, 0.0)
        s = jnp.where(keep, s, 0.0)
        return jnp.concatenate([jnp.where(later, s, c), jnp.where(later, c, -s)], axis=0).astype(bf)

    sign = -first.astype(jnp.float32)
    turn_s = sign * turn_s
    in_all = jnp.concatenate(
        [
            rows_in(c * turn_c + s * turn_s, s * turn_c - c * turn_s, second, second_in),
            rows_in(c * turn_c - s * turn_s, s * turn_c + c * turn_s, first, first_in),
            rows_in(c, s, 0, True),
        ],
        axis=0,
    )

    freq_row = jnp.broadcast_to(col_freqs_ref[...].astype(jnp.float32), (8, fc))
    step_row_c, step_row_s = turn(freq_row * float(LANES), float(cols))
    kind = lax.broadcasted_iota(jnp.int32, (8, fc), 0)
    packed = jnp.where(kind == 0, freq_row, jnp.where(kind == 1, step_row_c, step_row_s)).T

    def make_columns(start, number):
        f = packed[start : start + number, 0:1]
        spot = lax.broadcasted_iota(jnp.int32, (number, LANES), 1).astype(jnp.float32)
        c, s = turn(f * (2.0 * spot + 1.0), 2.0 * cols)
        step_c = jnp.broadcast_to(packed[start : start + number, 1:2], (number, LANES))
        step_s = jnp.broadcast_to(packed[start : start + number, 2:3], (number, LANES))
        twice = 2.0 * step_c
        c_old, s_old = c, s
        here = slice(start, start + number)
        for b in range(half // LANES):
            if b == 1:
                c, s = c * step_c - s * step_s, s * step_c + c * step_s
            elif b:
                c, s, c_old, s_old = twice * c - c_old, twice * s - s_old, c, s
            table_ref[here, b * LANES : (b + 1) * LANES] = c.astype(bf)
            table_ref[here, half + b * LANES : half + (b + 1) * LANES] = s.astype(bf)

    def transform(start, number):
        here = slice(start, start + number)
        p_re = dot_t(mask_ref[:, :half], table_ref[here, :half])
        p_im = -dot_t(mask_ref[:, half:], table_ref[here, half:])
        spec = dot(in_all, jnp.concatenate([p_re, p_im], axis=0).astype(bf))
        send_b_ref[: 2 * fr, here] = spec[: 2 * fr].astype(bf)
        send_a_ref[: 2 * fr, here] = spec[2 * fr : 4 * fr].astype(bf)
        own_ref[:, here] = spec[4 * fr :]

    piece = 64
    start = 0
    for share in GROUPS:
        group = fc * share // 8
        for part in range(start, start + group, piece):
            make_columns(part, piece)
        if start == 0:
            load_phi.wait()
            for b in range(half // LANES):
                left = jnp.tanh(phi_ref[:, b * LANES : (b + 1) * LANES])
                right = mirrored(jnp.tanh(phi_ref[:, cols - (b + 1) * LANES : cols - b * LANES]))
                mask_ref[:, b * LANES : (b + 1) * LANES] = (left + right).astype(bf)
                mask_ref[:, half + b * LANES : half + (b + 1) * LANES] = (left - right).astype(bf)
        transform(start, group)
        start += group
    tops = [phi_ref[i : i + 1, q : q + fc] for i in range(HALO) for q in range(0, cols, fc)]
    lows = [
        phi_ref[rows - HALO + i : rows - HALO + i + 1, q : q + fc]
        for i in range(HALO)
        for q in range(0, cols, fc)
    ]
    tops = jnp.concatenate(tops, axis=0)
    lows = jnp.concatenate(lows, axis=0)
    send_a_ref[2 * fr :] = jnp.where(first > 0, lows, tops).astype(bf)
    send_b_ref[2 * fr :] = jnp.where(second > 0, lows, tops).astype(bf)
    for load in later_loads:
        load.wait()


def defocus_kernel(defocus_ref, after_ref, out_ref):
    middle = (LEVELS - 1) / 2.0
    defocus = (defocus_ref[0].astype(jnp.float32) - middle) * (1.0 / middle)
    out_ref[...] = jnp.full(out_ref.shape, defocus, jnp.float32)


def kernels_at(defocus_ref, psi_ref, kernels_ref, k_re_ref, k_im_ref):
    cycles = psi_ref[...] * (defocus_ref[0:1, 0:1] * (0.5 / jnp.pi))
    turn_c, turn_s = cos_sin(cycles)
    for k in range(kernels_ref.shape[1]):
        k_re_ref[k] = kernels_ref[0, k] * turn_c - kernels_ref[1, k] * turn_s
        k_im_ref[k] = kernels_ref[0, k] * turn_s + kernels_ref[1, k] * turn_c


def second_kernel(
    defocus_ref,
    freq_ref,
    kernels_ref,
    psi_ref,
    target_ref,
    inner_ref,
    inner_t_ref,
    k_re_ref,
    k_im_ref,
    goal_ref,
):
    rows, cols = target_ref.shape
    half = cols // 2
    fr = psi_ref.shape[0]
    window = rows + 2 * MARGIN
    bf = jnp.bfloat16
    across = freq_ref[0:1, :]
    down = freq_ref[...].T[: 2 * fr, :1]

    inner_ref[...] = interleaved(down, (2 * fr, 2 * rows), 0, fr, MARGIN, window).astype(bf)
    table = interleaved(across, (2 * rows, LANES), 1, fr, MARGIN, window)
    inner_t_ref[...] = table[:, : 2 * fr].astype(bf)

    kernels_at(defocus_ref, psi_ref, kernels_ref, k_re_ref, k_im_ref)

    goal_ref[:, :half] = target_ref[:, :half].astype(jnp.float32)
    for b in range(half // LANES):
        goal_ref[:, half + b * LANES : half + (b + 1) * LANES] = mirrored(
            target_ref[:, cols - (b + 1) * LANES : cols - b * LANES].astype(jnp.float32)
        )


def third_kernel(
    strips,
    groups,
    freq_ref,
    phi_ref,
    from_a_ref,
    from_b_ref,
    part_ref,
    tall_ref,
    far_ref,
    slope_ref,
    halo_ref,
    halo_slope_ref,
):
    rows, cols = phi_ref.shape
    fr, fc = part_ref.shape[0] // 2, part_ref.shape[1]
    window = rows + 2 * MARGIN
    bf = jnp.bfloat16
    place, first, second, first_in, second_in = partners(strips)
    across = freq_ref[0:1, :]

    tall = rows + 2 * PAD
    for index, (offset, keep) in enumerate(((0, True), (first, first_in), (second, second_in))):
        table, spot = rotation(
            across, (2 * tall, LANES), tall, 1, fr, MARGIN - PAD - offset * rows, window
        )
        keep = keep & (spot >= 0) & (spot < window)
        tall_ref[index] = jnp.where(keep, table, 0.0)[:, : 2 * fr].astype(bf)
    shape = (4 * HALO, LANES)
    index = lax.broadcasted_iota(jnp.int32, shape, 0)
    imag_row = index >= 2 * HALO
    index = jnp.where(imag_row, index - 2 * HALO, index)
    low = index >= HALO
    row = jnp.where(low, index + (rows - HALO), index - HALO)
    imag = lax.broadcasted_iota(jnp.int32, shape, 1) >= fr
    for group, offsets in enumerate(groups.values()):
        total = jnp.zeros(shape, jnp.float32)
        for offset in offsets:
            spot = row - offset * rows + MARGIN
            keep = (spot >= 0) & (spot < window) & (low if offset > 0 else ~low)
            keep = keep & (place - offset >= 0) & (place - offset < strips)
            c, s = turn(across * spot.astype(jnp.float32), float(window))
            total = total + jnp.where(keep, quarter(imag_row, imag, c, s), 0.0)
        far_ref[group] = total[:, : 2 * fr].astype(bf)

    scale = 1.0 / float(window * cols) ** 0.5
    mask = jnp.tanh(phi_ref[...])
    slope_ref[...] = (step_size * scale) * (1.0 - mask * mask)

    halo_ref[...] = jnp.zeros_like(halo_ref)
    edges_a = from_a_ref[2 * fr :].astype(jnp.float32)
    edges_b = from_b_ref[2 * fr :].astype(jnp.float32)
    top_in = (place > 0).astype(jnp.float32)
    low_in = (place < strips - 1).astype(jnp.float32)
    above = jnp.where(first < 0, edges_a, edges_b) * top_in
    below = jnp.where(first < 0, edges_b, edges_a) * low_in
    per_row = cols // fc
    for i in range(HALO):
        for q in range(per_row):
            here = slice(q * fc, (q + 1) * fc)
            spot = i * per_row + q
            halo_ref[PAD - HALO + i : PAD - HALO + i + 1, here] = above[spot : spot + 1]
            halo_ref[PAD + i : PAD + i + 1, here] = below[spot : spot + 1]
    for edge, inside in ((0, top_in), (PAD, low_in)):
        mask = jnp.tanh(halo_ref[edge : edge + PAD])
        halo_slope_ref[edge : edge + PAD] = (step_size * scale) * inside * (1.0 - mask * mask)


def own_kernel(tall_ref, y_ref, z_ref):
    z_ref[...] = dot(tall_ref[0], y_ref[...])


def main_kernel(
    own_ref,
    from_a_ref,
    from_b_ref,
    goal_ref,
    table_ref,
    inner_ref,
    inner_t_ref,
    *rest,
):
    rows, cols = goal_ref.shape
    half = cols // 2
    if len(rest) == 5:
        base_refs, (k_re_ref, k_im_ref, out_ref, q_ref, x_ref) = (), rest
    else:
        base_refs, (defocus_ref, psi_ref, kernels_ref) = rest[:1], rest[1:4]
        out_ref, q_ref, x_ref, k_re_ref, k_im_ref = rest[4:]
        kernels_at(defocus_ref, psi_ref, kernels_ref, k_re_ref, k_im_ref)
    count, fr, _ = k_re_ref.shape
    scale = 1.0 / float((rows + 2 * MARGIN) * cols) ** 0.5
    bf = jnp.bfloat16
    f32 = jnp.float32

    spec = scale * (
        own_ref[...] + from_a_ref[: 2 * fr].astype(f32) + from_b_ref[: 2 * fr].astype(f32)
    )
    s_re, s_im = spec[:fr], spec[fr:]
    unit = 16 * count
    gain = 4.0 * slope_resist / count * scale
    norm = scale * scale / count
    width = min(CHUNK, half)

    def weight(intensity, goal):
        resist = jax.nn.sigmoid(slope_resist * (norm * intensity - level_resist))
        return gain * (resist - goal) * resist * (1.0 - resist)

    def fields(k_re_ref, k_im_ref, q_ref):
        for k in range(count):
            k_re, k_im = k_re_ref[k], k_im_ref[k]
            g = jnp.concatenate([k_re * s_re - k_im * s_im, k_re * s_im + k_im * s_re], axis=0)
            q = dot(inner_t_ref[...], g.astype(bf)).astype(bf)
            for r in range(rows // 8):
                q_ref[r * unit + 16 * k : r * unit + 16 * k + 16] = q[16 * r : 16 * r + 16]

    def weighted(q_ref, x_ref, start):
        left_half = slice(start, start + width)
        right_half = slice(half + start, half + start + width)
        af = dot(q_ref[...], table_ref[:, left_half])
        db = dot(q_ref[...], table_ref[:, right_half])
        for r in range(rows // 8):

            def parts(k):
                at = r * unit + 16 * k
                return af[at : at + 8], db[at + 8 : at + 16], af[at + 8 : at + 16], db[at : at + 8]

            even = 0.0
            cross = 0.0
            for k in range(count):
                a, b, f, d = parts(k)
                even = even + ((a * a + f * f) + (d * d + b * b))
                cross = cross + (a * b - d * f)
            cross = 2.0 * cross
            here = slice(8 * r, 8 * r + 8)
            w_left = weight(even - cross, goal_ref[here, left_half])
            w_right = weight(even + cross, goal_ref[here, right_half])
            p_w = w_left + w_right
            q_w = w_right - w_left
            for k in range(count):
                a, b, f, d = parts(k)
                at = slice(r * unit + 16 * k, r * unit + 16 * k + 16)
                x_ref[at, left_half] = jnp.concatenate(
                    [p_w * a + q_w * b, p_w * f - q_w * d], axis=0
                ).astype(bf)
                x_ref[at, right_half] = jnp.concatenate(
                    [p_w * d - q_w * f, q_w * a + p_w * b], axis=0
                ).astype(bf)

    def adjoint(k_re_ref, k_im_ref, q_ref, x_ref):
        q_ref[...] = dot_t(x_ref[...], table_ref[...]).astype(bf)
        y_re = 0.0
        y_im = 0.0
        for k in range(count):
            u = jnp.concatenate(
                [q_ref[r * unit + 16 * k : r * unit + 16 * k + 16] for r in range(rows // 8)],
                axis=0,
            )
            w = scale * dot(inner_ref[...], u)
            w_re, w_im = w[:fr], w[fr:]
            k_re, k_im = k_re_ref[k], k_im_ref[k]
            y_re = y_re + (k_re * w_re + k_im * w_im)
            y_im = y_im + (k_re * w_im - k_im * w_re)
        return y_re, y_im

    fields(k_re_ref, k_im_ref, q_ref)
    for start in range(0, half, width):
        weighted(q_ref, x_ref, start)
    y_re, y_im = adjoint(k_re_ref, k_im_ref, q_ref, x_ref)
    for base_ref in base_refs:
        y_re = y_re + base_ref[:fr]
        y_im = y_im + base_ref[fr:]
    out_ref[:fr] = y_re.astype(out_ref.dtype)
    out_ref[fr:] = y_im.astype(out_ref.dtype)


def sum_kernel(part_ref, other_ref, far_ref, total_ref, *payload_refs):
    total = part_ref[...].astype(jnp.float32) + other_ref[...].astype(jnp.float32)
    total = total.astype(jnp.bfloat16)
    total_ref[...] = total
    for index, payload_ref in enumerate(payload_refs):
        payload_ref[...] = dot(far_ref[index], total).astype(jnp.bfloat16)


def final_kernel(
    strips,
    phi_ref,
    slope_ref,
    halo_ref,
    halo_slope_ref,
    table_ref,
    tall_ref,
    z_own_ref,
    y_a_ref,
    y_b_ref,
    *rest,
):
    payload_refs = rest[:-9]
    out_hbm, out_ref, sems = rest[-9:-6]
    level_ref, level_across, level_both, next_ref, next_across, next_both = rest[-6:]
    place, _, _, _, _ = partners(strips)
    rows, cols = phi_ref.shape
    half = cols // 2
    blocks = cols // LANES
    tall = rows + 2 * PAD
    bf = jnp.bfloat16
    f32 = jnp.float32

    z = z_own_ref[...] + dot(tall_ref[1], y_a_ref[...]) + dot(tall_ref[2], y_b_ref[...])
    if payload_refs:
        down = lax.broadcasted_iota(jnp.int32, (2 * tall, 4 * HALO), 0)
        index = lax.broadcasted_iota(jnp.int32, (2 * tall, 4 * HALO), 1)
        imag = index >= 2 * HALO
        index = jnp.where(imag, index - 2 * HALO, index)
        goes = jnp.where(index < HALO, index + (PAD - HALO), index + (PAD + rows - HALO))
        goes = jnp.where(imag, goes + tall, goes)
        place_rows = jnp.where(down == goes, 1.0, 0.0).astype(bf)
        for payload_ref in payload_refs:
            z = z + dot(place_rows, payload_ref[...])
    z = z.astype(bf)

    top_in = place > 0
    low_in = place < strips - 1

    def advance(b, grad):
        here = slice(b * LANES, (b + 1) * LANES)
        level_ref[b, PAD : PAD + rows] = phi_ref[:, here] - slope_ref[:, here] * grad[
            PAD : PAD + rows
        ]
        for edge, to in ((0, 0), (PAD, PAD + rows)):
            step = halo_slope_ref[edge : edge + PAD, here] * grad[to : to + PAD]
            level_ref[b, to : to + PAD] = halo_ref[edge : edge + PAD, here] - step

    width = min(CHUNK, half)
    for start in range(0, half, width):
        even = dot(z[:tall], table_ref[:, start : start + width])
        odd = dot(z[tall:], table_ref[:, half + start : half + start + width])
        for b in range(width // LANES):
            part = slice(b * LANES, (b + 1) * LANES)
            spot = start // LANES + b
            advance(spot, even[:, part] - odd[:, part])
            advance(blocks - 1 - spot, mirrored(even[:, part] + odd[:, part]))

    lane = lax.broadcasted_iota(jnp.int32, (8, LANES), 1)
    nothing = jnp.zeros((8, LANES), f32)

    def beside(values):
        ahead = [pltpu.roll(value, LANES - 1, 1) for value in values] + [nothing]
        behind = [nothing] + [pltpu.roll(value, 1, 1) for value in values]
        for b in range(len(values)):
            right = jnp.where(lane == LANES - 1, ahead[b + 1], ahead[b])
            left = jnp.where(lane == 0, behind[b], behind[b + 1])
            yield right - left, right + left

    def sweep(refs, at, b):
        source, across_ref, both_ref = refs
        here = slice(at, at + 8)
        c = source[b, here]
        up, down = source[b, at + 1 : at + 9], source[b, at - 1 : at + 7]
        y = across_ref[b, here]
        crossed = across_ref[b, at + 1 : at + 9] - across_ref[b, at - 1 : at + 7]
        twice = c + c
        x = up - down
        second_x = (up + down) - twice
        second_y = both_ref[b, here] - twice
        x_x = x * x
        y_y = y * y
        numer = second_x * y_y + second_y * x_x - (0.5 * x) * y * crossed
        return c + flow_rate * (numer / (4.0 + x_x + y_y))

    levels = (level_ref, level_across, level_both)
    nexts = (next_ref, next_across, next_both)

    def fill(refs, at, values):
        for b, (difference, total) in enumerate(beside(values)):
            refs[1][b, at : at + 8] = difference
            refs[2][b, at : at + 8] = total

    def cover(first_row, end):
        starts = list(range(first_row, end - 7, 8))
        return starts if starts[-1] + 8 >= end else starts + [end - 8]

    for at in cover(PAD - 2, PAD + rows + 2):
        fill(levels, at, [level_ref[b, at : at + 8] for b in range(blocks)])
    for at in cover(PAD - 1, PAD + rows + 1):
        values = [sweep(levels, at, b) for b in range(blocks)]
        if at < PAD or at + 8 > PAD + rows:
            spot = lax.broadcasted_iota(jnp.int32, (8, LANES), 0) + at
            keep = ((spot >= PAD) | top_in) & ((spot < PAD + rows) | low_in)
            values = [jnp.where(keep, value, 0.0) for value in values]
        for b in range(blocks):
            next_ref[b, at : at + 8] = values[b]
        fill(nexts, at, values)
    copies = []
    for index in range(rows // 8):
        here = slice(8 * index, 8 * index + 8)
        for b in range(blocks):
            out_ref[here, b * LANES : (b + 1) * LANES] = sweep(nexts, PAD + 8 * index, b)
        here = pl.ds(8 * index, 8)
        copies.append(pltpu.make_async_copy(out_ref.at[here], out_hbm.at[here], sems.at[index]))
        copies[-1].start()
    for copy in copies:
        copy.wait()


def spec(kind):
    return pl.BlockSpec(memory_space={"v": pltpu.VMEM, "s": pltpu.SMEM, "h": pltpu.HBM}[kind])


def call(kernel, outs, args, kinds=None, out_kinds=None, scratch=(), limit=24, flops=1000000):
    kinds = kinds or "v" * len(args)
    out_kinds = out_kinds or "v" * len(outs)
    args = [
        pltpu.with_memory_space_constraint(arg, pltpu.HBM) if kind == "h" else arg
        for kind, arg in zip(kinds, args)
    ]
    return pl.pallas_call(
        kernel,
        out_shape=outs,
        in_specs=[spec(kind) for kind in kinds],
        out_specs=[spec(kind) for kind in out_kinds],
        scratch_shapes=list(scratch),
        compiler_params=pltpu.CompilerParams(vmem_limit_bytes=limit << 20),
        cost_estimate=pl.CostEstimate(flops=flops, bytes_accessed=4 << 20, transcendentals=0),
    )(*args)


def pair_up(block, first):
    strips, planes = lax.axis_size("strip"), lax.axis_size("focus")
    moves = []
    for strip in range(strips):
        up = (strip % 2 == 0) == first
        partner = strip + 1 if up else strip - 1
        for plane in range(planes):
            here = strip * planes + plane
            if 0 <= partner < strips:
                moves.append((here, partner * planes + plane))
            else:
                moves.append((here, strip * planes + (plane ^ 1 if planes > 1 else plane)))
    return lax.ppermute(block, ("strip", "focus"), moves)


def on_device(phi, target, defocus_ids, kernels, psi, row_freqs, col_freqs):
    rows, cols = phi.shape
    fr, fc = psi.shape
    count = kernels.shape[1]
    strips = lax.axis_size("strip")
    planes = lax.axis_size("focus")
    groups = offset_groups(rows, strips)
    tall = rows + 2 * PAD
    bf = jnp.bfloat16
    f32 = jnp.float32
    shape = jax.ShapeDtypeStruct
    packet = shape((2 * fr + HALO * (cols // fc), fc), bf)
    row_freqs = row_freqs.reshape(1, fr)

    table, s_own, send_a, send_b, phi, freqs, kernels_v, psi_v, target_v = call(
        functools.partial(first_kernel, strips),
        [
            shape((fc, cols), bf),
            shape((2 * fr, fc), f32),
            packet,
            packet,
            shape((rows, cols), f32),
            shape((8, LANES), f32),
            shape(kernels.shape, f32),
            shape(psi.shape, f32),
            shape(target.shape, jnp.int32),
        ],
        (phi, row_freqs, col_freqs.reshape(1, fc), kernels, psi, target),
        kinds="hhhhhh",
        scratch=[
            pltpu.VMEM((rows, cols), bf),
            pltpu.VMEM((1, fr), jnp.int32),
            pltpu.VMEM((1, fc), jnp.int32),
            pltpu.SemaphoreType.DMA((6,)),
        ],
    )
    (defocus,) = call(
        defocus_kernel, [shape((8, LANES), f32)], (defocus_ids, freqs), kinds="sv"
    )
    paired = planes > 1
    from_b = pair_up(send_b, False)
    from_a = pair_up(send_a, True)
    if paired:
        swap = [(i, i ^ (planes // 2)) for i in range(planes)]
        other_defocus = lax.ppermute(defocus, "focus", swap)
    inner, inner_t, k_re, k_im, goal = call(
        second_kernel,
        [
            shape((2 * fr, 2 * rows), bf),
            shape((2 * rows, 2 * fr), bf),
            shape((count, fr, fc), f32),
            shape((count, fr, fc), f32),
            shape((rows, cols), f32),
        ],
        (defocus, freqs, kernels_v, psi_v, target_v),
        flops=4000000000,
    )
    scratch = [
        pltpu.VMEM((count * 2 * rows, fc), bf),
        pltpu.VMEM((count * 2 * rows, cols), bf),
    ]
    common = (s_own, from_a, from_b, goal, table, inner, inner_t)
    (part,) = call(
        main_kernel,
        [shape((2 * fr, fc), f32 if paired else bf)],
        common + (k_re, k_im),
        scratch=scratch,
        flops=4000000000,
    )
    if paired:
        (part,) = call(
            main_kernel,
            [shape((2 * fr, fc), bf)],
            common + (part, other_defocus, psi_v, kernels_v),
            scratch=scratch + [pltpu.VMEM((count, fr, fc), f32)] * 2,
            flops=4000000000,
        )
    tall_t, far_t, slope, halo, halo_slope = call(
        functools.partial(third_kernel, strips, groups),
        [
            shape((3, 2 * tall, 2 * fr), bf),
            shape((max(1, len(groups)), 4 * HALO, 2 * fr), bf),
            shape((rows, cols), f32),
            shape((2 * PAD, cols), f32),
            shape((2 * PAD, cols), f32),
        ],
        (freqs, phi, from_a, from_b, part),
        flops=2000000000,
    )
    step = 1
    other = jnp.zeros_like(part)
    while step < planes // 2:
        if step > 1:
            part = lax.optimization_barrier(
                (part.astype(f32) + other.astype(f32)).astype(bf)
            )
        other = lax.ppermute(part, "focus", [(i, i ^ step) for i in range(planes)])
        step *= 2
    total, *payloads = call(
        sum_kernel,
        [shape((2 * fr, fc), bf)] + [shape((4 * HALO, fc), bf)] * len(groups),
        (part, other, far_t),
    )
    y_b = pair_up(total, False)
    y_a = pair_up(total, True)
    far = [
        lax.ppermute(payload, "strip", [(i, (i - turn_by) % strips) for i in range(strips)])
        for turn_by, payload in zip(groups, payloads)
    ]
    (z_own,) = call(own_kernel, [shape((2 * tall, fc), f32)], (tall_t, total), flops=2000000000)
    return call(
        functools.partial(final_kernel, strips),
        [shape((rows, cols), f32)],
        (phi, slope, halo, halo_slope, table, tall_t, z_own, y_a, y_b, *far),
        out_kinds="h",
        scratch=[
            pltpu.VMEM((rows, cols), f32),
            pltpu.SemaphoreType.DMA((rows // 8,)),
        ]
        + [pltpu.VMEM((cols // LANES, tall, LANES), f32)] * 6,
    )[0]


def solution(mesh):
    return jax.shard_map(
        on_device,
        mesh=mesh,
        in_specs=(
            P(("tile", "strip"), None),
            P(("tile", "strip"), None),
            P(("tile", "focus")),
            P(),
            P(),
            P(),
            P(),
        ),
        out_specs=P(("tile", "strip"), None),
        check_vma=False,
    )
```
